32 devices in a mesh: shard: 4 (over y, x), ctx: 4 (over z), tensor: 2 (over core).
Axes of the slice: x: 2, y: 2, z: 4, core: 2. Of those that a mesh axis runs over, the one named last changes fastest.
Arguments:
- streams: bfloat16 [2048, 4, 2048], P(('shard', 'ctx')), may hold values from -6 to 6
- lengths: int32 [4, 4], P('shard'), may hold values from 1 to 384, 512 in all within a row
- destination: int32 [2048], P(('shard', 'ctx')), may hold values from 0 to 2047, as said below
- w_query: bfloat16 [2048, 2048], P('shard', 'tensor'), may hold values from -0.125 to 0.125
- w_key: bfloat16 [2048, 2048], P('shard', 'tensor'), may hold values from -0.125 to 0.125
- w_value: bfloat16 [2048, 2048], P('shard', 'tensor'), may hold values from -0.125 to 0.125
- w_output: bfloat16 [2048, 2048], P('tensor', 'shard'), may hold values from -1.5 to 1.5
- w_gate: bfloat16 [2048, 8192], P('shard', 'tensor'), may hold values from -0.125 to 0.125
- w_up: bfloat16 [2048, 8192], P('shard', 'tensor'), may hold values from -0.125 to 0.125
- w_down: bfloat16 [8192, 2048], P('tensor', 'shard'), may hold values from -0.0625 to 0.0625
- mix_weight: float32 [2, 2048, 6], replicated, may hold values from -0.125 to 0.125
- mix_static: float32 [2, 4, 6], replicated, may hold values from -3 to 3
- cotangent: bfloat16 [2048, 4, 2048], P(('shard', 'ctx')), may hold values from -6 to 6
Outputs:
- streams_out: bfloat16 [2048, 4, 2048], P(('shard', 'ctx'))
- grad_streams: bfloat16 [2048, 4, 2048], P(('shard', 'ctx'))
- grad_query: float32 [2048, 2048], P(('shard', 'ctx'), 'tensor')
- grad_key: float32 [2048, 2048], P(('shard', 'ctx'), 'tensor')
- grad_value: float32 [2048, 2048], P(('shard', 'ctx'), 'tensor')
- grad_output: float32 [2048, 2048], P('tensor', ('shard', 'ctx'))
- grad_gate: float32 [2048, 8192], P(('shard', 'ctx'), 'tensor')
- grad_up: float32 [2048, 8192], P(('shard', 'ctx'), 'tensor')
- grad_down: float32 [8192, 2048], P('tensor', ('shard', 'ctx'))
- grad_mix_weight: float32 [2, 2048, 6], replicated
- grad_mix_static: float32 [2, 4, 6], replicated
The draws below stay inside these ranges and needn't reach their ends.
Inputs may be any that keep to these rules, and one draw needn't show every extreme that they name: `lengths`: each row sums to 512 and its largest entry is 384. `destination`: A permutation that keeps every group of 512 consecutive indices within itself; the 128 tokens of each aligned block of 128 indices send exactly 32 tokens to each aligned block of 128 slots of their group, as 32 consecutive tokens to 32 consecutive slots in the same order.
All inputs are finite; a program needn't handle non-finite values.
Results may differ from the reference program's by a relative error of at most 0.02.
The reference program's roundings to bfloat16 on the way count: a program that leaves them out, or rounds other values in their place, can miss the bound.
Values may be sent and summed in bfloat16 or wider, within the bound.
A program may use at most 384 MiB of HBM per device.

```python
import math
import jax
import jax.numpy as jnp
import numpy as np
from jax import lax

D = 2048
HEADS = 16
HD = 128
FF = 8192
STREAMS = 4
HCOLS = 6
TOK_DEV = 128
NSEQ = 4
GROUP = 512
GROUPS = 4
TOKENS = 2048
PER = 32
MAXLEN = 384


def draw_destination(key, part):
    groups = TOKENS // GROUP
    owners = GROUP // TOK_DEV
    key_runs, key_order = jax.random.split(jax.random.fold_in(key, 7))
    run_keys = jax.random.split(key_runs, groups * owners)
    targets = jax.vmap(lambda k: jax.random.permutation(k, owners))(run_keys).reshape(groups, owners, owners)
    order_keys = jax.random.split(key_order, groups * owners)
    arrival = jax.vmap(lambda k: jax.random.permutation(k, owners))(order_keys).reshape(groups, owners, owners)
    indices = jnp.arange(TOKENS, dtype=jnp.int32)
    group_of = indices // GROUP
    source = indices % GROUP // TOK_DEV
    local_row = indices % TOK_DEV
    run_index = local_row // PER
    within = local_row % PER
    target = targets[group_of, source, run_index]
    slot_here = arrival[group_of, target, source] * PER + within
    return (group_of * GROUP + target * TOK_DEV + slot_here).astype(jnp.int32)


def block_levels(key, shape, pieces, least, high):
    gain, own = 1.0, jax.random.fold_in(key, 6)
    for dim, shards_of in pieces:
        steps = jnp.exp(jax.random.uniform(jax.random.fold_in(own, dim), (shards_of,), jnp.float32, least / len(pieces), high / len(pieces)))
        gain = gain * jnp.repeat(steps, shape[dim] // shards_of).reshape([-1 if axis == dim else 1 for axis in range(len(shape))])
    return gain


def length_profile(amount, total, limit, skew):
    weights = [(1 << 20) // math.isqrt(grade ** skew) + 1 for grade in range(2, amount + 1)]
    spare, given = total - limit - (amount - 1), [1] * (amount - 1)
    while spare > 0:
        movable = [i for i in range(amount - 1) if given[i] < limit]
        pool, left = sum([weights[i] for i in movable]), spare
        for i in movable:
            more = min(limit - given[i], max(1, left * weights[i] // pool), spare)
            given[i] = given[i] + more
            spare = spare - more
    return np.array([limit] + given)


def ragged(stream_key, amount, total, limit, slope):
    if amount == 2:
        one = jax.random.randint(stream_key, (), max(1, total - limit), min(limit, total - 1) + 1)
        return jnp.stack([one, total - one])
    sizes = jnp.asarray(length_profile(amount, total, limit, slope), jnp.int32)
    couples = (amount - 1) // 2
    source_of, receiver = sizes[1:1 + 2 * couples:2], sizes[2:2 + 2 * couples:2]
    margin = jnp.minimum(source_of - 1, limit - receiver)
    shifted = jax.random.randint(jax.random.fold_in(stream_key, 1), (couples,), 0, 1 << 20) % (margin + 1)
    sizes = sizes.at[1:1 + 2 * couples:2].set(source_of - shifted).at[2:2 + 2 * couples:2].set(receiver + shifted)
    return sizes[jax.random.permutation(jax.random.fold_in(stream_key, 2), amount)]


def scatter_about(stream_key, shape, scale, reach, shards=(), held_as=jnp.bfloat16):
    drawn = jax.random.normal(stream_key, shape, jnp.float32) * scale
    if len(shards) > 0:
        drawn = block_levels(stream_key, shape, shards, -0.22, 0.18) * drawn
    return jnp.clip(drawn, min=-reach, max=reach).astype(held_as)


def setup_inputs(seed: int = 0) -> dict:
    key_list = jax.random.split(jax.random.key(seed), 14)
    return {
        "streams": scatter_about(key_list[0], (TOKENS, STREAMS, D), 1.0, 6.0, ((0, 16),)),
        "lengths": jax.vmap(lambda own: ragged(own, NSEQ, GROUP, MAXLEN, 2))(jax.random.split(key_list[1], GROUPS)).reshape((GROUPS, NSEQ)).astype(jnp.int32),
        "destination": draw_destination(jax.random.fold_in(key_list[13], 71), 0),
        "w_query": scatter_about(key_list[3], (D, D), D ** -0.5, 0.125, ((0, 4), (1, 2))),
        "w_key": scatter_about(key_list[4], (D, D), D ** -0.5, 0.125, ((0, 4), (1, 2))),
        "w_value": scatter_about(key_list[5], (D, D), D ** -0.5, 0.125, ((0, 4), (1, 2))),
        "w_output": scatter_about(key_list[6], (D, D), (max(D // 128, 1)) ** -0.5, 1.5, ((0, 2), (1, 4))),
        "w_gate": scatter_about(key_list[7], (D, FF), D ** -0.5, 0.125, ((0, 4), (1, 2))),
        "w_up": scatter_about(key_list[8], (D, FF), D ** -0.5, 0.125, ((0, 4), (1, 2))),
        "w_down": scatter_about(key_list[9], (FF, D), FF ** -0.5, 0.0625, ((0, 2), (1, 4))),
        "mix_weight": scatter_about(key_list[10], (2, D, HCOLS), D ** -0.5, 0.125, (), jnp.float32),
        "mix_static": scatter_about(key_list[11], (2, STREAMS, HCOLS), 0.5, 3.0, (), jnp.float32),
        "cotangent": scatter_about(key_list[12], (TOKENS, STREAMS, D), 1.0, 6.0, ((0, 16),)),
    }


PRECISE = lax.Precision.HIGHEST

@jax.custom_vjp
def low(v):
    return lax.optimization_barrier(v.astype(jnp.bfloat16)).astype(jnp.float32)

@jax.custom_vjp
def low_back(v):
    return v

def low_keep(v):
    return (low(v), None)

def low_pass(kept, grad):
    return (grad,)

def back_keep(v):
    return (v, None)

def back_low(kept, grad):
    return (low(grad),)
low.defvjp(low_keep, low_pass)
low_back.defvjp(back_keep, back_low)

def norm_rows(value):
    centred = value - lax.optimization_barrier(jnp.mean(value, -1, keepdims=True))
    return centred * lax.rsqrt(lax.optimization_barrier(jnp.mean(centred * centred, -1, keepdims=True)) + 1e-05)

def angles(positions):
    indices = jnp.arange(HD // 2, dtype=jnp.float32)
    frequency = 10000.0 ** (-(2.0 * indices / HD))
    turned = positions.astype(jnp.float32)[:, None] * frequency[None, :]
    return (jnp.cos(turned)[:, None, :], jnp.sin(turned)[:, None, :])

def rotate(value, cosine, sine):
    half = value.shape[-1] // 2
    first = value[..., :half]
    second = value[..., half:]
    return jnp.concatenate([first * cosine - second * sine, second * cosine + first * sine], -1)

def mixing(current, weight, static):
    table = jnp.tanh(jnp.einsum('tsd,dk->tsk', norm_rows(current), weight, precision=PRECISE)) + static
    branch_in = jnp.einsum('ts,tsd->td', table[..., 0], current, precision=PRECISE)
    return (branch_in, table)

def combine(current, branch_out, table):
    beta = table[..., STREAMS + 1]
    mixer = table[..., 1:STREAMS + 1]
    return beta[..., None] * branch_out[:, None, :] + jnp.einsum('tij,tid->tjd', mixer, current, precision=PRECISE)

def attend(queries, keys, values, segment, position):
    allowed = (segment[:, None] == segment[None, :]) & (position[None, :] <= position[:, None])

    def one_head(operands):
        query_head, key_head, value_head = operands
        scores = low_back(jnp.dot(query_head, key_head.T, precision=PRECISE) * HD ** (-0.5))
        top = lax.optimization_barrier(jnp.max(jnp.where(allowed, scores, -1e+30), -1, keepdims=True))
        weights = jnp.where(allowed, jnp.exp(scores - top), 0.0)
        probs = low(weights / lax.optimization_barrier(jnp.sum(weights, -1, keepdims=True)))
        return jnp.dot(probs, value_head, precision=PRECISE)
    heads = lax.map(jax.checkpoint(one_head), (queries.transpose(1, 0, 2), keys.transpose(1, 0, 2), values.transpose(1, 0, 2)))
    return heads.transpose(1, 0, 2)

def layer(current, segment, position, params):
    w_query, w_key, w_value, w_output, w_gate, w_up, w_down, mix_weight, mix_static = params
    rows_here = current.shape[0]
    shape = (rows_here, HEADS, HD)
    branch_in, table = mixing(current, mix_weight[0], mix_static[0])
    normed = low(norm_rows(branch_in))
    cosine, sine = angles(position)
    queries = low(rotate(low_back(jnp.dot(normed, w_query, precision=PRECISE)).reshape(shape), cosine, sine))
    keys = low(rotate(low_back(jnp.dot(normed, w_key, precision=PRECISE)).reshape(shape), cosine, sine))
    values = low(low_back(jnp.dot(normed, w_value, precision=PRECISE))).reshape(shape)
    mixed = low(low_back(attend(queries, keys, values, segment, position).reshape(rows_here, D)))
    current = combine(current, low_back(jnp.dot(mixed, w_output, precision=PRECISE)), table)
    branch_in, table = mixing(current, mix_weight[1], mix_static[1])
    normed = low(norm_rows(branch_in))
    gate = low_back(jnp.dot(normed, w_gate, precision=PRECISE))
    upward = low_back(jnp.dot(normed, w_up, precision=PRECISE))
    hidden = low(jax.nn.silu(gate) * upward)
    return combine(current, low_back(jnp.dot(hidden, w_down, precision=PRECISE)), table)

def reference(streams, lengths, destination, w_query, w_key, w_value, w_output, w_gate, w_up, w_down, mix_weight, mix_static, cotangent):
    placed = jnp.arange(GROUP, dtype=jnp.int32)
    ends = jnp.cumsum(lengths, axis=1).astype(jnp.int32)
    starts = ends - lengths
    segment = lax.optimization_barrier(jnp.sum((placed[None, :, None] >= ends[:, None, :]).astype(jnp.int32), axis=2))
    begin = lax.optimization_barrier(jnp.max(jnp.where(starts[:, None, :] <= placed[None, :, None], starts[:, None, :], 0), axis=2))
    position = placed[None, :] - begin

    def forward(current, params):

        def one_group(operands):
            return layer(operands[0], operands[1], operands[2], params)
        result = lax.map(jax.checkpoint(one_group), (current.reshape(GROUPS, GROUP, STREAMS, D), segment, position))
        return result.reshape(TOKENS, STREAMS, D)
    params = tuple((w.astype(jnp.float32) for w in (w_query, w_key, w_value, w_output, w_gate, w_up, w_down)))
    params = params + (mix_weight, mix_static)
    result, pull = jax.vjp(forward, streams.astype(jnp.float32), params)
    grad_current, grad_params = pull(cotangent.astype(jnp.float32)[destination])
    return (result.astype(jnp.bfloat16), grad_current.astype(jnp.bfloat16), grad_params[0], grad_params[1], grad_params[2], grad_params[3], grad_params[4], grad_params[5], grad_params[6], grad_params[7], grad_params[8])
```

```python
import jax
import jax.numpy as jnp
from jax import lax
from jax.sharding import PartitionSpec as P

HD = 128


PRECISE = lax.Precision.HIGHEST
EPSILON = 1e-05
FLOOR_SCORE = -1e30
TEAM = ("ctx", "tensor")


def norm_rows(value):
    centred = value - jnp.mean(value, -1, keepdims=True)
    scaled = lax.rsqrt(jnp.mean(centred * centred, -1, keepdims=True) + EPSILON)
    return (centred * scaled, scaled)


def norm_back(normed, scaled, grad):
    return scaled * (
        grad
        - jnp.mean(grad, -1, keepdims=True)
        - normed * jnp.mean(grad * normed, -1, keepdims=True)
    )


def angles(positions, head_size):
    indices = jnp.arange(head_size // 2, dtype=jnp.float32)
    frequency = 10000.0 ** (-(2.0 * indices / head_size))
    turned = positions.astype(jnp.float32)[:, None] * frequency[None, :]
    return (jnp.cos(turned)[:, None, :], jnp.sin(turned)[:, None, :])


def rotate(value, cosine, sine):
    half = value.shape[-1] // 2
    first = value[..., :half]
    second = value[..., half:]
    return jnp.concatenate([first * cosine - second * sine, second * cosine + first * sine], -1)


def dot(left, right):
    return jnp.dot(left, right, preferred_element_type=jnp.float32)


def contract_rows(left, right):
    return lax.dot_general(
        left, right, (((0,), (0,)), ((), ())), preferred_element_type=jnp.float32
    )


def contract_cols(left, right):
    return lax.dot_general(
        left, right, (((1,), (1,)), ((), ())), preferred_element_type=jnp.float32
    )


def mixing(current, weight, static):
    normed, scaled = norm_rows(current)
    active = jnp.tanh(jnp.einsum("tsd,dk->tsk", normed, weight, precision=PRECISE))
    table = active + static
    total = current.shape[1]
    branch_in = sum(table[:, i, 0][:, None] * current[:, i] for i in range(total))
    return (branch_in, table, active, normed, scaled)


def combine(current, branch_out, table):
    total = current.shape[1]
    return jnp.stack(
        [
            table[:, j, total + 1][:, None] * branch_out
            + sum(table[:, i, 1 + j][:, None] * current[:, i] for i in range(total))
            for j in range(total)
        ],
        1,
    )


def combine_back(current, table, grad_top):
    total = current.shape[1]
    grad_mixer = jnp.stack(
        [jnp.sum(current * grad_top[:, j][:, None], -1) for j in range(total)], -1
    )
    grad_current = jnp.stack(
        [
            sum(table[:, i, 1 + j][:, None] * grad_top[:, j] for j in range(total))
            for i in range(total)
        ],
        1,
    )
    return (grad_mixer, grad_current)


def branch_grad(table, grad_top):
    total = grad_top.shape[1]
    return sum(table[:, j, total + 1][:, None] * grad_top[:, j] for j in range(total))


def mixing_back(
    current, table, active, normed, scaled, weight, grad_in, grad_beta, grad_mixer, grad_current
):
    grad_alpha = jnp.sum(grad_in[:, None] * current, -1)
    grad_table = jnp.concatenate([grad_alpha[..., None], grad_mixer, grad_beta[..., None]], -1)
    grad_inner = grad_table * (1.0 - active * active)
    grad_weight = jnp.einsum("tsd,tsk->dk", normed, grad_inner, precision=PRECISE)
    grad_normed = jnp.einsum("tsk,dk->tsd", grad_inner, weight, precision=PRECISE)
    grad_current = (
        grad_current
        + table[..., 0][..., None] * grad_in[:, None, :]
        + norm_back(normed, scaled, grad_normed)
    )
    return (grad_current, grad_weight, jnp.sum(grad_table, 0))


def team_gather(value):
    return lax.all_gather(value, TEAM, axis=0, tiled=True)


def team_sum(value, kind=jnp.bfloat16):
    return lax.psum_scatter(
        value.astype(kind), TEAM, scatter_dimension=0, tiled=True
    ).astype(jnp.float32)


def shards(
    streams,
    lengths,
    destination,
    w_query,
    w_key,
    w_value,
    w_output,
    w_gate,
    w_up,
    w_down,
    mix_weight,
    mix_static,
    cotangent,
):
    rows_here, stream_total, width = streams.shape
    owners = lax.axis_size("ctx")
    cores = lax.axis_size("tensor")
    here = lax.axis_index("ctx")
    core = lax.axis_index("tensor")
    run_rows = rows_here // owners
    part = run_rows // cores
    mine = rows_here // cores
    group_rows = rows_here * owners
    head_cols = w_query.shape[1] // owners
    heads = head_cols // HD
    units = w_gate.shape[1] // owners
    scale = HD ** (-0.5)

    def columns(weight, count):
        return lax.dynamic_slice_in_dim(weight, here * count, count, 1)

    def rows(weight, count):
        return lax.dynamic_slice_in_dim(weight, here * count, count, 0)

    qkv = jnp.concatenate([columns(w, head_cols) for w in (w_query, w_key, w_value)], 1)
    qkv = lax.all_gather(qkv, "shard", axis=0, tiled=True)
    out_w = lax.all_gather(rows(w_output, head_cols), "shard", axis=0)
    out_w = out_w.transpose(1, 0, 2).reshape(head_cols, width)
    gate_up = jnp.concatenate([columns(w, units) for w in (w_gate, w_up)], 1)
    gate_up = lax.all_gather(gate_up, "shard", axis=0, tiled=True)
    down = lax.all_gather(rows(w_down, units), "shard", axis=0)
    down = down.transpose(1, 0, 2).reshape(units, width)

    order = jnp.arange(group_rows, dtype=jnp.int32)
    within = order % mine
    placed = (
        order // rows_here * rows_here
        + within // part * run_rows
        + order % rows_here // mine * part
        + within % part
    )
    spans = lengths[0]
    count = jnp.arange(spans.shape[0], dtype=jnp.int32)
    ends = jnp.sum(jnp.where(count[None, :] <= count[:, None], spans[None, :], 0), 1)
    starts = ends - spans
    segment = jnp.sum((placed[:, None] >= ends[None, :]).astype(jnp.int32), axis=1)
    begin = jnp.max(jnp.where(starts[None, :] <= placed[:, None], starts[None, :], 0), axis=1)
    position = placed - begin

    local_dest = destination - lax.axis_index("shard") * group_rows
    heads_of_runs = local_dest.reshape(owners, run_rows)[:, 0]
    every = lax.all_gather(heads_of_runs, "ctx", axis=0)
    sent = jnp.sum(jnp.where(every // rows_here == here, every % rows_here, 0), 1) + core * part
    packed = jnp.concatenate(
        [lax.dynamic_slice_in_dim(cotangent, sent[c], part, 0) for c in range(owners)], 0
    )
    arrived = lax.all_to_all(packed, "ctx", split_axis=0, concat_axis=0, tiled=True)
    came_from = heads_of_runs // rows_here * part
    grad_top = jnp.concatenate(
        [lax.dynamic_slice_in_dim(arrived, came_from[r], part, 0) for r in range(owners)], 0
    ).astype(jnp.float32)

    def own_rows(value):
        split = value.reshape(owners, cores, part, stream_total, width)
        return lax.dynamic_index_in_dim(split, core, 1, keepdims=False).reshape(
            mine, stream_total, width
        )

    current = own_rows(streams).astype(jnp.float32)
    branch_in, table_one, active_one, normed_one, scaled_one = mixing(
        current, mix_weight[0], mix_static[0]
    )
    attn_normed, attn_scaled = norm_rows(branch_in)
    attn_input = team_gather(attn_normed.astype(jnp.bfloat16))
    cosine, sine = angles(position, HD)
    lin = dot(attn_input, qkv).reshape(group_rows, 3, heads, HD)
    queries = rotate(lin[:, 0], cosine, sine).astype(jnp.bfloat16)
    keys = rotate(lin[:, 1], cosine, sine).astype(jnp.bfloat16)
    values = lin[:, 2].astype(jnp.bfloat16)
    allowed = (segment[:, None] == segment[None, :]) & (position[None, :] <= position[:, None])
    scores = jnp.einsum("qhd,khd->hqk", queries, keys, preferred_element_type=jnp.float32) * scale
    scores = jnp.where(allowed[None], scores, FLOOR_SCORE)
    top = jnp.max(scores, -1, keepdims=True)
    probs = jnp.where(allowed[None], jnp.exp(scores - top), 0.0)
    probs = probs / jnp.sum(probs, -1, keepdims=True)
    probs_low = probs.astype(jnp.bfloat16)
    attended = jnp.einsum("hqk,khd->qhd", probs_low, values, preferred_element_type=jnp.float32)
    attended = attended.reshape(group_rows, head_cols).astype(jnp.bfloat16)
    attn_out = team_sum(dot(attended, out_w), jnp.float32)

    middle = combine(current, attn_out, table_one)
    branch_two, table_two, active_two, normed_two, scaled_two = mixing(
        middle, mix_weight[1], mix_static[1]
    )
    ffn_normed, ffn_scaled = norm_rows(branch_two)
    ffn_input = team_gather(ffn_normed.astype(jnp.bfloat16))
    grad_ffn_out = team_gather(branch_grad(table_two, grad_top).astype(jnp.bfloat16))
    both = dot(ffn_input, gate_up)
    gate, upward = both[:, :units], both[:, units:]
    sigma = jax.nn.sigmoid(gate)
    hidden = (gate * sigma * upward).astype(jnp.bfloat16)
    ffn_out = team_sum(dot(hidden, down))
    grad_hidden = contract_cols(grad_ffn_out, down)
    grad_both = jnp.concatenate(
        [
            (grad_hidden * upward * sigma * (1.0 + gate * (1.0 - sigma))).astype(jnp.bfloat16),
            (grad_hidden * gate * sigma).astype(jnp.bfloat16),
        ],
        1,
    )
    grad_ffn_input = team_sum(contract_cols(grad_both, gate_up))

    def to_owner_rows(partial):
        summed = lax.psum_scatter(
            partial.astype(jnp.bfloat16), "shard", scatter_dimension=0, tiled=True
        )
        moved = lax.all_to_all(summed, "ctx", split_axis=0, concat_axis=0, tiled=True)
        return moved.reshape(owners, summed.shape[0] // owners, summed.shape[1])

    def row_parts(moved, amount):
        split = moved.reshape(owners, moved.shape[1], amount, moved.shape[2] // amount)
        return [
            split[:, :, i].transpose(1, 0, 2).reshape(moved.shape[1], -1).astype(jnp.float32)
            for i in range(amount)
        ]

    def to_owner_columns(left, right):
        shard_total = lax.axis_size("shard")
        partial = jnp.einsum(
            "th,tsd->shd",
            left,
            right.reshape(group_rows, shard_total, -1),
            preferred_element_type=jnp.float32,
        )
        summed = lax.psum_scatter(
            partial.astype(jnp.bfloat16), "shard", scatter_dimension=0, tiled=False
        )
        split = summed.reshape(left.shape[1], owners, -1).transpose(1, 0, 2)
        moved = lax.all_to_all(split, "ctx", split_axis=0, concat_axis=0, tiled=True)
        return moved.reshape(owners * left.shape[1], -1).astype(jnp.float32)

    grad_down = to_owner_columns(hidden, grad_ffn_out)
    grad_gate, grad_up = row_parts(to_owner_rows(contract_rows(ffn_input, grad_both)), 2)

    grad_beta = jnp.sum(grad_top * ffn_out[:, None], -1)
    grad_mixer, grad_middle = combine_back(middle, table_two, grad_top)
    grad_branch_two = norm_back(ffn_normed, ffn_scaled, grad_ffn_input)
    grad_middle, grad_weight_two, grad_static_two = mixing_back(
        middle,
        table_two,
        active_two,
        normed_two,
        scaled_two,
        mix_weight[1],
        grad_branch_two,
        grad_beta,
        grad_mixer,
        grad_middle,
    )
    grad_attn_out = team_gather(branch_grad(table_one, grad_middle).astype(jnp.bfloat16))
    final = combine(middle, ffn_out, table_two).astype(jnp.bfloat16)

    grad_attended = (
        contract_cols(grad_attn_out, out_w).astype(jnp.bfloat16).reshape(group_rows, heads, HD)
    )
    grad_probs = jnp.einsum(
        "qhd,khd->hqk", grad_attended, values, preferred_element_type=jnp.float32
    )
    delta = jnp.sum(probs * grad_probs, -1, keepdims=True)
    grad_scores = (probs * (grad_probs - delta)).astype(jnp.bfloat16)
    grad_query_rot = (
        jnp.einsum("hqk,khd->qhd", grad_scores, keys, preferred_element_type=jnp.float32) * scale
    )
    grad_key_rot = (
        jnp.einsum("hqk,qhd->khd", grad_scores, queries, preferred_element_type=jnp.float32)
        * scale
    )
    grad_value_vec = jnp.einsum(
        "hqk,qhd->khd", probs_low, grad_attended, preferred_element_type=jnp.float32
    )
    grad_lin = jnp.concatenate(
        [
            rotate(grad_query_rot, cosine, -sine).reshape(group_rows, head_cols),
            rotate(grad_key_rot, cosine, -sine).reshape(group_rows, head_cols),
            grad_value_vec.reshape(group_rows, head_cols),
        ],
        1,
    ).astype(jnp.bfloat16)
    grad_attn_input = team_sum(contract_cols(grad_lin, qkv))
    grad_output = to_owner_columns(attended, grad_attn_out)
    grad_query, grad_key, grad_value = row_parts(
        to_owner_rows(contract_rows(attn_input, grad_lin)), 3
    )

    grad_beta = jnp.sum(grad_middle * attn_out[:, None], -1)
    grad_mixer, grad_current = combine_back(current, table_one, grad_middle)
    grad_branch_one = norm_back(attn_normed, attn_scaled, grad_attn_input)
    grad_current, grad_weight_one, grad_static_one = mixing_back(
        current,
        table_one,
        active_one,
        normed_one,
        scaled_one,
        mix_weight[0],
        grad_branch_one,
        grad_beta,
        grad_mixer,
        grad_current,
    )
    grad_mix_weight, grad_mix_static = lax.psum(
        (
            jnp.stack([grad_weight_one, grad_weight_two]),
            jnp.stack([grad_static_one, grad_static_two]),
        ),
        ("shard", "ctx", "tensor"),
    )

    def all_rows(value):
        value = value.astype(jnp.bfloat16).reshape(owners, part, stream_total, width)
        full = lax.all_gather(value, "tensor", axis=1)
        return full.reshape(rows_here, stream_total, width)

    return (
        all_rows(final),
        all_rows(grad_current),
        grad_query,
        grad_key,
        grad_value,
        grad_output,
        grad_gate,
        grad_up,
        grad_down,
        grad_mix_weight,
        grad_mix_static,
    )


def solution(mesh):
    return jax.shard_map(
        shards,
        mesh=mesh,
        in_specs=(
            P(("shard", "ctx"), None, None),
            P("shard", None),
            P(("shard", "ctx")),
            P("shard", "tensor"),
            P("shard", "tensor"),
            P("shard", "tensor"),
            P("tensor", "shard"),
            P("shard", "tensor"),
            P("shard", "tensor"),
            P("tensor", "shard"),
            P(),
            P(),
            P(("shard", "ctx"), None, None),
        ),
        out_specs=(
            P(("shard", "ctx"), None, None),
            P(("shard", "ctx"), None, None),
            P(("shard", "ctx"), "tensor"),
            P(("shard", "ctx"), "tensor"),
            P(("shard", "ctx"), "tensor"),
            P("tensor", ("shard", "ctx")),
            P(("shard", "ctx"), "tensor"),
            P(("shard", "ctx"), "tensor"),
            P("tensor", ("shard", "ctx")),
            P(),
            P(),
        ),
        check_vma=False,
    )
```

```python
import functools

import jax
import jax.numpy as jnp
from jax import lax
from jax.experimental import pallas as pl
from jax.experimental.pallas import tpu as pltpu
from jax.sharding import PartitionSpec as P

HD = 128


PRECISE = lax.Precision.HIGHEST
EPSILON = 1e-05
FLOOR_SCORE = -1e30
TEAM = ("ctx", "tensor")


def norm_rows(value):
    centred = value - jnp.mean(value, -1, keepdims=True)
    scaled = lax.rsqrt(jnp.mean(centred * centred, -1, keepdims=True) + EPSILON)
    return (centred * scaled, scaled)


def norm_back(normed, scaled, grad):
    return scaled * (
        grad
        - jnp.mean(grad, -1, keepdims=True)
        - normed * jnp.mean(grad * normed, -1, keepdims=True)
    )


def angles(positions, head_size):
    indices = jnp.arange(head_size // 2, dtype=jnp.float32)
    frequency = 10000.0 ** (-(2.0 * indices / head_size))
    turned = positions.astype(jnp.float32)[:, None] * frequency[None, :]
    return (jnp.cos(turned)[:, None, :], jnp.sin(turned)[:, None, :])


def rotate(value, cosine, sine):
    half = value.shape[-1] // 2
    first = value[..., :half]
    second = value[..., half:]
    return jnp.concatenate([first * cosine - second * sine, second * cosine + first * sine], -1)


def dot(left, right):
    return jnp.dot(left, right, preferred_element_type=jnp.float32)


def contract_rows(left, right):
    return lax.dot_general(
        left, right, (((0,), (0,)), ((), ())), preferred_element_type=jnp.float32
    )


def contract_cols(left, right):
    return lax.dot_general(
        left, right, (((1,), (1,)), ((), ())), preferred_element_type=jnp.float32
    )


def mixing(current, weight, static):
    normed, scaled = norm_rows(current)
    active = jnp.tanh(jnp.einsum("tsd,dk->tsk", normed, weight, precision=PRECISE))
    table = active + static
    total = current.shape[1]
    branch_in = sum(table[:, i, 0][:, None] * current[:, i] for i in range(total))
    return (branch_in, table, active, normed, scaled)


def combine(current, branch_out, table):
    total = current.shape[1]
    return jnp.stack(
        [
            table[:, j, total + 1][:, None] * branch_out
            + sum(table[:, i, 1 + j][:, None] * current[:, i] for i in range(total))
            for j in range(total)
        ],
        1,
    )


def combine_back(current, table, grad_top):
    total = current.shape[1]
    grad_mixer = jnp.stack(
        [jnp.sum(current * grad_top[:, j][:, None], -1) for j in range(total)], -1
    )
    grad_current = jnp.stack(
        [
            sum(table[:, i, 1 + j][:, None] * grad_top[:, j] for j in range(total))
            for i in range(total)
        ],
        1,
    )
    return (grad_mixer, grad_current)


def branch_grad(table, grad_top):
    total = grad_top.shape[1]
    return sum(table[:, j, total + 1][:, None] * grad_top[:, j] for j in range(total))


def mixing_back(
    current, table, active, normed, scaled, weight, grad_in, grad_beta, grad_mixer, grad_current
):
    grad_alpha = jnp.sum(grad_in[:, None] * current, -1)
    grad_table = jnp.concatenate([grad_alpha[..., None], grad_mixer, grad_beta[..., None]], -1)
    grad_inner = grad_table * (1.0 - active * active)
    grad_weight = jnp.einsum("tsd,tsk->dk", normed, grad_inner, precision=PRECISE)
    grad_normed = jnp.einsum("tsk,dk->tsd", grad_inner, weight, precision=PRECISE)
    grad_current = (
        grad_current
        + table[..., 0][..., None] * grad_in[:, None, :]
        + norm_back(normed, scaled, grad_normed)
    )
    return (grad_current, grad_weight, jnp.sum(grad_table, 0))


def greet(partners):
    barrier = pltpu.get_barrier_semaphore()
    for partner in partners:
        pl.semaphore_signal(
            barrier, inc=1, device_id=partner, device_id_type=pl.DeviceIdType.MESH
        )
    pl.semaphore_wait(barrier, len(partners))


def send(source, target, sent, received, device):
    pltpu.make_async_remote_copy(
        src_ref=source,
        dst_ref=target,
        send_sem=sent,
        recv_sem=received,
        device_id=device,
        device_id_type=pl.DeviceIdType.MESH,
    ).start()


def landed(block, semaphore):
    pltpu.make_async_copy(block, block, semaphore).wait()


def ring(owners, cores):
    here = lax.axis_index("ctx")
    core = lax.axis_index("tensor")
    right, left = lax.rem(here + 1, owners), lax.rem(here + owners - 1, owners)
    return here, core, cores - 1 - core, right, left


def gather_first(values, outs, sems, owners, cores):
    local, sent_right, sent_left, sent_pair, came, came_pair = sems
    here, core, pair, right, left = ring(owners, cores)
    for i, (value, out) in enumerate(zip(values, outs)):
        target = out.at[here, core]

        @pl.when(here < owners - 1)
        def _():
            send(value, target, sent_right.at[i, here], came.at[i, here], {"ctx": right})

        @pl.when(here > 0)
        def _():
            send(value, target, sent_left.at[i, here], came.at[i, here], {"ctx": left})

        send(value, target, sent_pair.at[i, here], came_pair.at[i, here], {"tensor": pair})
        pltpu.make_async_copy(value, target, local.at[i]).start()


def gather_rest(values, outs, sems, owners, cores):
    local, sent_right, sent_left, sent_pair, came, came_pair = sems
    here, core, pair, right, left = ring(owners, cores)

    def arrive(i, out, block, onward, sent, device):
        held = out.at[block, core]
        landed(held, came.at[i, block])

        @pl.when(onward)
        def _():
            send(held, held, sent.at[i, block], came.at[i, block], device)

        send(held, held, sent_pair.at[i, block], came_pair.at[i, block], {"tensor": pair})

    for step in range(1, owners):
        for i, out in enumerate(outs):

            @pl.when(here >= step)
            def _():
                arrive(i, out, here - step, here < owners - 1, sent_right, {"ctx": right})

            @pl.when(here + step < owners)
            def _():
                arrive(i, out, here + step, here > 0, sent_left, {"ctx": left})

    for i, (value, out) in enumerate(zip(values, outs)):
        pltpu.make_async_copy(value, out.at[here, core], local.at[i]).wait()
        for block in range(owners):
            landed(out.at[block, pair], came_pair.at[i, block])
            landed(out.at[block, core], sent_pair.at[i, block])

            @pl.when((here < owners - 1) & (block <= here))
            def _():
                landed(out.at[block, core], sent_right.at[i, block])

            @pl.when((here > 0) & (block >= here))
            def _():
                landed(out.at[block, core], sent_left.at[i, block])


def gather_sems(amount, owners):
    return [pltpu.SemaphoreType.DMA((amount,))] + [
        pltpu.SemaphoreType.DMA((amount, owners)) for _ in range(5)
    ]


def line_partners(owners, cores):
    here, core, pair, right, left = ring(owners, cores)
    return [{"ctx": right}, {"ctx": left}, {"tensor": pair}]


def gather_kernel(amount, owners, cores, *refs):
    values, outs, sems = refs[:amount], refs[amount : 2 * amount], refs[2 * amount :]
    greet(line_partners(owners, cores))
    gather_first(values, outs, sems, owners, cores)
    gather_rest(values, outs, sems, owners, cores)


ANY = pl.BlockSpec(memory_space=pl.ANY)
INSIDE = pl.BlockSpec(memory_space=pltpu.VMEM)


def params(collective_id):
    return pltpu.CompilerParams(
        collective_id=collective_id, has_side_effects=True, vmem_limit_bytes=48 << 20
    )


def cost(micros):
    return pl.CostEstimate(flops=0, transcendentals=0, bytes_accessed=int(micros * 3.0e6))


def team_gather(collective_id, *values):
    owners, cores = lax.axis_size("ctx"), lax.axis_size("tensor")
    amount = len(values)
    outs = pl.pallas_call(
        functools.partial(gather_kernel, amount, owners, cores),
        out_shape=[jax.ShapeDtypeStruct((owners, cores, *v.shape), v.dtype) for v in values],
        in_specs=[ANY] * amount,
        out_specs=[ANY] * amount,
        scratch_shapes=gather_sems(amount, owners),
        compiler_params=params(collective_id),
        cost_estimate=cost(20 * amount),
        name="team_gather",
    )(*values)
    return [o.reshape(-1, v.shape[1]) for o, v in zip(outs, values)]


def swap_kernel(owners, value, out, sent, came):
    here = lax.axis_index("ctx")
    others = [lax.rem(here + step, owners) for step in range(1, owners)]
    greet([{"ctx": other} for other in others])
    out[here] = value[...]
    for other in others:
        send(value, out.at[here], sent.at[other], came.at[here], {"ctx": other})
    for other in others:
        landed(out.at[other], came.at[other])
        landed(value, sent.at[other])


def team_swap(collective_id, value):
    owners = lax.axis_size("ctx")
    return pl.pallas_call(
        functools.partial(swap_kernel, owners),
        out_shape=jax.ShapeDtypeStruct((owners, *value.shape), value.dtype),
        in_specs=[INSIDE],
        out_specs=INSIDE,
        scratch_shapes=[pltpu.SemaphoreType.DMA((owners,))] * 2,
        compiler_params=params(collective_id),
        cost_estimate=cost(3),
        name="team_swap",
    )(value)


def plane(index, shards_in):
    across_x = index + 1 - 2 * lax.rem(index, 2)
    return across_x, lax.rem(index + 2, shards_in), lax.rem(across_x + 2, shards_in)


def open_kernel(shards_in, owners, cores, *refs):
    value, w_query, w_key, w_value, w_output, out, qkv, out_w = refs[:8]
    own_sem, sent_w, came_w, passed_w = refs[8:12]
    sems = refs[12:]
    index = lax.axis_index("shard")
    here = lax.axis_index("ctx")
    depth = w_query.shape[0]
    count = w_query.shape[1] // owners
    columns = pl.ds(pl.multiple_of(here * count, count), count)
    sources = [w.at[:, columns] for w in (w_query, w_key, w_value)] + [w_output.at[columns, :]]

    def target(weight, block):
        if weight == 3:
            wide = w_output.shape[1]
            return out_w.at[:, pl.ds(pl.multiple_of(block * wide, wide), wide)]
        rows = pl.ds(pl.multiple_of(block * depth, depth), depth)
        return qkv.at[rows, pl.ds(weight * count, count)]

    others = [lax.rem(index + step, shards_in) for step in range(1, shards_in)]
    greet([{"shard": other} for other in others] + line_partners(owners, cores))
    square = shards_in == 4
    near = plane(index, shards_in)[:2] if square else others
    for weight in range(4):
        for other in near:
            send(
                sources[weight],
                target(weight, index),
                sent_w.at[weight, other],
                came_w.at[weight, index],
                {"shard": other},
            )
    gather_first([value], [out], sems, owners, cores)
    for weight in range(4):
        pltpu.make_async_copy(
            sources[weight], target(weight, index), own_sem.at[weight]
        ).start()
    if square:
        across_x, across_y, far = plane(index, shards_in)
        for weight, source, device in (
            (0, across_x, across_y),
            (2, across_y, across_x),
            (1, across_x, across_y),
            (3, across_y, across_x),
        ):
            held = target(weight, source)
            landed(held, came_w.at[weight, source])
            send(
                held, held, passed_w.at[weight], came_w.at[weight, source], {"shard": device}
            )
    gather_rest([value], [out], sems, owners, cores)
    for weight in range(4):
        pltpu.make_async_copy(
            sources[weight], target(weight, index), own_sem.at[weight]
        ).wait()
        for other in near:
            landed(sources[weight], sent_w.at[weight, other])
    if square:
        for weight, source in ((0, across_y), (2, across_x), (1, across_y), (3, across_x)):
            landed(target(weight, source), came_w.at[weight, source])
        for weight in range(4):
            landed(target(weight, far), came_w.at[weight, far])
            landed(sources[weight], passed_w.at[weight])
    else:
        for weight in range(4):
            for other in others:
                landed(target(weight, other), came_w.at[weight, other])


def open_team(collective_id, value, weights):
    shards_in, owners, cores = [lax.axis_size(a) for a in ("shard", "ctx", "tensor")]
    depth = weights[0].shape[0]
    count = weights[0].shape[1] // owners
    out, qkv, out_w = pl.pallas_call(
        functools.partial(open_kernel, shards_in, owners, cores),
        out_shape=[
            jax.ShapeDtypeStruct((owners, cores, *value.shape), value.dtype),
            jax.ShapeDtypeStruct((shards_in * depth, 3 * count), value.dtype),
            jax.ShapeDtypeStruct((count, shards_in * weights[3].shape[1]), value.dtype),
        ],
        in_specs=[ANY] * 5,
        out_specs=[ANY] * 3,
        scratch_shapes=[
            pltpu.SemaphoreType.DMA((4,)),
            pltpu.SemaphoreType.DMA((4, shards_in)),
            pltpu.SemaphoreType.DMA((4, shards_in)),
            pltpu.SemaphoreType.DMA((4,)),
        ]
        + gather_sems(1, owners),
        compiler_params=params(collective_id),
        cost_estimate=cost(40),
        name="open_team",
    )(value, *weights)
    return out.reshape(-1, value.shape[1]), qkv, out_w


def scatter_kernel(amount, owners, cores, *refs):
    parts, outs = refs[:amount], refs[amount : 2 * amount]
    pairs, halves, from_left, from_right = [
        refs[k * amount : (k + 1) * amount] for k in range(2, 6)
    ]
    total, sent_pair, came_pair, sent, came_left, came_right = refs[6 * amount :]
    here, core, pair, right, left = ring(owners, cores)
    greet(line_partners(owners, cores))
    order = [k // 2 if k % 2 else owners - 1 - k // 2 for k in range(owners)]
    for i in range(amount):
        for block in order:
            send(
                parts[i].at[block, pair],
                pairs[i].at[block],
                sent_pair.at[i, block],
                came_pair.at[i, block],
                {"tensor": pair},
            )

    def add_up(i, block, more, arrived, came):
        landed(pairs[i].at[block], came_pair.at[i, block])
        total[...] = parts[i][block, core].astype(jnp.float32) + pairs[i][block].astype(
            jnp.float32
        )

        @pl.when(more)
        def _():
            landed(arrived[i].at[block], came.at[i, block])
            total[...] += arrived[i][block].astype(jnp.float32)

    def pass_on(i, block, more, arrived, came, device):
        add_up(i, block, more, arrived, came)
        halves[i][block] = total[...].astype(halves[i].dtype)
        send(
            halves[i].at[block],
            arrived[i].at[block],
            sent.at[i, block],
            came.at[i, block],
            {"ctx": device},
        )

    for step in range(2 * owners - 2):
        for i in range(amount):
            rightward = owners - 1 - (step - here)
            leftward = step - (owners - 1 - here)

            @pl.when((rightward > here) & (step >= here))
            def _():
                pass_on(i, rightward, here > 0, from_left, came_left, right)

            @pl.when((leftward >= 0) & (leftward < here))
            def _():
                pass_on(i, leftward, here < owners - 1, from_right, came_right, left)

    for i in range(amount):
        add_up(i, here, here > 0, from_left, came_left)

        @pl.when(here < owners - 1)
        def _():
            landed(from_right[i].at[here], came_right.at[i, here])
            total[...] += from_right[i][here].astype(jnp.float32)

        outs[i][...] = total[...]
    for i in range(amount):
        for block in range(owners):
            landed(pairs[i].at[block], sent_pair.at[i, block])

            @pl.when(block != here)
            def _():
                landed(halves[i].at[block], sent.at[i, block])


def team_sum(collective_id, *values):
    owners, cores = lax.axis_size("ctx"), lax.axis_size("tensor")
    amount = len(values)
    width = values[0].shape[1]
    mine = values[0].shape[0] // (owners * cores)
    blocks = [pltpu.VMEM((owners, mine, width), v.dtype) for v in values]
    return pl.pallas_call(
        functools.partial(scatter_kernel, amount, owners, cores),
        out_shape=[jax.ShapeDtypeStruct((mine, width), jnp.float32)] * amount,
        in_specs=[INSIDE] * amount,
        out_specs=[INSIDE] * amount,
        scratch_shapes=blocks * 4
        + [pltpu.VMEM((mine, width), jnp.float32)]
        + [pltpu.SemaphoreType.DMA((amount, owners)) for _ in range(5)],
        compiler_params=params(collective_id),
        cost_estimate=cost(20 * amount),
        name="team_sum",
    )(*[v.reshape(owners, cores, mine, width) for v in values])


def close_kernel(amount, shards_in, owners, cores, *refs):
    values, mixed = refs[:amount], refs[amount]
    outs, summed = refs[amount + 1 : 2 * amount + 1], refs[2 * amount + 1]
    pairs, half, quarters, blocks, local, sent, came = refs[2 * amount + 2 : 2 * amount + 9]
    sent_c, came_c, sent_s, came_s, sent_b, came_b = refs[2 * amount + 9 :]
    here, core, pair, right, left = ring(owners, cores)
    index = lax.axis_index("shard")
    around = [lax.rem(here + step, owners) for step in range(1, owners)]
    others = [lax.rem(index + step, shards_in) for step in range(1, shards_in)]
    greet(
        [{"tensor": pair}]
        + [{"ctx": other} for other in around]
        + [{"shard": other} for other in others]
    )
    wide = mixed.shape[1] // cores
    thin = wide // owners
    send(
        mixed.at[:, pl.ds(pl.multiple_of(pair * wide, wide), wide)],
        pairs,
        sent.at[amount],
        came.at[amount],
        {"tensor": pair},
    )
    for i in range(amount):
        target = outs[i].at[:, core]
        send(values[i], target, sent.at[i], came.at[i], {"tensor": pair})
        pltpu.make_async_copy(values[i], target, local.at[i]).start()
    landed(pairs, came.at[amount])
    half[...] = mixed[:, pl.ds(pl.multiple_of(core * wide, wide), wide)] + pairs[...]
    for other in around:
        send(
            half.at[:, pl.ds(pl.multiple_of(other * thin, thin), thin)],
            quarters.at[here],
            sent_c.at[other],
            came_c.at[here],
            {"ctx": other},
        )
    total = half[:, pl.ds(pl.multiple_of(here * thin, thin), thin)]
    for other in around:
        landed(quarters.at[other], came_c.at[other])
        total += quarters[other]
    blocks[index] = total
    for other in others:
        send(
            blocks.at[index], blocks.at[index], sent_s.at[other], came_s.at[index], {"shard": other}
        )
    for other in others:
        landed(blocks.at[other], came_s.at[other])
    total = blocks[0]
    for block in range(1, shards_in):
        total += blocks[block]

    def place(owner, half_of):
        return summed.at[half_of * owners + owner]

    summed[core * owners + here] = total
    for other in around:
        send(place(here, core), place(here, core), sent_b.at[other], came_b.at[here, core], {"ctx": other})
    send(place(here, core), place(here, core), sent_b.at[here], came_b.at[here, core], {"tensor": pair})
    for other in around:
        landed(place(other, core), came_b.at[other, core])
        send(
            place(other, core),
            place(other, core),
            sent_b.at[owners + other],
            came_b.at[other, core],
            {"tensor": pair},
        )
    for owner in range(owners):
        landed(place(owner, pair), came_b.at[owner, pair])
        landed(place(owner, core), sent_b.at[owner])
    for other in around:
        landed(place(other, core), sent_b.at[owners + other])
        landed(quarters.at[other], sent_c.at[other])
    for other in others:
        landed(blocks.at[other], sent_s.at[other])
    landed(pairs, sent.at[amount])
    for i in range(amount):
        target = outs[i].at[:, core]
        landed(outs[i].at[:, pair], came.at[i])
        landed(target, sent.at[i])
        pltpu.make_async_copy(values[i], target, local.at[i]).wait()


def close_team(collective_id, mixed, *values):
    shards_in, owners, cores = [lax.axis_size(a) for a in ("shard", "ctx", "tensor")]
    amount = len(values)
    height, width = mixed.shape
    thin = width // (cores * owners)
    out = pl.pallas_call(
        functools.partial(close_kernel, amount, shards_in, owners, cores),
        out_shape=[
            jax.ShapeDtypeStruct((v.shape[0], cores, *v.shape[1:]), v.dtype) for v in values
        ]
        + [jax.ShapeDtypeStruct((cores * owners, height, thin), jnp.float32)],
        in_specs=[ANY] * amount + [INSIDE],
        out_specs=[ANY] * amount + [INSIDE],
        scratch_shapes=[
            pltpu.VMEM((height, width // cores), jnp.float32),
            pltpu.VMEM((height, width // cores), jnp.float32),
            pltpu.VMEM((owners, height, thin), jnp.float32),
            pltpu.VMEM((shards_in, height, thin), jnp.float32),
            pltpu.SemaphoreType.DMA((amount,)),
            pltpu.SemaphoreType.DMA((amount + 1,)),
            pltpu.SemaphoreType.DMA((amount + 1,)),
            pltpu.SemaphoreType.DMA((owners,)),
            pltpu.SemaphoreType.DMA((owners,)),
            pltpu.SemaphoreType.DMA((shards_in,)),
            pltpu.SemaphoreType.DMA((shards_in,)),
            pltpu.SemaphoreType.DMA((2 * owners,)),
            pltpu.SemaphoreType.DMA((owners, cores)),
        ],
        compiler_params=params(collective_id),
        cost_estimate=cost(10),
        name="close_team",
    )(*values, mixed)
    return out[-1].transpose(1, 0, 2).reshape(height, width), *out[:-1]


def shards(
    streams,
    lengths,
    destination,
    w_query,
    w_key,
    w_value,
    w_output,
    w_gate,
    w_up,
    w_down,
    mix_weight,
    mix_static,
    cotangent,
):
    rows_here, stream_total, width = streams.shape
    owners = lax.axis_size("ctx")
    cores = lax.axis_size("tensor")
    here = lax.axis_index("ctx")
    core = lax.axis_index("tensor")
    run_rows = rows_here // owners
    part = run_rows // cores
    mine = rows_here // cores
    group_rows = rows_here * owners
    head_cols = w_query.shape[1] // owners
    heads = head_cols // HD
    units = w_gate.shape[1] // owners
    scale = HD ** (-0.5)

    def columns(weight, count):
        return lax.dynamic_slice_in_dim(weight, here * count, count, 1)

    def rows(weight, count):
        return lax.dynamic_slice_in_dim(weight, here * count, count, 0)

    down = lax.all_gather(rows(w_down, units).T, "shard", axis=0, tiled=True)

    order = jnp.arange(group_rows, dtype=jnp.int32)
    within = order % mine
    placed = (
        order // rows_here * rows_here
        + within // part * run_rows
        + order % rows_here // mine * part
        + within % part
    )
    spans = lengths[0]
    count = jnp.arange(spans.shape[0], dtype=jnp.int32)
    ends = jnp.sum(jnp.where(count[None, :] <= count[:, None], spans[None, :], 0), 1)
    starts = ends - spans
    segment = jnp.sum((placed[:, None] >= ends[None, :]).astype(jnp.int32), axis=1)
    begin = jnp.max(jnp.where(starts[None, :] <= placed[:, None], starts[None, :], 0), axis=1)
    position = placed - begin

    local_dest = destination - lax.axis_index("shard") * group_rows
    heads_of_runs = local_dest.reshape(owners, run_rows)[:, 0]
    every = team_swap(6, jnp.broadcast_to(jnp.pad(heads_of_runs, (0, 128 - owners)), (8, 128)))
    every = every[:, 0, :owners]
    sent = jnp.sum(jnp.where(every // rows_here == here, every % rows_here, 0), 1) + core * part
    packed = jnp.concatenate(
        [lax.dynamic_slice_in_dim(cotangent, sent[c], part, 0) for c in range(owners)], 0
    )
    arrived = lax.all_to_all(packed, "ctx", split_axis=0, concat_axis=0, tiled=True)
    came_from = heads_of_runs // rows_here * part
    grad_top = jnp.concatenate(
        [lax.dynamic_slice_in_dim(arrived, came_from[r], part, 0) for r in range(owners)], 0
    ).astype(jnp.float32)

    def own_rows(value):
        split = value.reshape(owners, cores, part, stream_total, width)
        return lax.dynamic_index_in_dim(split, core, 1, keepdims=False).reshape(
            mine, stream_total, width
        )

    current = own_rows(streams).astype(jnp.float32)
    branch_in, table_one, active_one, normed_one, scaled_one = mixing(
        current, mix_weight[0], mix_static[0]
    )
    attn_normed, attn_scaled = norm_rows(branch_in)
    attn_input, qkv, out_w = open_team(
        0, attn_normed.astype(jnp.bfloat16), (w_query, w_key, w_value, w_output)
    )
    gate_up = jnp.concatenate([columns(w, units) for w in (w_gate, w_up)], 1)
    attn_input, gate_up = lax.optimization_barrier((attn_input, gate_up))
    gate_up = lax.all_gather(gate_up, "shard", axis=0, tiled=True)
    cosine, sine = angles(position, HD)
    lin = dot(attn_input, qkv).reshape(group_rows, 3, heads, HD)
    queries = rotate(lin[:, 0], cosine, sine).astype(jnp.bfloat16)
    keys = rotate(lin[:, 1], cosine, sine).astype(jnp.bfloat16)
    values = lin[:, 2].astype(jnp.bfloat16)
    allowed = (segment[:, None] == segment[None, :]) & (position[None, :] <= position[:, None])
    scores = jnp.einsum("qhd,khd->hqk", queries, keys, preferred_element_type=jnp.float32) * scale
    scores = jnp.where(allowed[None], scores, FLOOR_SCORE)
    top = jnp.max(scores, -1, keepdims=True)
    probs = jnp.where(allowed[None], jnp.exp(scores - top), 0.0)
    probs = probs / jnp.sum(probs, -1, keepdims=True)
    probs_low = probs.astype(jnp.bfloat16)
    attended = jnp.einsum("hqk,khd->qhd", probs_low, values, preferred_element_type=jnp.float32)
    attended = attended.reshape(group_rows, head_cols).astype(jnp.bfloat16)
    [attn_out] = team_sum(1, dot(attended, out_w))

    middle = combine(current, attn_out, table_one)
    branch_two, table_two, active_two, normed_two, scaled_two = mixing(
        middle, mix_weight[1], mix_static[1]
    )
    ffn_normed, ffn_scaled = norm_rows(branch_two)
    ffn_input, grad_ffn_out = team_gather(
        2, ffn_normed.astype(jnp.bfloat16), branch_grad(table_two, grad_top).astype(jnp.bfloat16)
    )
    both = dot(ffn_input, gate_up)
    gate, upward = both[:, :units], both[:, units:]
    sigma = jax.nn.sigmoid(gate)
    hidden = (gate * sigma * upward).astype(jnp.bfloat16)
    ffn_part = contract_cols(hidden, down).astype(jnp.bfloat16)
    grad_hidden = dot(grad_ffn_out, down)
    grad_both = jnp.concatenate(
        [
            (grad_hidden * upward * sigma * (1.0 + gate * (1.0 - sigma))).astype(jnp.bfloat16),
            (grad_hidden * gate * sigma).astype(jnp.bfloat16),
        ],
        1,
    )
    ffn_input_part = contract_cols(grad_both, gate_up).astype(jnp.bfloat16)
    down_part = contract_rows(grad_ffn_out, hidden).astype(jnp.bfloat16)
    gate_up_part = contract_rows(ffn_input, grad_both).astype(jnp.bfloat16)
    ffn_part, ffn_input_part, down_part, gate_up_part = lax.optimization_barrier(
        (ffn_part, ffn_input_part, down_part, gate_up_part)
    )

    def shard_sum(partial):
        return lax.psum_scatter(partial, "shard", scatter_dimension=0, tiled=True)

    def to_owner_rows(summed):
        moved = lax.all_to_all(summed, "ctx", split_axis=0, concat_axis=0, tiled=True)
        return moved.reshape(owners, summed.shape[0] // owners, summed.shape[1])

    def row_part(moved, first, count):
        cut = moved[:, :, first : first + count]
        return cut.transpose(1, 0, 2).reshape(moved.shape[1], -1).astype(jnp.float32)

    def column_part(moved, first, count):
        cut = moved[:, :, first : first + count]
        return cut.transpose(0, 2, 1).reshape(-1, moved.shape[1]).astype(jnp.float32)

    down_sum = shard_sum(down_part)
    gate_up_sum = shard_sum(gate_up_part)
    ffn_out, grad_ffn_input = team_sum(3, ffn_part, ffn_input_part)
    grad_beta = jnp.sum(grad_top * ffn_out[:, None], -1)
    grad_mixer, grad_middle = combine_back(middle, table_two, grad_top)
    grad_branch_two = norm_back(ffn_normed, ffn_scaled, grad_ffn_input)
    grad_middle, grad_weight_two, grad_static_two = mixing_back(
        middle,
        table_two,
        active_two,
        normed_two,
        scaled_two,
        mix_weight[1],
        grad_branch_two,
        grad_beta,
        grad_mixer,
        grad_middle,
    )
    grad_attn_low, down_sum = lax.optimization_barrier(
        (branch_grad(table_one, grad_middle).astype(jnp.bfloat16), down_sum)
    )
    [grad_attn_out] = team_gather(4, grad_attn_low)
    final = combine(middle, ffn_out, table_two).astype(jnp.bfloat16)

    grad_attended = (
        contract_cols(grad_attn_out, out_w).astype(jnp.bfloat16).reshape(group_rows, heads, HD)
    )
    grad_probs = jnp.einsum(
        "qhd,khd->hqk", grad_attended, values, preferred_element_type=jnp.float32
    )
    delta = jnp.sum(probs * grad_probs, -1, keepdims=True)
    grad_scores = (probs * (grad_probs - delta)).astype(jnp.bfloat16)
    grad_query_rot = (
        jnp.einsum("hqk,khd->qhd", grad_scores, keys, preferred_element_type=jnp.float32) * scale
    )
    grad_key_rot = (
        jnp.einsum("hqk,qhd->khd", grad_scores, queries, preferred_element_type=jnp.float32)
        * scale
    )
    grad_value_vec = jnp.einsum(
        "hqk,qhd->khd", probs_low, grad_attended, preferred_element_type=jnp.float32
    )
    grad_lin = jnp.concatenate(
        [
            rotate(grad_query_rot, cosine, -sine).reshape(group_rows, head_cols),
            rotate(grad_key_rot, cosine, -sine).reshape(group_rows, head_cols),
            grad_value_vec.reshape(group_rows, head_cols),
        ],
        1,
    ).astype(jnp.bfloat16)
    attn_input_part = contract_cols(grad_lin, qkv).astype(jnp.bfloat16)
    attn_part = jnp.concatenate(
        [contract_rows(attn_input, grad_lin), contract_rows(grad_attn_out, attended)], 1
    ).astype(jnp.bfloat16)
    attn_input_part, attn_part, gate_up_sum = lax.optimization_barrier(
        (attn_input_part, attn_part, gate_up_sum)
    )
    grad_down = column_part(to_owner_rows(down_sum), 0, units)
    moved = to_owner_rows(gate_up_sum)
    grad_gate, grad_up = row_part(moved, 0, units), row_part(moved, units, units)
    attn_sum = shard_sum(attn_part)
    [grad_attn_input] = team_sum(5, attn_input_part)
    moved = to_owner_rows(attn_sum)
    grad_query, grad_key, grad_value = [
        row_part(moved, i * head_cols, head_cols) for i in range(3)
    ]
    grad_output = column_part(moved, 3 * head_cols, head_cols)

    grad_beta = jnp.sum(grad_middle * attn_out[:, None], -1)
    grad_mixer, grad_current = combine_back(current, table_one, grad_middle)
    grad_branch_one = norm_back(attn_normed, attn_scaled, grad_attn_input)
    grad_current, grad_weight_one, grad_static_one = mixing_back(
        current,
        table_one,
        active_one,
        normed_one,
        scaled_one,
        mix_weight[0],
        grad_branch_one,
        grad_beta,
        grad_mixer,
        grad_current,
    )
    statics = jnp.stack([grad_static_one, grad_static_two])
    mixed = jnp.concatenate(
        [
            grad_weight_one.T,
            grad_weight_two.T,
            jnp.pad(statics.reshape(1, -1), ((0, 3), (0, width - statics.size))),
        ],
        0,
    )

    def runs(value):
        return value.astype(jnp.bfloat16).reshape(owners, part, stream_total, width)

    mixed, streams_out, grad_streams = close_team(7, mixed, runs(final), runs(grad_current))
    tables = 2 * mix_weight.shape[2]
    grad_mix_weight = mixed[:tables].reshape(2, -1, width).transpose(0, 2, 1)
    grad_mix_static = mixed[tables, : statics.size].reshape(statics.shape)

    return (
        streams_out.reshape(rows_here, stream_total, width),
        grad_streams.reshape(rows_here, stream_total, width),
        grad_query,
        grad_key,
        grad_value,
        grad_output,
        grad_gate,
        grad_up,
        grad_down,
        grad_mix_weight,
        grad_mix_static,
    )


def solution(mesh):
    return jax.shard_map(
        shards,
        mesh=mesh,
        in_specs=(
            P(("shard", "ctx"), None, None),
            P("shard", None),
            P(("shard", "ctx")),
            P("shard", "tensor"),
            P("shard", "tensor"),
            P("shard", "tensor"),
            P("tensor", "shard"),
            P("shard", "tensor"),
            P("shard", "tensor"),
            P("tensor", "shard"),
            P(),
            P(),
            P(("shard", "ctx"), None, None),
        ),
        out_specs=(
            P(("shard", "ctx"), None, None),
            P(("shard", "ctx"), None, None),
            P(("shard", "ctx"), "tensor"),
            P(("shard", "ctx"), "tensor"),
            P(("shard", "ctx"), "tensor"),
            P("tensor", ("shard", "ctx")),
            P(("shard", "ctx"), "tensor"),
            P(("shard", "ctx"), "tensor"),
            P("tensor", ("shard", "ctx")),
            P(),
            P(),
        ),
        check_vma=False,
    )
```

```python
import functools

import jax
import jax.numpy as jnp
import numpy as np
from jax import lax
from jax.experimental import pallas as pl
from jax.experimental.pallas import tpu as pltpu
from jax.sharding import PartitionSpec as P

HD = 128


PRECISE = lax.Precision.HIGHEST
EPSILON = 1e-05
FLOOR_SCORE = -1e30
BLOCKS = 4


def mean_of(value):
    width = value.shape[-1]
    while value.shape[-1] > 128 and value.shape[-1] % 256 == 0:
        half = value.shape[-1] // 2
        value = value[..., :half] + value[..., half:]
    return jnp.sum(value, -1, keepdims=True) * (1.0 / width)


def norm_rows(value):
    centred = value - mean_of(value)
    scaled = lax.rsqrt(mean_of(centred * centred) + EPSILON)
    return (centred * scaled, scaled)


def norm_back(normed, scaled, grad):
    return scaled * (grad - mean_of(grad) - normed * mean_of(grad * normed))


def angles(positions, head_size):
    indices = np.arange(head_size // 2, dtype=np.float64)
    frequency = (10000.0 ** (-(2.0 * indices / head_size))).astype(np.float32)
    turned = positions.astype(jnp.float32)[:, None] * frequency[None, :]
    return (jnp.cos(turned)[:, None, :], jnp.sin(turned)[:, None, :])


def dot(left, right):
    return jnp.dot(left, right, preferred_element_type=jnp.float32)


def contract_rows(left, right):
    return lax.dot_general(
        left, right, (((0,), (0,)), ((), ())), preferred_element_type=jnp.float32
    )


def contract_cols(left, right):
    return lax.dot_general(
        left, right, (((1,), (1,)), ((), ())), preferred_element_type=jnp.float32
    )


def greet(partners):
    barrier = pltpu.get_barrier_semaphore()
    for partner in partners:
        pl.semaphore_signal(
            barrier, inc=1, device_id=partner, device_id_type=pl.DeviceIdType.MESH
        )
    pl.semaphore_wait(barrier, len(partners))


def send(source, target, sent, received, device):
    pltpu.make_async_remote_copy(
        src_ref=source,
        dst_ref=target,
        send_sem=sent,
        recv_sem=received,
        device_id=device,
        device_id_type=pl.DeviceIdType.MESH,
    ).start()


def landed(block, semaphore):
    pltpu.make_async_copy(block, block, semaphore).wait()


def ring(owners, cores):
    here = lax.axis_index("ctx")
    core = lax.axis_index("tensor")
    right, left = lax.rem(here + 1, owners), lax.rem(here + owners - 1, owners)
    return here, core, cores - 1 - core, right, left


def gather_first(values, outs, sems, owners, cores):
    local, sent_right, sent_left, sent_pair, came, came_pair = sems
    here, core, pair, right, left = ring(owners, cores)
    for i, (value, out) in enumerate(zip(values, outs)):
        target = out.at[here, core]

        @pl.when(here < owners - 1)
        def _():
            send(value, target, sent_right.at[i, here], came.at[i, here], {"ctx": right})

        @pl.when(here > 0)
        def _():
            send(value, target, sent_left.at[i, here], came.at[i, here], {"ctx": left})

        send(value, target, sent_pair.at[i, here], came_pair.at[i, here], {"tensor": pair})
        pltpu.make_async_copy(value, target, local.at[i]).start()


def gather_rest(values, outs, sems, owners, cores):
    local, sent_right, sent_left, sent_pair, came, came_pair = sems
    here, core, pair, right, left = ring(owners, cores)

    def arrive(i, out, block, onward, sent, device):
        held = out.at[block, core]
        landed(held, came.at[i, block])

        @pl.when(onward)
        def _():
            send(held, held, sent.at[i, block], came.at[i, block], device)

        send(held, held, sent_pair.at[i, block], came_pair.at[i, block], {"tensor": pair})

    for step in range(1, owners):
        for i, out in enumerate(outs):

            @pl.when(here >= step)
            def _():
                arrive(i, out, here - step, here < owners - 1, sent_right, {"ctx": right})

            @pl.when(here + step < owners)
            def _():
                arrive(i, out, here + step, here > 0, sent_left, {"ctx": left})

    for i, (value, out) in enumerate(zip(values, outs)):
        pltpu.make_async_copy(value, out.at[here, core], local.at[i]).wait()
        for block in range(owners):
            landed(out.at[block, pair], came_pair.at[i, block])
            landed(out.at[block, core], sent_pair.at[i, block])

            @pl.when((here < owners - 1) & (block <= here))
            def _():
                landed(out.at[block, core], sent_right.at[i, block])

            @pl.when((here > 0) & (block >= here))
            def _():
                landed(out.at[block, core], sent_left.at[i, block])


def gather_sems(amount, owners):
    return [pltpu.SemaphoreType.DMA((amount,))] + [
        pltpu.SemaphoreType.DMA((amount, owners)) for _ in range(5)
    ]


def line_partners(owners, cores):
    here, core, pair, right, left = ring(owners, cores)
    return [{"ctx": right}, {"ctx": left}, {"tensor": pair}]


def gather_kernel(amount, owners, cores, *refs):
    values, outs, sems = refs[:amount], refs[amount : 2 * amount], refs[2 * amount :]
    greet(line_partners(owners, cores))
    gather_first(values, outs, sems, owners, cores)
    gather_rest(values, outs, sems, owners, cores)


ANY = pl.BlockSpec(memory_space=pl.ANY)
FAR = pl.BlockSpec(memory_space=pltpu.HBM)
INSIDE = pl.BlockSpec(memory_space=pltpu.VMEM)


def params(collective_id):
    return pltpu.CompilerParams(
        collective_id=collective_id, has_side_effects=True, vmem_limit_bytes=48 << 20
    )


def cost(micros):
    return pl.CostEstimate(flops=0, transcendentals=0, bytes_accessed=int(micros * 3.0e6))


def team_gather(collective_id, *values):
    owners, cores = lax.axis_size("ctx"), lax.axis_size("tensor")
    amount = len(values)
    outs = pl.pallas_call(
        functools.partial(gather_kernel, amount, owners, cores),
        out_shape=[jax.ShapeDtypeStruct((owners, cores, *v.shape), v.dtype) for v in values],
        in_specs=[ANY] * amount,
        out_specs=[ANY] * amount,
        scratch_shapes=gather_sems(amount, owners),
        compiler_params=params(collective_id),
        cost_estimate=cost(20 * amount),
        name="team_gather",
    )(*values)
    return [o.reshape(-1, v.shape[1]) for o, v in zip(outs, values)]


def plane(index, shards_in):
    across_x = index + 1 - 2 * lax.rem(index, 2)
    return across_x, lax.rem(index + 2, shards_in), lax.rem(across_x + 2, shards_in)


def open_kernel(shards_in, owners, cores, *refs):
    value, w_query, w_key, w_value, w_output, w_gate, w_up, w_down, note = refs[:9]
    out, qkv, out_w, packed, notes = refs[9:14]
    own_sem, sent_w, came_w, passed_w, sent_n, came_n, pack_sem, load_sem = refs[14:22]
    stage, stage_out, stage_pack = refs[22:25]
    sems = refs[25:]
    index = lax.axis_index("shard")
    here = lax.axis_index("ctx")
    depth = w_query.shape[0]
    count = w_query.shape[1] // owners
    columns = pl.ds(pl.multiple_of(here * count, count), count)
    stored = [w.at[:, columns] for w in (w_query, w_key, w_value)] + [w_output.at[columns, :]]
    sources = [stage.at[0], stage.at[1], stage.at[2], stage_out]
    for k, (slow, source) in enumerate(zip(stored, sources)):
        pltpu.make_async_copy(slow, source, load_sem.at[k]).start()

    def target(weight, block):
        if weight == 3:
            wide = w_output.shape[1]
            return out_w.at[:, pl.ds(pl.multiple_of(block * wide, wide), wide)]
        rows = pl.ds(pl.multiple_of(block * depth, depth), depth)
        return qkv.at[rows, pl.ds(weight * count, count)]

    others = [lax.rem(index + step, shards_in) for step in range(1, shards_in)]
    greet(around("shard", shards_in) + around("ctx", owners) + around("tensor", cores))
    units = w_gate.shape[1] // owners
    hidden = pl.ds(pl.multiple_of(here * units, units), units)
    wide_down = w_down.shape[1]
    pieces = [
        (w_gate.at[:, hidden], stage_pack.at[:, pl.ds(0, units)]),
        (w_up.at[:, hidden], stage_pack.at[:, pl.ds(units, units)]),
    ]
    for k in range(units // depth):
        start = pl.multiple_of(here * units + k * depth, depth)
        place = pl.ds(2 * units + k * wide_down, wide_down)
        pieces.append((w_down.at[pl.ds(start, depth), :], stage_pack.at[:, place]))
    for k, (source, place) in enumerate(pieces):
        pltpu.make_async_copy(source, place, pack_sem.at[k]).start()
    notes[here] = note[...]
    fellows = [lax.rem(here + step, owners) for step in range(1, owners)]
    for fellow in fellows:
        send(note, notes.at[here], sent_n.at[fellow], came_n.at[here], {"ctx": fellow})
    square = shards_in == 4
    near = plane(index, shards_in)[:2] if square else others
    for weight in range(4):
        pltpu.make_async_copy(stored[weight], sources[weight], load_sem.at[weight]).wait()
        for other in near:
            send(
                sources[weight],
                target(weight, index),
                sent_w.at[weight, other],
                came_w.at[weight, index],
                {"shard": other},
            )
    gather_first([value], [out], sems, owners, cores)
    for weight in range(4):
        pltpu.make_async_copy(
            sources[weight], target(weight, index), own_sem.at[weight]
        ).start()
    for k, (source, place) in enumerate(pieces):
        pltpu.make_async_copy(source, place, pack_sem.at[k]).wait()
    pltpu.make_async_copy(stage_pack, packed, load_sem.at[4]).start()
    if square:
        across_x, across_y, far = plane(index, shards_in)
        for weight, source, device in (
            (0, across_x, across_y),
            (2, across_y, across_x),
            (1, across_x, across_y),
            (3, across_y, across_x),
        ):
            held = target(weight, source)
            landed(held, came_w.at[weight, source])
            send(
                held, held, passed_w.at[weight], came_w.at[weight, source], {"shard": device}
            )
    gather_rest([value], [out], sems, owners, cores)
    for fellow in fellows:
        landed(notes.at[fellow], came_n.at[fellow])
        landed(note, sent_n.at[fellow])
    pltpu.make_async_copy(stage_pack, packed, load_sem.at[4]).wait()
    for weight in range(4):
        pltpu.make_async_copy(
            sources[weight], target(weight, index), own_sem.at[weight]
        ).wait()
        for other in near:
            landed(sources[weight], sent_w.at[weight, other])
    if square:
        for weight, source in ((0, across_y), (2, across_x), (1, across_y), (3, across_x)):
            landed(target(weight, source), came_w.at[weight, source])
        for weight in range(4):
            landed(target(weight, far), came_w.at[weight, far])
            landed(sources[weight], passed_w.at[weight])
    else:
        for weight in range(4):
            for other in others:
                landed(target(weight, other), came_w.at[weight, other])


def open_team(collective_id, value, weights, note):
    shards_in, owners, cores = [lax.axis_size(a) for a in ("shard", "ctx", "tensor")]
    depth = weights[0].shape[0]
    count = weights[0].shape[1] // owners
    units = weights[4].shape[1] // owners
    pieces = 2 + units // depth
    out, qkv, out_w, packed, notes = pl.pallas_call(
        functools.partial(open_kernel, shards_in, owners, cores),
        out_shape=[
            jax.ShapeDtypeStruct((owners, cores, *value.shape), value.dtype),
            jax.ShapeDtypeStruct((shards_in * depth, 3 * count), value.dtype),
            jax.ShapeDtypeStruct((count, shards_in * weights[3].shape[1]), value.dtype),
            jax.ShapeDtypeStruct((depth, 3 * units), value.dtype),
            jax.ShapeDtypeStruct((owners, *note.shape), note.dtype),
        ],
        in_specs=[ANY] + [FAR] * 7 + [INSIDE],
        out_specs=[ANY] * 3 + [FAR] + [INSIDE],
        scratch_shapes=[
            pltpu.SemaphoreType.DMA((4,)),
            pltpu.SemaphoreType.DMA((4, shards_in)),
            pltpu.SemaphoreType.DMA((4, shards_in)),
            pltpu.SemaphoreType.DMA((4,)),
            pltpu.SemaphoreType.DMA((owners,)),
            pltpu.SemaphoreType.DMA((owners,)),
            pltpu.SemaphoreType.DMA((pieces,)),
            pltpu.SemaphoreType.DMA((5,)),
            pltpu.VMEM((3, depth, count), value.dtype),
            pltpu.VMEM((count, weights[3].shape[1]), value.dtype),
            pltpu.VMEM((depth, 3 * units), value.dtype),
        ]
        + gather_sems(1, owners),
        compiler_params=params(collective_id),
        cost_estimate=cost(40),
        name="open_team",
    )(value, *weights, note)
    return out.reshape(-1, value.shape[1]), qkv, out_w, packed, notes


def scatter_kernel(amount, swapped, owners, cores, *refs):
    parts, refs = refs[:amount], refs[amount:]
    if swapped:
        summed, refs = refs[0], refs[1:]
    outs, refs = refs[:amount], refs[amount:]
    if swapped:
        rows, refs = refs[0], refs[1:]
    pairs, halves, from_left, from_right = [
        refs[k * amount : (k + 1) * amount] for k in range(4)
    ]
    total, sent_pair, came_pair, sent, came_left, came_right = refs[4 * amount : 4 * amount + 6]
    swap = refs[4 * amount + 6 :]
    here, core, pair, right, left = ring(owners, cores)
    if swapped:
        greet(around("ctx", owners) + around("tensor", cores))
    else:
        greet(line_partners(owners, cores))
    order = [k // 2 if k % 2 else owners - 1 - k // 2 for k in range(owners)]
    for i in range(amount):
        for block in order:
            send(
                parts[i].at[block, pair],
                pairs[i].at[block],
                sent_pair.at[i, block],
                came_pair.at[i, block],
                {"tensor": pair},
            )

    if swapped:
        swap_first(summed, rows, *swap, owners)

    def add_up(i, block, more, arrived, came):
        landed(pairs[i].at[block], came_pair.at[i, block])
        total[...] = parts[i][block, core].astype(jnp.float32) + pairs[i][block].astype(
            jnp.float32
        )

        @pl.when(more)
        def _():
            landed(arrived[i].at[block], came.at[i, block])
            total[...] += arrived[i][block].astype(jnp.float32)

    def pass_on(i, block, more, arrived, came, device):
        add_up(i, block, more, arrived, came)
        halves[i][block] = total[...].astype(halves[i].dtype)
        send(
            halves[i].at[block],
            arrived[i].at[block],
            sent.at[i, block],
            came.at[i, block],
            {"ctx": device},
        )

    for step in range(2 * owners - 2):
        for i in range(amount):
            rightward = owners - 1 - (step - here)
            leftward = step - (owners - 1 - here)

            @pl.when((rightward > here) & (step >= here))
            def _():
                pass_on(i, rightward, here > 0, from_left, came_left, right)

            @pl.when((leftward >= 0) & (leftward < here))
            def _():
                pass_on(i, leftward, here < owners - 1, from_right, came_right, left)

    for i in range(amount):
        add_up(i, here, here > 0, from_left, came_left)

        @pl.when(here < owners - 1)
        def _():
            landed(from_right[i].at[here], came_right.at[i, here])
            total[...] += from_right[i][here].astype(jnp.float32)

        outs[i][...] = total[...]
    if swapped:
        swap_rest(summed, rows, *swap, owners, (), 0)
    for i in range(amount):
        for block in range(owners):
            landed(pairs[i].at[block], sent_pair.at[i, block])

            @pl.when(block != here)
            def _():
                landed(halves[i].at[block], sent.at[i, block])


def team_sum(collective_id, *values):
    return team_sum_and_rows(collective_id, None, *values)[0]


def team_sum_and_rows(collective_id, summed, *values):
    owners, cores = lax.axis_size("ctx"), lax.axis_size("tensor")
    amount = len(values)
    width = values[0].shape[1]
    mine = values[0].shape[0] // (owners * cores)
    blocks = [pltpu.VMEM((owners, mine, width), v.dtype) for v in values]
    more = [] if summed is None else [summed]
    out = pl.pallas_call(
        functools.partial(scatter_kernel, amount, bool(more), owners, cores),
        out_shape=[jax.ShapeDtypeStruct((mine, width), jnp.float32)] * amount
        + [jax.ShapeDtypeStruct(held_shape(m, owners), m.dtype) for m in more],
        in_specs=[INSIDE] * amount + [FAR] * len(more),
        out_specs=[INSIDE] * amount + [FAR] * len(more),
        scratch_shapes=blocks * 4
        + [pltpu.VMEM((mine, width), jnp.float32)]
        + [pltpu.SemaphoreType.DMA((amount, owners)) for _ in range(5)]
        + [sem for m in more for sem in swap_sems(owners)],
        compiler_params=params(collective_id),
        cost_estimate=cost(20 * amount),
        name="team_sum",
    )(*[v.reshape(owners, cores, mine, width) for v in values], *more)
    return out[:amount], out[amount:]


def swap_first(summed, held, local, sent, came, owners):
    here = lax.axis_index("ctx")
    count = summed.shape[0] // owners

    def rows(owner):
        return summed.at[pl.ds(pl.multiple_of(owner * count, count), count), :]

    for step in range(1, owners):
        other = lax.rem(here + step, owners)
        send(rows(other), held.at[here], sent.at[other], came.at[here], {"ctx": other})
    pltpu.make_async_copy(rows(here), held.at[here], local).start()


def put_rows(held, source, outs, block, half, halves):
    amount = len(outs)
    units = held.shape[2] // amount
    for j in range(units // block):
        start = pl.multiple_of((source * halves + half) * units + j * block, block)
        for i, out in enumerate(outs):
            first = (j * amount + i) * block
            piece = held[source, :, first : first + block].astype(jnp.float32)
            if i < amount - 1:
                out[:, pl.ds(start, block)] = piece
            else:
                out[pl.ds(start, block), :] = piece.T


def swap_rest(summed, held, local, sent, came, owners, outs, block, half=0, halves=1):
    here = lax.axis_index("ctx")
    count = summed.shape[0] // owners
    own = summed.at[pl.ds(pl.multiple_of(here * count, count), count), :]
    for step in range(owners):
        source = lax.rem(here + owners - step, owners)
        if step == 0:
            pltpu.make_async_copy(own, held.at[here], local).wait()
        else:
            landed(held.at[source], came.at[source])
        if outs:
            put_rows(held, source, outs, block, half, halves)
    for step in range(1, owners):
        other = lax.rem(here + step, owners)
        landed(held.at[other], sent.at[other])


def held_shape(summed, owners):
    return (owners, summed.shape[0] // owners, summed.shape[1])


def swap_sems(owners):
    return [
        pltpu.SemaphoreType.DMA,
        pltpu.SemaphoreType.DMA((owners,)),
        pltpu.SemaphoreType.DMA((owners,)),
    ]


def swap_outs(summed, owners, amount, halves=1):
    count, units = summed.shape[0] // owners, summed.shape[1] // amount * halves
    shapes = [(count, owners * units)] * (amount - 1) + [(owners * units, count)]
    return [jax.ShapeDtypeStruct(shape, jnp.float32) for shape in shapes]


def around(axis, size):
    index = lax.axis_index(axis)
    return [{axis: lax.rem(index + step, size)} for step in range(1, size)]


def swap_kernel_alone(owners, block, amount, *refs):
    summed, outs, scratch = refs[0], refs[1 : 1 + amount], refs[1 + amount :]
    greet(around("ctx", owners))
    swap_first(summed, *scratch, owners)
    swap_rest(summed, *scratch, owners, outs, block)


def team_rows(collective_id, summed, amount, block):
    owners = lax.axis_size("ctx")
    return pl.pallas_call(
        functools.partial(swap_kernel_alone, owners, block, amount),
        out_shape=swap_outs(summed, owners, amount),
        in_specs=[ANY],
        out_specs=[INSIDE] * amount,
        scratch_shapes=[pltpu.VMEM(held_shape(summed, owners), summed.dtype)]
        + swap_sems(owners),
        compiler_params=params(collective_id),
        cost_estimate=cost(20),
        name="team_rows",
    )(summed)


def close_kernel(amount, shards_in, owners, cores, *refs):
    values, mixed, grads, early = refs[:amount], refs[amount], refs[amount + 1], refs[amount + 2]
    refs = refs[amount + 3 :]
    outs, summed, grad_outs = refs[:amount], refs[amount], refs[amount + 1 : amount + 4]
    refs = refs[amount + 4 :]
    pairs, half, quarters, blocks, local, sent, came = refs[:7]
    sent_c, came_c, sent_s, came_s, sent_b, came_b = refs[7:13]
    swap = refs[13:]
    here, core, pair, right, left = ring(owners, cores)
    index = lax.axis_index("shard")
    near = [lax.rem(here + step, owners) for step in range(1, owners)]
    others = [lax.rem(index + step, shards_in) for step in range(1, shards_in)]
    greet([{"tensor": pair}] + around("ctx", owners) + around("shard", shards_in))
    wide = mixed.shape[1] // cores
    thin = wide // owners
    send(
        mixed.at[:, pl.ds(pl.multiple_of(pair * wide, wide), wide)],
        pairs,
        sent.at[amount],
        came.at[amount],
        {"tensor": pair},
    )
    for i in range(amount):
        target = outs[i].at[:, core]
        send(values[i], target, sent.at[i], came.at[i], {"tensor": pair})
        pltpu.make_async_copy(values[i], target, local.at[i]).start()
    landed(pairs, came.at[amount])
    half[...] = mixed[:, pl.ds(pl.multiple_of(core * wide, wide), wide)] + pairs[...]
    for other in near:
        send(
            half.at[:, pl.ds(pl.multiple_of(other * thin, thin), thin)],
            quarters.at[here],
            sent_c.at[other],
            came_c.at[here],
            {"ctx": other},
        )
    total = half[:, pl.ds(pl.multiple_of(here * thin, thin), thin)]
    for other in near:
        landed(quarters.at[other], came_c.at[other])
        total += quarters[other]
    blocks[index] = total
    for other in others:
        send(
            blocks.at[index], blocks.at[index], sent_s.at[other], came_s.at[index], {"shard": other}
        )
    swap_first(grads, *swap, owners)
    for other in others:
        landed(blocks.at[other], came_s.at[other])
    total = blocks[0]
    for block in range(1, shards_in):
        total += blocks[block]

    def place(owner, half_of):
        return summed.at[half_of * owners + owner]

    summed[core * owners + here] = total
    for other in near:
        send(place(here, core), place(here, core), sent_b.at[other], came_b.at[here, core], {"ctx": other})
    send(place(here, core), place(here, core), sent_b.at[here], came_b.at[here, core], {"tensor": pair})
    for other in near:
        landed(place(other, core), came_b.at[other, core])
        send(
            place(other, core),
            place(other, core),
            sent_b.at[owners + other],
            came_b.at[other, core],
            {"tensor": pair},
        )
    for owner in range(owners):
        landed(place(owner, pair), came_b.at[owner, pair])
        landed(place(owner, core), sent_b.at[owner])
    for other in near:
        landed(place(other, core), sent_b.at[owners + other])
        landed(quarters.at[other], sent_c.at[other])
    for other in others:
        landed(blocks.at[other], sent_s.at[other])
    landed(pairs, sent.at[amount])
    block = grads.shape[1] // (3 * BLOCKS // 2)
    for source in range(owners):
        put_rows(early, source, grad_outs, block, 0, 2)
    swap_rest(grads, *swap, owners, grad_outs, block, 1, 2)
    for i in range(amount):
        target = outs[i].at[:, core]
        landed(outs[i].at[:, pair], came.at[i])
        landed(target, sent.at[i])
        pltpu.make_async_copy(values[i], target, local.at[i]).wait()


def close_team(collective_id, early, grads, mixed, *values):
    shards_in, owners, cores = [lax.axis_size(a) for a in ("shard", "ctx", "tensor")]
    amount = len(values)
    height, width = mixed.shape
    thin = width // (cores * owners)
    out = pl.pallas_call(
        functools.partial(close_kernel, amount, shards_in, owners, cores),
        out_shape=[
            jax.ShapeDtypeStruct((v.shape[0], cores, *v.shape[1:]), v.dtype) for v in values
        ]
        + [jax.ShapeDtypeStruct((cores * owners, height, thin), jnp.float32)]
        + swap_outs(grads, owners, 3, 2),
        in_specs=[ANY] * amount + [INSIDE, FAR, INSIDE],
        out_specs=[ANY] * amount + [INSIDE] * 4,
        scratch_shapes=[
            pltpu.VMEM((height, width // cores), jnp.float32),
            pltpu.VMEM((height, width // cores), jnp.float32),
            pltpu.VMEM((owners, height, thin), jnp.float32),
            pltpu.VMEM((shards_in, height, thin), jnp.float32),
            pltpu.SemaphoreType.DMA((amount,)),
            pltpu.SemaphoreType.DMA((amount + 1,)),
            pltpu.SemaphoreType.DMA((amount + 1,)),
            pltpu.SemaphoreType.DMA((owners,)),
            pltpu.SemaphoreType.DMA((owners,)),
            pltpu.SemaphoreType.DMA((shards_in,)),
            pltpu.SemaphoreType.DMA((shards_in,)),
            pltpu.SemaphoreType.DMA((2 * owners,)),
            pltpu.SemaphoreType.DMA((owners, cores)),
        ]
        + [pltpu.VMEM(held_shape(grads, owners), grads.dtype)]
        + swap_sems(owners),
        compiler_params=params(collective_id),
        cost_estimate=cost(60),
        name="close_team",
    )(*values, mixed, grads, early)
    mixed = out[amount].transpose(1, 0, 2).reshape(height, width)
    return mixed, out[:amount], out[amount + 1 :]


def ffn_kernel(
    u_ref,
    dy_ref,
    gate_ref,
    up_ref,
    down_ref,
    y_ref,
    du_ref,
    early_ref,
    late_ref,
    y_sum,
    du_sum,
    u_t,
    dy_t,
):
    step = pl.program_id(0)
    early = step < pl.num_programs(0) // 2
    total, width = u_ref.shape
    block = gate_ref.shape[1]
    tile = down_ref.shape[2]

    @pl.when(step == 0)
    def _():
        y_sum[...] = jnp.zeros_like(y_sum)
        du_sum[...] = jnp.zeros_like(du_sum)
        for start in range(0, width, tile):
            u_t[start : start + tile, :] = u_ref[:, start : start + tile].T
            dy_t[start : start + tile, :] = dy_ref[:, start : start + tile].T

    gate = dot(u_ref[...], gate_ref[...])
    upward = dot(u_ref[...], up_ref[...])
    shards_in = down_ref.shape[0]
    grad_hidden = 0.0
    for k in range(shards_in):
        grad_hidden = grad_hidden + contract_cols(
            dy_ref[:, k * tile : (k + 1) * tile], down_ref[k]
        )
    sigma = jax.nn.sigmoid(gate)
    swish = gate * sigma
    hidden = (swish * upward).astype(jnp.bfloat16)
    grad_gate = (grad_hidden * upward * (sigma + swish * (1.0 - sigma))).astype(jnp.bfloat16)
    grad_up = (grad_hidden * swish).astype(jnp.bfloat16)
    for k in range(shards_in):
        span = slice(k * tile, (k + 1) * tile)
        y_sum[:, span] += dot(hidden, down_ref[k])
        du_sum[:, span] += contract_cols(grad_gate, gate_ref[span, :]) + contract_cols(
            grad_up, up_ref[span, :]
        )

    def weights_back(grad_ref):
        for start in range(0, width, tile):
            span = slice(start, start + tile)
            grad_ref[span, :block] = dot(u_t[span, :], grad_gate).astype(jnp.bfloat16)
            grad_ref[span, block : 2 * block] = dot(u_t[span, :], grad_up).astype(jnp.bfloat16)
            grad_ref[span, 2 * block :] = dot(dy_t[span, :], hidden).astype(jnp.bfloat16)

    @pl.when(early)
    def _():
        weights_back(early_ref)

    @pl.when(jnp.logical_not(early))
    def _():
        weights_back(late_ref)

    @pl.when(step == pl.num_programs(0) - 1)
    def _():
        y_ref[...] = y_sum[...].astype(jnp.bfloat16)
        du_ref[...] = du_sum[...].astype(jnp.bfloat16)


def ffn(u, dy, weights):
    total, width = u.shape
    shards_in = lax.axis_size("shard")
    depth = width // shards_in
    units = weights.shape[1] // 3
    blocks = BLOCKS
    block = units // blocks
    half = blocks // 2
    whole = pl.BlockSpec((total, width), lambda j: (0, 0), pipeline_mode=pl.Buffered(1))
    low = functools.partial(jax.ShapeDtypeStruct, dtype=jnp.bfloat16)
    return pl.pallas_call(
        ffn_kernel,
        grid=(blocks,),
        in_specs=[
            whole,
            whole,
            pl.BlockSpec((width, block), lambda j: (0, j)),
            pl.BlockSpec((width, block), lambda j: (0, blocks + j)),
            pl.BlockSpec(
                (shards_in, block, depth),
                lambda j: (0, j % (depth // block), 2 * units // depth + j // (depth // block)),
            ),
        ],
        out_specs=[
            whole,
            whole,
            pl.BlockSpec((width, 3 * block), lambda j: (0, jnp.minimum(j, half - 1))),
            pl.BlockSpec((width, 3 * block), lambda j: (0, jnp.maximum(j - half, 0))),
        ],
        out_shape=[low((total, width))] * 2 + [low((width, 3 * units // 2))] * 2,
        scratch_shapes=[
            pltpu.VMEM((total, width), jnp.float32),
            pltpu.VMEM((total, width), jnp.float32),
            pltpu.VMEM((width, total), jnp.bfloat16),
            pltpu.VMEM((width, total), jnp.bfloat16),
        ],
        compiler_params=pltpu.CompilerParams(
            dimension_semantics=("arbitrary",), vmem_limit_bytes=60 << 20
        ),
        cost_estimate=cost(30),
        name="ffn",
    )(u, dy, weights, weights, weights.reshape(shards_in, depth, 3 * units))


def pack_kernel(sent, value, out):
    out[0] = value[...]


def pack_runs(value, sent, part):
    total, rows_in, width = value.shape
    return pl.pallas_call(
        pack_kernel,
        grid_spec=pltpu.PrefetchScalarGridSpec(
            num_scalar_prefetch=1,
            grid=(sent.shape[0],),
            in_specs=[
                pl.BlockSpec((total, part, width), lambda c, first: (0, first[c], 0)),
            ],
            out_specs=pl.BlockSpec((1, total, part, width), lambda c, first: (c, 0, 0, 0)),
        ),
        out_shape=jax.ShapeDtypeStruct((sent.shape[0], total, part, width), value.dtype),
        compiler_params=pltpu.CompilerParams(dimension_semantics=("arbitrary",)),
        cost_estimate=cost(2),
        name="pack_runs",
    )(sent, value)


def head_probs(query, key, placing, placed):
    scores = contract_cols(query, key) * HD ** (-0.5)
    allowed = (placed >= placing[:, 0:1]) & (placed <= placing[:, 1:2])
    scores = jnp.where(allowed, scores, FLOOR_SCORE)
    probs = jnp.exp(scores - jnp.max(scores, -1, keepdims=True))
    return probs / jnp.sum(probs, -1, keepdims=True)


def turn(value, turns, back):
    swung = pltpu.roll(value, HD // 2, 1) * turns[1]
    return value * turns[0] - swung if back else value * turns[0] + swung


def attend_kernel(
    u_ref, qkv_ref, out_ref, turns, placing, placed, y_ref, q_ref, k_ref, v_ref, o_ref
):
    count = q_ref.shape[1]
    u = u_ref[...]
    for first in range(0, count, HD):
        head = slice(first, first + HD)

        def lin(which):
            start = which * count + first
            return dot(u, qkv_ref[:, start : start + HD])

        query = turn(lin(0), turns, False).astype(jnp.bfloat16)
        key = turn(lin(1), turns, False).astype(jnp.bfloat16)
        value = lin(2).astype(jnp.bfloat16)
        q_ref[:, head] = query
        k_ref[:, head] = key
        v_ref[:, head] = value
        probs = head_probs(query, key, placing[...], placed[...])
        o_ref[:, head] = dot(probs.astype(jnp.bfloat16), value).astype(jnp.bfloat16)
    width = y_ref.shape[1]
    for start in range(0, width, 512):
        y_ref[:, start : start + 512] = dot(o_ref[...], out_ref[:, start : start + 512])


def attend(u, qkv, out_w, turns, placing, placed):
    total, count = u.shape[0], out_w.shape[0]
    low = jax.ShapeDtypeStruct((total, count), jnp.bfloat16)
    return pl.pallas_call(
        attend_kernel,
        out_shape=[jax.ShapeDtypeStruct((total, out_w.shape[1]), jnp.float32)] + [low] * 4,
        in_specs=[INSIDE] * 6,
        out_specs=[INSIDE] * 5,
        compiler_params=pltpu.CompilerParams(vmem_limit_bytes=56 << 20),
        cost_estimate=cost(12),
        name="attend",
    )(u, qkv, out_w, turns, placing, placed)


def attend_back_kernel(
    dy_ref,
    u_ref,
    qkv_ref,
    out_ref,
    q_ref,
    k_ref,
    v_ref,
    o_ref,
    turns,
    placing,
    placed,
    du_ref,
    grad_ref,
    lin,
):
    count = q_ref.shape[1]
    width = du_ref.shape[1]
    scale = HD ** (-0.5)
    low = jnp.bfloat16
    for first in range(0, count, HD):
        head = slice(first, first + HD)
        query, key, value = q_ref[:, head], k_ref[:, head], v_ref[:, head]
        grad_out = contract_cols(dy_ref[...], out_ref[head, :]).astype(low)
        probs = head_probs(query, key, placing[...], placed[...])
        grad_probs = contract_cols(grad_out, value)
        delta = jnp.sum(probs * grad_probs, -1, keepdims=True)
        grad_scores = (probs * (grad_probs - delta)).astype(low)
        grad_query = turn(dot(grad_scores, key) * scale, turns, True)
        grad_key = turn(contract_rows(grad_scores, query) * scale, turns, True)
        grad_value = contract_rows(probs.astype(low), grad_out)
        for which, grad in enumerate((grad_query, grad_key, grad_value)):
            start = which * count + first
            lin[:, start : start + HD] = grad.astype(low)
    tile = min(512, width)
    edge = lin.shape[1]
    for start in range(0, width, tile):
        span = slice(start, start + tile)
        du_ref[:, span] = contract_cols(lin[...], qkv_ref[span, :]).astype(low)
        grad_ref[span, :edge] = dot(u_ref[:, span].T, lin[...]).astype(low)
        grad_ref[span, edge:] = dot(dy_ref[:, span].T, o_ref[...]).astype(low)


def attend_back(dy, u, qkv, out_w, q, k, v, o, turns, placing, placed):
    total, width = u.shape
    count = q.shape[1]
    return pl.pallas_call(
        attend_back_kernel,
        out_shape=[
            jax.ShapeDtypeStruct((total, width), jnp.bfloat16),
            jax.ShapeDtypeStruct((width, 4 * count), jnp.bfloat16),
        ],
        in_specs=[INSIDE] * 11,
        out_specs=[INSIDE] * 2,
        scratch_shapes=[pltpu.VMEM((total, 3 * count), jnp.bfloat16)],
        compiler_params=pltpu.CompilerParams(vmem_limit_bytes=56 << 20),
        cost_estimate=cost(20),
        name="attend_back",
    )(dy, u, qkv, out_w, q, k, v, o, turns, placing, placed)


EXACT = functools.partial(
    lax.dot_general, precision=PRECISE, preferred_element_type=jnp.float32
)


def columns_of(pieces):
    rows_in = pieces[0].shape[0]
    lane = lax.broadcasted_iota(jnp.int32, (rows_in, 8), 1)
    out = jnp.zeros((rows_in, 8), jnp.float32)
    for k, piece in enumerate(pieces):
        out = jnp.where(lane == k, piece, out)
    return out


def tables_of(current, weight, static, table_ref, active_ref):
    branch_in = 0.0
    tables = []
    for i, stream in enumerate(current):
        normed, scaled = norm_rows(stream)
        active = jnp.tanh(EXACT(normed, weight, (((1,), (1,)), ((), ()))))
        table = active + static[i : i + 1, :]
        table_ref[i] = table
        active_ref[i] = active
        tables.append(table)
        branch_in = branch_in + table[:, 0:1] * stream
    return tables, branch_in


def norm_plain(value):
    centred = value - jnp.mean(value, -1, keepdims=True)
    scaled = lax.rsqrt(jnp.mean(centred * centred, -1, keepdims=True) + EPSILON)
    return (centred * scaled, scaled)


def mix_first(current, weight, static):
    normed, _ = norm_plain(current)
    active = jnp.tanh(jnp.einsum("tsd,dk->tsk", normed, weight, precision=PRECISE))
    table = active + static
    total = current.shape[1]
    branch_in = sum(table[:, i, 0][:, None] * current[:, i] for i in range(total))
    normed, scaled = norm_plain(branch_in)

    def by_stream(value):
        return jnp.pad(value.transpose(1, 0, 2), ((0, 0), (0, 0), (0, 8 - value.shape[2])))

    scaled = jnp.pad(scaled, ((0, 0), (0, 7)))
    return normed.astype(jnp.bfloat16), normed, scaled, by_stream(table), by_stream(active)


def mix_second_kernel(
    source,
    streams,
    branch_out,
    table_one,
    arrived,
    weight,
    static,
    middle_ref,
    low_ref,
    grad_low_ref,
    normed_ref,
    scaled_ref,
    table_ref,
    active_ref,
    top_ref,
):
    total = streams.shape[0]
    y = branch_out[...]
    first = [table_one[i] for i in range(total)]
    current = [streams[i].astype(jnp.float32) for i in range(total)]
    middle = []
    for j in range(total):
        mixed = first[j][:, total + 1 : total + 2] * y
        for i in range(total):
            mixed = mixed + first[i][:, 1 + j : 2 + j] * current[i]
        middle.append(mixed)
        middle_ref[j] = mixed
    tables, branch_in = tables_of(middle, weight[...], static[...], table_ref, active_ref)
    normed, scaled = norm_rows(branch_in)
    normed_ref[...] = normed
    low_ref[...] = normed.astype(jnp.bfloat16)
    scaled_ref[...] = columns_of([scaled])
    grad = 0.0
    for j in range(total):
        top = arrived[0, j]
        top_ref[j] = top
        grad = grad + tables[j][:, total + 1 : total + 2] * top.astype(jnp.float32)
    grad_low_ref[...] = grad.astype(jnp.bfloat16)


def connection_back(
    current, grad_top, branch_out, grad_in, normed_in, scaled_in, tables, actives, weight, sums
):
    total = len(current)
    weight_sum, static_sum = sums
    dx = scaled_in * (grad_in - mean_of(grad_in) - normed_in * mean_of(grad_in * normed_in))
    result = []
    for i, stream in enumerate(current):
        pieces = [jnp.sum(dx * stream, -1, keepdims=True)]
        pieces += [jnp.sum(stream * top, -1, keepdims=True) for top in grad_top]
        pieces.append(jnp.sum(grad_top[i] * branch_out, -1, keepdims=True))
        grad_table = columns_of(pieces)
        static_sum[i : i + 1, :] += jnp.sum(grad_table, 0, keepdims=True)
        grad_inner = grad_table * (1.0 - actives[i] * actives[i])
        normed, scaled = norm_rows(stream)
        weight_sum[...] += EXACT(grad_inner, normed, (((0,), (0,)), ((), ())))
        grad_normed = EXACT(grad_inner, weight, (((1,), (0,)), ((), ())))
        grad = tables[i][:, 0:1] * dx + norm_back(normed, scaled, grad_normed)
        for j in range(total):
            grad = grad + tables[i][:, 1 + j : 2 + j] * grad_top[j]
        result.append(grad)
    return result


def start_sums(sums):
    @pl.when(pl.program_id(0) == 0)
    def _():
        for ref in sums:
            ref[...] = jnp.zeros_like(ref)


def back_second_kernel(
    middle,
    top,
    branch_out,
    grad_in,
    normed_in,
    scaled_in,
    table,
    active,
    table_one,
    weight,
    final_ref,
    grad_ref,
    grad_low_ref,
    *sums,
):
    start_sums(sums)
    total = middle.shape[0]
    current = [middle[i] for i in range(total)]
    grad_top = [top[i].astype(jnp.float32) for i in range(total)]
    tables = [table[i] for i in range(total)]
    y = branch_out[...]
    for j in range(total):
        mixed = tables[j][:, total + 1 : total + 2] * y
        for i in range(total):
            mixed = mixed + tables[i][:, 1 + j : 2 + j] * current[i]
        final_ref[j] = mixed.astype(jnp.bfloat16)
    grads = connection_back(
        current,
        grad_top,
        y,
        grad_in[...],
        normed_in[...],
        scaled_in[:, 0:1],
        tables,
        [active[i] for i in range(total)],
        weight[...],
        sums,
    )
    low = 0.0
    for j in range(total):
        grad_ref[j] = grads[j]
        low = low + table_one[j][:, total + 1 : total + 2] * grads[j]
    grad_low_ref[...] = low.astype(jnp.bfloat16)


def back_first_kernel(
    streams,
    top,
    branch_out,
    grad_in,
    normed_in,
    scaled_in,
    table,
    active,
    weight,
    grad_ref,
    *sums,
):
    start_sums(sums)
    total = streams.shape[0]
    grads = connection_back(
        [streams[i].astype(jnp.float32) for i in range(total)],
        [top[i] for i in range(total)],
        branch_out[...],
        grad_in[...],
        normed_in[...],
        scaled_in[:, 0:1],
        [table[i] for i in range(total)],
        [active[i] for i in range(total)],
        weight[...],
        sums,
    )
    for j in range(total):
        grad_ref[j] = grads[j].astype(jnp.bfloat16)


def by_token(tile, shape, kind=jnp.float32):
    block = (*shape[:-2], tile, shape[-1])
    lead = (0,) * (len(shape) - 2)
    spec = pl.BlockSpec(block, lambda step, *_: (*lead, step, 0))
    return spec, jax.ShapeDtypeStruct(shape, kind)


def fixed(shape, kind=jnp.float32):
    spec = pl.BlockSpec(shape, lambda step, *_: (0,) * len(shape))
    return spec, jax.ShapeDtypeStruct(shape, kind)


def token_call(kernel, name, tile, ins, outs, prefetch=(), special=None):
    specs, values = [], []
    for value, tiled in ins:
        if tiled == "run":
            specs.append(special)
        else:
            specs.append(by_token(tile, value.shape)[0] if tiled else fixed(value.shape)[0])
        values.append(value)
    tokens = outs[0][1].shape[-2]
    return pl.pallas_call(
        kernel,
        grid_spec=pltpu.PrefetchScalarGridSpec(
            num_scalar_prefetch=len(prefetch),
            grid=(tokens // tile,),
            in_specs=specs,
            out_specs=[o[0] for o in outs],
        ),
        out_shape=[o[1] for o in outs],
        compiler_params=pltpu.CompilerParams(
            dimension_semantics=("arbitrary",), vmem_limit_bytes=48 << 20
        ),
        cost_estimate=cost(5),
        name=name,
    )(*prefetch, *values)


def shards(
    streams,
    lengths,
    destination,
    w_query,
    w_key,
    w_value,
    w_output,
    w_gate,
    w_up,
    w_down,
    mix_weight,
    mix_static,
    cotangent,
):
    rows_here, stream_total, width = streams.shape
    owners = lax.axis_size("ctx")
    cores = lax.axis_size("tensor")
    here = lax.axis_index("ctx")
    core = lax.axis_index("tensor")
    run_rows = rows_here // owners
    part = run_rows // cores
    mine = rows_here // cores
    group_rows = rows_here * owners
    head_cols = w_query.shape[1] // owners
    heads = head_cols // HD
    units = w_gate.shape[1] // owners
    scale = HD ** (-0.5)

    def columns(weight, count):
        return lax.dynamic_slice_in_dim(weight, here * count, count, 1)

    def rows(weight, count):
        return lax.dynamic_slice_in_dim(weight, here * count, count, 0)

    order = jnp.arange(group_rows, dtype=jnp.int32)
    within = order % mine
    placed = (
        order // rows_here * rows_here
        + within // part * run_rows
        + order % rows_here // mine * part
        + within % part
    )
    spans = lengths[0]
    count = jnp.arange(spans.shape[0], dtype=jnp.int32)
    starts = jnp.sum(jnp.where(count[None, :] < count[:, None], spans[None, :], 0), 1)
    begin = jnp.max(jnp.where(starts[None, :] <= placed[:, None], starts[None, :], 0), axis=1)
    cosine, sine = angles(placed - begin, HD)
    turns = jnp.stack(
        [jnp.concatenate([cosine, cosine], -1), jnp.concatenate([-sine, sine], -1)]
    ).reshape(2, group_rows, HD)
    placing = jnp.stack([begin, placed], 1)
    placed = placed[None]

    local_dest = destination - lax.axis_index("shard") * group_rows
    heads_of_runs = local_dest.reshape(owners, run_rows)[:, 0]
    came_from = heads_of_runs // rows_here
    note = jnp.broadcast_to(jnp.pad(heads_of_runs, (0, 128 - owners)), (8, 128))

    turned_weight = jnp.pad(mix_weight.transpose(0, 2, 1), ((0, 0), (0, 2), (0, 0)))
    static = jnp.pad(mix_static, ((0, 0), (0, 0), (0, 2)))
    split = streams.reshape(owners, cores, part, stream_total, width)
    current = lax.dynamic_index_in_dim(split, core, 1, keepdims=False)
    current = current.reshape(mine, stream_total, width)
    attn_low, attn_normed, attn_scaled, table_one, active_one = mix_first(
        current.astype(jnp.float32), mix_weight[0], mix_static[0]
    )
    current = current.transpose(1, 0, 2)
    low = jnp.bfloat16
    tile = min(16, part)
    small = by_token(tile, (stream_total, mine, 8))
    attn_input, qkv, out_w, packed, notes = open_team(
        0, attn_low, (w_query, w_key, w_value, w_output, w_gate, w_up, w_down), note
    )
    ffn_weights = lax.all_gather(packed, "shard", axis=0, tiled=True)
    every = notes[:, 0, :owners]
    sent = jnp.sum(jnp.where(every // rows_here == here, every % rows_here, 0), 1) // part + core
    packed = pack_runs(cotangent.transpose(1, 0, 2), sent, part)
    arrived = lax.all_to_all(packed, "ctx", split_axis=0, concat_axis=0, tiled=True)
    attn_part, queries, keys, values, attended = attend(
        attn_input, qkv, out_w, turns, placing, placed
    )
    [attn_out] = team_sum(1, attn_part)

    (
        middle,
        ffn_low,
        grad_ffn_low,
        ffn_normed,
        ffn_scaled,
        table_two,
        active_two,
        grad_top,
    ) = token_call(
        mix_second_kernel,
        "mix_second",
        tile,
        [
            (current, True),
            (attn_out, True),
            (table_one, True),
            (arrived, "run"),
            (turned_weight[1], False),
            (static[1], False),
        ],
        [
            by_token(tile, (stream_total, mine, width)),
            by_token(tile, (mine, width), low),
            by_token(tile, (mine, width), low),
            by_token(tile, (mine, width)),
            by_token(tile, (mine, 8)),
            small,
            small,
            by_token(tile, (stream_total, mine, width), low),
        ],
        (came_from,),
        pl.BlockSpec(
            (1, stream_total, tile, width),
            lambda step, source: (source[step * tile // part], 0, step % (part // tile), 0),
        ),
    )
    ffn_input, grad_ffn_out = team_gather(2, ffn_low, grad_ffn_low)
    ffn_part, ffn_input_part, *ffn_grads = ffn(ffn_input, grad_ffn_out, ffn_weights)

    def shard_sum(partial):
        return lax.psum_scatter(partial, "shard", scatter_dimension=0, tiled=True)

    early_sum, late_sum = [shard_sum(grads) for grads in ffn_grads]
    ffn_out, grad_ffn_input = team_sum(3, ffn_part, ffn_input_part)
    sums = [fixed((8, width)), fixed((stream_total, 8))]
    final, grad_middle, grad_attn_low, weight_two, static_two = token_call(
        back_second_kernel,
        "back_second",
        tile,
        [
            (middle, True),
            (grad_top, True),
            (ffn_out, True),
            (grad_ffn_input, True),
            (ffn_normed, True),
            (ffn_scaled, True),
            (table_two, True),
            (active_two, True),
            (table_one, True),
            (turned_weight[1], False),
        ],
        [
            by_token(tile, (stream_total, mine, width), low),
            by_token(tile, (stream_total, mine, width)),
            by_token(tile, (mine, width), low),
            *sums,
        ],
    )
    [grad_attn_out] = team_gather(4, grad_attn_low)

    attn_input_part, attn_grads = attend_back(
        grad_attn_out, attn_input, qkv, out_w, queries, keys, values, attended, turns, placing, placed
    )
    attn_sum = shard_sum(attn_grads)
    [grad_attn_input], [early_rows] = team_sum_and_rows(5, early_sum, attn_input_part)
    grad_current, weight_one, static_one = token_call(
        back_first_kernel,
        "back_first",
        tile,
        [
            (current, True),
            (grad_middle, True),
            (attn_out, True),
            (grad_attn_input, True),
            (attn_normed, True),
            (attn_scaled, True),
            (table_one, True),
            (active_one, True),
            (turned_weight[0], False),
        ],
        [by_token(tile, (stream_total, mine, width), low), *sums],
    )
    statics = jnp.stack([static_one, static_two]).reshape(1, -1)
    mixed = jnp.concatenate(
        [
            jnp.stack([weight_one, weight_two], 1).reshape(16, width),
            jnp.pad(statics, ((0, 7), (0, width - statics.size))),
        ],
        0,
    )

    def runs(value):
        return value.transpose(1, 0, 2).reshape(owners, part, stream_total, width)

    mixed, (streams_out, grad_streams), (grad_gate, grad_up, grad_down) = close_team(
        7, early_rows, late_sum, mixed, runs(final), runs(grad_current)
    )
    mixed, attn_sum = lax.optimization_barrier((mixed, attn_sum))
    grad_query, grad_key, grad_value, grad_output = team_rows(8, attn_sum, 4, head_cols)
    columns_in = mix_weight.shape[2]
    grad_mix_weight = mixed[: 2 * columns_in].reshape(columns_in, 2, width).transpose(1, 2, 0)
    grad_mix_static = mixed[16, : statics.size].reshape(2, stream_total, 8)[:, :, :columns_in]

    return (
        streams_out.reshape(rows_here, stream_total, width),
        grad_streams.reshape(rows_here, stream_total, width),
        grad_query,
        grad_key,
        grad_value,
        grad_output,
        grad_gate,
        grad_up,
        grad_down,
        grad_mix_weight,
        grad_mix_static,
    )


def solution(mesh):
    return jax.shard_map(
        shards,
        mesh=mesh,
        in_specs=(
            P(("shard", "ctx"), None, None),
            P("shard", None),
            P(("shard", "ctx")),
            P("shard", "tensor"),
            P("shard", "tensor"),
            P("shard", "tensor"),
            P("tensor", "shard"),
            P("shard", "tensor"),
            P("shard", "tensor"),
            P("tensor", "shard"),
            P(),
            P(),
            P(("shard", "ctx"), None, None),
        ),
        out_specs=(
            P(("shard", "ctx"), None, None),
            P(("shard", "ctx"), None, None),
            P(("shard", "ctx"), "tensor"),
            P(("shard", "ctx"), "tensor"),
            P(("shard", "ctx"), "tensor"),
            P("tensor", ("shard", "ctx")),
            P(("shard", "ctx"), "tensor"),
            P(("shard", "ctx"), "tensor"),
            P("tensor", ("shard", "ctx")),
            P(),
            P(),
        ),
        check_vma=False,
    )
```

```python
import functools

import jax
import jax.numpy as jnp
import numpy as np
from jax import lax
from jax.experimental import pallas as pl
from jax.experimental.pallas import tpu as pltpu
from jax.sharding import PartitionSpec as P

HD = 128


PRECISE = lax.Precision.HIGHEST
EPSILON = 1e-05
FLOOR_SCORE = -1e30
BLOCKS = 4


def mean_of(value):
    width = value.shape[-1]
    while value.shape[-1] > 128 and value.shape[-1] % 256 == 0:
        half = value.shape[-1] // 2
        value = value[..., :half] + value[..., half:]
    return jnp.sum(value, -1, keepdims=True) * (1.0 / width)


def norm_rows(value):
    centred = value - mean_of(value)
    scaled = lax.rsqrt(mean_of(centred * centred) + EPSILON)
    return (centred * scaled, scaled)


def norm_back(normed, scaled, grad):
    return scaled * (grad - mean_of(grad) - normed * mean_of(grad * normed))


def angles(positions, head_size):
    indices = np.arange(head_size // 2, dtype=np.float64)
    frequency = (10000.0 ** (-(2.0 * indices / head_size))).astype(np.float32)
    turned = positions.astype(jnp.float32)[:, None] * frequency[None, :]
    return (jnp.cos(turned)[:, None, :], jnp.sin(turned)[:, None, :])


def dot(left, right):
    return jnp.dot(left, right, preferred_element_type=jnp.float32)


def contract_rows(left, right):
    return lax.dot_general(
        left, right, (((0,), (0,)), ((), ())), preferred_element_type=jnp.float32
    )


def contract_cols(left, right):
    return lax.dot_general(
        left, right, (((1,), (1,)), ((), ())), preferred_element_type=jnp.float32
    )


def greet(partners):
    barrier = pltpu.get_barrier_semaphore()
    for partner in partners:
        pl.semaphore_signal(
            barrier, inc=1, device_id=partner, device_id_type=pl.DeviceIdType.MESH
        )
    pl.semaphore_wait(barrier, len(partners))


def send(source, target, sent, received, device):
    pltpu.make_async_remote_copy(
        src_ref=source,
        dst_ref=target,
        send_sem=sent,
        recv_sem=received,
        device_id=device,
        device_id_type=pl.DeviceIdType.MESH,
    ).start()


def landed(block, semaphore):
    pltpu.make_async_copy(block, block, semaphore).wait()


def ring(owners, cores):
    here = lax.axis_index("ctx")
    core = lax.axis_index("tensor")
    right, left = lax.rem(here + 1, owners), lax.rem(here + owners - 1, owners)
    return here, core, cores - 1 - core, right, left


def gather_first(values, outs, sems, owners, cores):
    local, sent_right, sent_left, sent_pair, came, came_pair = sems
    here, core, pair, right, left = ring(owners, cores)
    for i, (value, out) in enumerate(zip(values, outs)):
        target = out.at[here, core]

        @pl.when(here < owners - 1)
        def _():
            send(value, target, sent_right.at[i, here], came.at[i, here], {"ctx": right})

        @pl.when(here > 0)
        def _():
            send(value, target, sent_left.at[i, here], came.at[i, here], {"ctx": left})

        send(value, target, sent_pair.at[i, here], came_pair.at[i, here], {"tensor": pair})
        pltpu.make_async_copy(value, target, local.at[i]).start()


def gather_rest(values, outs, sems, owners, cores):
    local, sent_right, sent_left, sent_pair, came, came_pair = sems
    here, core, pair, right, left = ring(owners, cores)

    def arrive(i, out, block, onward, sent, device):
        held = out.at[block, core]
        landed(held, came.at[i, block])

        @pl.when(onward)
        def _():
            send(held, held, sent.at[i, block], came.at[i, block], device)

        send(held, held, sent_pair.at[i, block], came_pair.at[i, block], {"tensor": pair})

    for step in range(1, owners):
        for i, out in enumerate(outs):

            @pl.when(here >= step)
            def _():
                arrive(i, out, here - step, here < owners - 1, sent_right, {"ctx": right})

            @pl.when(here + step < owners)
            def _():
                arrive(i, out, here + step, here > 0, sent_left, {"ctx": left})

    for i, (value, out) in enumerate(zip(values, outs)):
        pltpu.make_async_copy(value, out.at[here, core], local.at[i]).wait()
        for block in range(owners):
            landed(out.at[block, pair], came_pair.at[i, block])
            landed(out.at[block, core], sent_pair.at[i, block])

            @pl.when((here < owners - 1) & (block <= here))
            def _():
                landed(out.at[block, core], sent_right.at[i, block])

            @pl.when((here > 0) & (block >= here))
            def _():
                landed(out.at[block, core], sent_left.at[i, block])


def gather_sems(amount, owners):
    return [pltpu.SemaphoreType.DMA((amount,))] + [
        pltpu.SemaphoreType.DMA((amount, owners)) for _ in range(5)
    ]


def line_partners(owners, cores):
    here, core, pair, right, left = ring(owners, cores)
    return [{"ctx": right}, {"ctx": left}, {"tensor": pair}]


def gather_kernel(amount, owners, cores, *refs):
    values, outs, sems = refs[:amount], refs[amount : 2 * amount], refs[2 * amount :]
    greet(line_partners(owners, cores))
    gather_first(values, outs, sems, owners, cores)
    gather_rest(values, outs, sems, owners, cores)


ANY = pl.BlockSpec(memory_space=pl.ANY)
FAR = pl.BlockSpec(memory_space=pltpu.HBM)
INSIDE = pl.BlockSpec(memory_space=pltpu.VMEM)


def params(collective_id):
    return pltpu.CompilerParams(
        collective_id=collective_id, has_side_effects=True, vmem_limit_bytes=60 << 20
    )


def cost(micros):
    return pl.CostEstimate(flops=0, transcendentals=0, bytes_accessed=int(micros * 3.0e6))


def team_gather(collective_id, *values):
    owners, cores = lax.axis_size("ctx"), lax.axis_size("tensor")
    amount = len(values)
    outs = pl.pallas_call(
        functools.partial(gather_kernel, amount, owners, cores),
        out_shape=[jax.ShapeDtypeStruct((owners, cores, *v.shape), v.dtype) for v in values],
        in_specs=[INSIDE] * amount,
        out_specs=[ANY] * amount,
        scratch_shapes=gather_sems(amount, owners),
        compiler_params=params(collective_id),
        cost_estimate=cost(20 * amount),
        name="team_gather",
    )(*values)
    return [o.reshape(-1, v.shape[1]) for o, v in zip(outs, values)]


def plane(index, shards_in):
    across_x = index + 1 - 2 * lax.rem(index, 2)
    return across_x, lax.rem(index + 2, shards_in), lax.rem(across_x + 2, shards_in)


def open_kernel(shards_in, owners, cores, *refs):
    value, w_query, w_key, w_value, w_output, w_gate, w_up, w_down, note = refs[:9]
    out, qkv, out_w, packed, notes = refs[9:14]
    own_sem, sent_w, came_w, passed_w, sent_n, came_n, pack_sem, load_sem = refs[14:22]
    stage, stage_out, stage_pack = refs[22:25]
    sems = refs[25:]
    index = lax.axis_index("shard")
    here = lax.axis_index("ctx")
    depth = w_query.shape[0]
    count = w_query.shape[1] // owners
    columns = pl.ds(pl.multiple_of(here * count, count), count)
    stored = [w.at[:, columns] for w in (w_query, w_key, w_value)] + [w_output.at[columns, :]]
    sources = [stage.at[0], stage.at[1], stage.at[2], stage_out]
    for k, (slow, source) in enumerate(zip(stored, sources)):
        pltpu.make_async_copy(slow, source, load_sem.at[k]).start()

    def target(weight, block):
        if weight == 3:
            wide = w_output.shape[1]
            return out_w.at[:, pl.ds(pl.multiple_of(block * wide, wide), wide)]
        rows = pl.ds(pl.multiple_of(block * depth, depth), depth)
        return qkv.at[rows, pl.ds(weight * count, count)]

    others = [lax.rem(index + step, shards_in) for step in range(1, shards_in)]
    greet(around("shard", shards_in) + around("ctx", owners) + around("tensor", cores))
    units = w_gate.shape[1] // owners
    hidden = pl.ds(pl.multiple_of(here * units, units), units)
    wide_down = w_down.shape[1]
    pieces = [
        (w_gate.at[:, hidden], stage_pack.at[:, pl.ds(0, units)]),
        (w_up.at[:, hidden], stage_pack.at[:, pl.ds(units, units)]),
    ]
    for k in range(units // depth):
        start = pl.multiple_of(here * units + k * depth, depth)
        place = pl.ds(2 * units + k * wide_down, wide_down)
        pieces.append((w_down.at[pl.ds(start, depth), :], stage_pack.at[:, place]))
    for k, (source, place) in enumerate(pieces):
        pltpu.make_async_copy(source, place, pack_sem.at[k]).start()
    notes[here] = note[...]
    fellows = [lax.rem(here + step, owners) for step in range(1, owners)]
    for fellow in fellows:
        send(note, notes.at[here], sent_n.at[fellow], came_n.at[here], {"ctx": fellow})
    square = shards_in == 4
    near = plane(index, shards_in)[:2] if square else others
    for weight in range(4):
        pltpu.make_async_copy(stored[weight], sources[weight], load_sem.at[weight]).wait()
        for other in near:
            send(
                sources[weight],
                target(weight, index),
                sent_w.at[weight, other],
                came_w.at[weight, index],
                {"shard": other},
            )
    gather_first([value], [out], sems, owners, cores)
    for weight in range(4):
        pltpu.make_async_copy(
            sources[weight], target(weight, index), own_sem.at[weight]
        ).start()
    for k, (source, place) in enumerate(pieces):
        pltpu.make_async_copy(source, place, pack_sem.at[k]).wait()
    pltpu.make_async_copy(stage_pack, packed, load_sem.at[4]).start()
    if square:
        across_x, across_y, far = plane(index, shards_in)
        for weight, source, device in (
            (0, across_x, across_y),
            (2, across_y, across_x),
            (1, across_x, across_y),
            (3, across_y, across_x),
        ):
            held = target(weight, source)
            landed(held, came_w.at[weight, source])
            send(
                held, held, passed_w.at[weight], came_w.at[weight, source], {"shard": device}
            )
    gather_rest([value], [out], sems, owners, cores)
    for fellow in fellows:
        landed(notes.at[fellow], came_n.at[fellow])
        landed(note, sent_n.at[fellow])
    pltpu.make_async_copy(stage_pack, packed, load_sem.at[4]).wait()
    for weight in range(4):
        pltpu.make_async_copy(
            sources[weight], target(weight, index), own_sem.at[weight]
        ).wait()
        for other in near:
            landed(sources[weight], sent_w.at[weight, other])
    if square:
        for weight, source in ((0, across_y), (2, across_x), (1, across_y), (3, across_x)):
            landed(target(weight, source), came_w.at[weight, source])
        for weight in range(4):
            landed(target(weight, far), came_w.at[weight, far])
            landed(sources[weight], passed_w.at[weight])
    else:
        for weight in range(4):
            for other in others:
                landed(target(weight, other), came_w.at[weight, other])


def open_team(collective_id, value, weights, note):
    shards_in, owners, cores = [lax.axis_size(a) for a in ("shard", "ctx", "tensor")]
    depth = weights[0].shape[0]
    count = weights[0].shape[1] // owners
    units = weights[4].shape[1] // owners
    pieces = 2 + units // depth
    out, qkv, out_w, packed, notes = pl.pallas_call(
        functools.partial(open_kernel, shards_in, owners, cores),
        out_shape=[
            jax.ShapeDtypeStruct((owners, cores, *value.shape), value.dtype),
            jax.ShapeDtypeStruct((shards_in * depth, 3 * count), value.dtype),
            jax.ShapeDtypeStruct((count, shards_in * weights[3].shape[1]), value.dtype),
            jax.ShapeDtypeStruct((depth, 3 * units), value.dtype),
            jax.ShapeDtypeStruct((owners, *note.shape), note.dtype),
        ],
        in_specs=[INSIDE] + [FAR] * 7 + [INSIDE],
        out_specs=[ANY] * 3 + [FAR] + [INSIDE],
        scratch_shapes=[
            pltpu.SemaphoreType.DMA((4,)),
            pltpu.SemaphoreType.DMA((4, shards_in)),
            pltpu.SemaphoreType.DMA((4, shards_in)),
            pltpu.SemaphoreType.DMA((4,)),
            pltpu.SemaphoreType.DMA((owners,)),
            pltpu.SemaphoreType.DMA((owners,)),
            pltpu.SemaphoreType.DMA((pieces,)),
            pltpu.SemaphoreType.DMA((5,)),
            pltpu.VMEM((3, depth, count), value.dtype),
            pltpu.VMEM((count, weights[3].shape[1]), value.dtype),
            pltpu.VMEM((depth, 3 * units), value.dtype),
        ]
        + gather_sems(1, owners),
        compiler_params=params(collective_id),
        cost_estimate=cost(40),
        name="open_team",
    )(value, *weights, note)
    return out.reshape(-1, value.shape[1]), qkv, out_w, packed, notes


def scatter_kernel(amount, swapped, owners, cores, *refs):
    parts, refs = refs[:amount], refs[amount:]
    if swapped:
        summed, refs = refs[0], refs[1:]
    outs, refs = refs[:amount], refs[amount:]
    if swapped:
        rows, refs = refs[0], refs[1:]
    pairs, halves, from_left, from_right, own = [
        refs[k * amount : (k + 1) * amount] for k in range(5)
    ]
    refs = refs[5 * amount :]
    total, sent_pair, came_pair, sent, came_left, came_right, load = refs[:7]
    swap = refs[7:]
    here, core, pair, right, left = ring(owners, cores)
    if swapped:
        greet(around("ctx", owners) + around("tensor", cores))
    else:
        greet(line_partners(owners, cores))
    order = [k // 2 if k % 2 else owners - 1 - k // 2 for k in range(owners)]
    for i in range(amount):
        for block in order:
            pltpu.make_async_copy(
                parts[i].at[block, core], own[i].at[block], load.at[i, block]
            ).start()
            send(
                parts[i].at[block, pair],
                pairs[i].at[block],
                sent_pair.at[i, block],
                came_pair.at[i, block],
                {"tensor": pair},
            )

    if swapped:
        swap_first(summed, rows, *swap, owners)

    def add_up(i, block, more, arrived, came):
        landed(pairs[i].at[block], came_pair.at[i, block])
        landed(own[i].at[block], load.at[i, block])
        total[...] = own[i][block].astype(jnp.float32) + pairs[i][block].astype(jnp.float32)

        @pl.when(more)
        def _():
            landed(arrived[i].at[block], came.at[i, block])
            total[...] += arrived[i][block].astype(jnp.float32)

    def pass_on(i, block, more, arrived, came, device):
        add_up(i, block, more, arrived, came)
        halves[i][block] = total[...].astype(halves[i].dtype)
        send(
            halves[i].at[block],
            arrived[i].at[block],
            sent.at[i, block],
            came.at[i, block],
            {"ctx": device},
        )

    for step in range(2 * owners - 2):
        for i in range(amount):
            rightward = owners - 1 - (step - here)
            leftward = step - (owners - 1 - here)

            @pl.when((rightward > here) & (step >= here))
            def _():
                pass_on(i, rightward, here > 0, from_left, came_left, right)

            @pl.when((leftward >= 0) & (leftward < here))
            def _():
                pass_on(i, leftward, here < owners - 1, from_right, came_right, left)

    for i in range(amount):
        add_up(i, here, here > 0, from_left, came_left)

        @pl.when(here < owners - 1)
        def _():
            landed(from_right[i].at[here], came_right.at[i, here])
            total[...] += from_right[i][here].astype(jnp.float32)

        outs[i][...] = total[...]
    if swapped:
        swap_rest(summed, rows, *swap, owners)
    for i in range(amount):
        for block in range(owners):
            landed(pairs[i].at[block], sent_pair.at[i, block])

            @pl.when(block != here)
            def _():
                landed(halves[i].at[block], sent.at[i, block])


def team_sum(collective_id, *values):
    return team_sum_and_rows(collective_id, None, *values)[0]


def team_sum_and_rows(collective_id, summed, *values):
    owners, cores = lax.axis_size("ctx"), lax.axis_size("tensor")
    amount = len(values)
    width = values[0].shape[1]
    mine = values[0].shape[0] // (owners * cores)
    blocks = [pltpu.VMEM((owners, mine, width), v.dtype) for v in values]
    more = [] if summed is None else [summed]
    out = pl.pallas_call(
        functools.partial(scatter_kernel, amount, bool(more), owners, cores),
        out_shape=[jax.ShapeDtypeStruct((mine, width), jnp.float32)] * amount
        + [jax.ShapeDtypeStruct(held_shape(m, owners), m.dtype) for m in more],
        in_specs=[ANY] * amount + [FAR] * len(more),
        out_specs=[INSIDE] * amount + [FAR] * len(more),
        scratch_shapes=blocks * 5
        + [pltpu.VMEM((mine, width), jnp.float32)]
        + [pltpu.SemaphoreType.DMA((amount, owners)) for _ in range(6)]
        + [sem for m in more for sem in swap_sems(owners)],
        compiler_params=params(collective_id),
        cost_estimate=cost(20 * amount),
        name="team_sum",
    )(*[v.reshape(owners, cores, mine, width) for v in values], *more)
    return out[:amount], out[amount:]


def swap_first(summed, held, local, sent, came, owners):
    here = lax.axis_index("ctx")
    count = summed.shape[0] // owners

    def rows(owner):
        return summed.at[pl.ds(pl.multiple_of(owner * count, count), count), :]

    for step in range(1, owners):
        other = lax.rem(here + step, owners)
        send(rows(other), held.at[here], sent.at[other], came.at[here], {"ctx": other})
    pltpu.make_async_copy(rows(here), held.at[here], local).start()


def put_rows(rows, outs, block, half, halves):
    amount = len(outs)
    units = rows.shape[1] // amount
    for j in range(units // block):
        start = half * units + j * block
        for i, out in enumerate(outs):
            first = (j * amount + i) * block
            piece = rows[:, first : first + block].astype(jnp.float32)
            if i < amount - 1:
                out[:, start : start + block] = piece
            else:
                out[start : start + block, :] = piece.T


def place_kernel(block, where, own_a, far_a, own_b, far_b, early, late, attn, *outs):
    core = where[0]
    for own, far, out in ((own_a, far_a, outs[0]), (own_b, far_b, outs[1])):
        out[0, core] = own[0]
        out[0, out.shape[1] - 1 - core] = far[0]
    put_rows(early[0], outs[2:5], block, 0, 2)
    put_rows(late[0], outs[2:5], block, 1, 2)
    put_rows(attn[0], outs[5:], outs[5].shape[1], 0, 1)


def place_all(streams, early, late, attn):
    owners, cores = lax.axis_size("ctx"), lax.axis_size("tensor")
    run = streams[0].shape
    block = late.shape[2] // (3 * BLOCKS // 2)

    def lead(shape):
        return pl.BlockSpec((1, *shape[1:]), lambda c, _: (c,) + (0,) * (len(shape) - 1))

    both = (run[0], cores, *run[1:])
    specs, shapes = [lead(both)] * 2, [jax.ShapeDtypeStruct(both, streams[0].dtype)] * 2
    for amount, units in ((3, 2 * late.shape[2] // 3), (4, attn.shape[2] // 4)):
        count = late.shape[1]
        specs += [pl.BlockSpec((count, units), lambda c, _: (0, c))] * (amount - 1)
        specs.append(pl.BlockSpec((units, count), lambda c, _: (c, 0)))
        wide = jax.ShapeDtypeStruct((count, owners * units), jnp.float32)
        shapes += [wide] * (amount - 1)
        shapes.append(jax.ShapeDtypeStruct((owners * units, count), jnp.float32))
    return pl.pallas_call(
        functools.partial(place_kernel, block),
        grid_spec=pltpu.PrefetchScalarGridSpec(
            num_scalar_prefetch=1,
            grid=(owners,),
            in_specs=[lead(v.shape) for v in (*streams, early, late, attn)],
            out_specs=specs,
        ),
        out_shape=shapes,
        compiler_params=pltpu.CompilerParams(
            dimension_semantics=("arbitrary",), vmem_limit_bytes=60 << 20
        ),
        cost_estimate=cost(7),
        name="place_all",
    )(lax.axis_index("tensor")[None].astype(jnp.int32), *streams, early, late, attn)


def swap_rest(summed, held, local, sent, came, owners):
    here = lax.axis_index("ctx")
    count = summed.shape[0] // owners
    own = summed.at[pl.ds(pl.multiple_of(here * count, count), count), :]
    for step in range(owners):
        source = lax.rem(here + owners - step, owners)
        if step == 0:
            pltpu.make_async_copy(own, held.at[here], local).wait()
        else:
            landed(held.at[source], came.at[source])
    for step in range(1, owners):
        other = lax.rem(here + step, owners)
        landed(held.at[other], sent.at[other])


def held_shape(summed, owners):
    return (owners, summed.shape[0] // owners, summed.shape[1])


def swap_sems(owners):
    return [
        pltpu.SemaphoreType.DMA,
        pltpu.SemaphoreType.DMA((owners,)),
        pltpu.SemaphoreType.DMA((owners,)),
    ]


def around(axis, size):
    index = lax.axis_index(axis)
    return [{axis: lax.rem(index + step, size)} for step in range(1, size)]


def swap_kernel_alone(owners, summed, held, *sems):
    greet(around("ctx", owners))
    swap_first(summed, held, *sems, owners)
    swap_rest(summed, held, *sems, owners)


def team_rows(collective_id, summed):
    owners = lax.axis_size("ctx")
    return pl.pallas_call(
        functools.partial(swap_kernel_alone, owners),
        out_shape=jax.ShapeDtypeStruct(held_shape(summed, owners), summed.dtype),
        in_specs=[INSIDE],
        out_specs=ANY,
        scratch_shapes=swap_sems(owners),
        compiler_params=params(collective_id),
        cost_estimate=cost(20),
        name="team_rows",
    )(summed)


def close_kernel(amount, shards_in, owners, cores, *refs):
    values, mixed, grads = refs[:amount], refs[amount], refs[amount + 1]
    refs = refs[amount + 2 :]
    outs, mix_out, late = refs[:amount], refs[amount], refs[amount + 1]
    summed, refs = refs[amount + 2], refs[amount + 3 :]
    pairs, half, quarters, blocks, sent, came = refs[:6]
    sent_c, came_c, sent_s, came_s, sent_b, came_b = refs[6:12]
    swap = refs[12:]
    here, core, pair, right, left = ring(owners, cores)
    index = lax.axis_index("shard")
    near = [lax.rem(here + step, owners) for step in range(1, owners)]
    others = [lax.rem(index + step, shards_in) for step in range(1, shards_in)]
    greet([{"tensor": pair}] + around("ctx", owners) + around("shard", shards_in))
    wide = mixed.shape[1] // cores
    thin = wide // owners
    send(
        mixed.at[:, pl.ds(pl.multiple_of(pair * wide, wide), wide)],
        pairs,
        sent.at[amount],
        came.at[amount],
        {"tensor": pair},
    )
    for i in range(amount):
        send(values[i], outs[i], sent.at[i], came.at[i], {"tensor": pair})
    landed(pairs, came.at[amount])
    half[...] = mixed[:, pl.ds(pl.multiple_of(core * wide, wide), wide)] + pairs[...]
    for other in near:
        send(
            half.at[:, pl.ds(pl.multiple_of(other * thin, thin), thin)],
            quarters.at[here],
            sent_c.at[other],
            came_c.at[here],
            {"ctx": other},
        )
    swap_first(grads, late, *swap, owners)
    total = half[:, pl.ds(pl.multiple_of(here * thin, thin), thin)]
    for other in near:
        landed(quarters.at[other], came_c.at[other])
        total += quarters[other]
    blocks[index] = total
    for other in others:
        send(
            blocks.at[index], blocks.at[index], sent_s.at[other], came_s.at[index], {"shard": other}
        )
    for other in others:
        landed(blocks.at[other], came_s.at[other])
    total = blocks[0]
    for block in range(1, shards_in):
        total += blocks[block]

    def place(owner, half_of):
        return summed.at[half_of * owners + owner]

    summed[core * owners + here] = total
    for other in near:
        send(place(here, core), place(here, core), sent_b.at[other], came_b.at[here, core], {"ctx": other})
    send(place(here, core), place(here, core), sent_b.at[here], came_b.at[here, core], {"tensor": pair})
    for other in near:
        landed(place(other, core), came_b.at[other, core])
        send(
            place(other, core),
            place(other, core),
            sent_b.at[owners + other],
            came_b.at[other, core],
            {"tensor": pair},
        )
    for owner in range(owners):
        landed(place(owner, pair), came_b.at[owner, pair])
        landed(place(owner, core), sent_b.at[owner])
    for owner in range(owners):
        for half_of in range(cores):
            found = summed[half_of * owners + owner]
            start = (half_of * owners + owner) * thin
            for row in range(mix_out.shape[0] * mix_out.shape[1]):
                k, h = row // mix_out.shape[1], row % mix_out.shape[1]
                mix_out[k, h : h + 1, start : start + thin] = found[row : row + 1, :]
    for other in near:
        landed(place(other, core), sent_b.at[owners + other])
        landed(quarters.at[other], sent_c.at[other])
    for other in others:
        landed(blocks.at[other], sent_s.at[other])
    landed(pairs, sent.at[amount])
    swap_rest(grads, late, *swap, owners)
    for i in range(amount):
        landed(outs[i], came.at[i])
        landed(values[i], sent.at[i])


def close_team(collective_id, grads, mixed, *values):
    shards_in, owners, cores = [lax.axis_size(a) for a in ("shard", "ctx", "tensor")]
    amount = len(values)
    height, width = mixed.shape
    thin = width // (cores * owners)
    out = pl.pallas_call(
        functools.partial(close_kernel, amount, shards_in, owners, cores),
        out_shape=[
            jax.ShapeDtypeStruct(v.shape, v.dtype) for v in values
        ]
        + [jax.ShapeDtypeStruct((height // 2, 2, width), jnp.float32)]
        + [jax.ShapeDtypeStruct(held_shape(grads, owners), grads.dtype)],
        in_specs=[INSIDE] * (amount + 2),
        out_specs=[ANY] * amount + [INSIDE, ANY],
        scratch_shapes=[
            pltpu.VMEM((cores * owners, height, thin), jnp.float32),
            pltpu.VMEM((height, width // cores), jnp.float32),
            pltpu.VMEM((height, width // cores), jnp.float32),
            pltpu.VMEM((owners, height, thin), jnp.float32),
            pltpu.VMEM((shards_in, height, thin), jnp.float32),
            pltpu.SemaphoreType.DMA((amount + 1,)),
            pltpu.SemaphoreType.DMA((amount + 1,)),
            pltpu.SemaphoreType.DMA((owners,)),
            pltpu.SemaphoreType.DMA((owners,)),
            pltpu.SemaphoreType.DMA((shards_in,)),
            pltpu.SemaphoreType.DMA((shards_in,)),
            pltpu.SemaphoreType.DMA((2 * owners,)),
            pltpu.SemaphoreType.DMA((owners, cores)),
        ]
        + swap_sems(owners),
        compiler_params=params(collective_id),
        cost_estimate=cost(60),
        name="close_team",
    )(*values, mixed, grads)
    return out[amount], out[:amount], out[amount + 1]


def ffn_kernel(
    u_ref,
    dy_ref,
    gate_ref,
    up_ref,
    down_ref,
    y_ref,
    du_ref,
    early_ref,
    late_ref,
    y_sum,
    du_sum,
    u_t,
    dy_t,
):
    step = pl.program_id(0)
    early = step < pl.num_programs(0) // 2
    total, width = u_ref.shape
    block = gate_ref.shape[1]
    tile = down_ref.shape[2]

    @pl.when(step == 0)
    def _():
        y_sum[...] = jnp.zeros_like(y_sum)
        du_sum[...] = jnp.zeros_like(du_sum)
        for start in range(0, width, tile):
            u_t[start : start + tile, :] = u_ref[:, start : start + tile].T
            dy_t[start : start + tile, :] = dy_ref[:, start : start + tile].T

    gate = dot(u_ref[...], gate_ref[...])
    upward = dot(u_ref[...], up_ref[...])
    shards_in = down_ref.shape[0]
    grad_hidden = 0.0
    for k in range(shards_in):
        grad_hidden = grad_hidden + contract_cols(
            dy_ref[:, k * tile : (k + 1) * tile], down_ref[k]
        )
    sigma = jax.nn.sigmoid(gate)
    swish = gate * sigma
    hidden = (swish * upward).astype(jnp.bfloat16)
    grad_gate = (grad_hidden * upward * (sigma + swish * (1.0 - sigma))).astype(jnp.bfloat16)
    grad_up = (grad_hidden * swish).astype(jnp.bfloat16)
    for k in range(shards_in):
        span = slice(k * tile, (k + 1) * tile)
        y_sum[:, span] += dot(hidden, down_ref[k])
        du_sum[:, span] += contract_cols(grad_gate, gate_ref[span, :]) + contract_cols(
            grad_up, up_ref[span, :]
        )

    def weights_back(grad_ref):
        for start in range(0, width, tile):
            span = slice(start, start + tile)
            grad_ref[span, :block] = dot(u_t[span, :], grad_gate).astype(jnp.bfloat16)
            grad_ref[span, block : 2 * block] = dot(u_t[span, :], grad_up).astype(jnp.bfloat16)
            grad_ref[span, 2 * block :] = dot(dy_t[span, :], hidden).astype(jnp.bfloat16)

    @pl.when(early)
    def _():
        weights_back(early_ref)

    @pl.when(jnp.logical_not(early))
    def _():
        weights_back(late_ref)

    @pl.when(step == pl.num_programs(0) - 1)
    def _():
        y_ref[...] = y_sum[...].astype(jnp.bfloat16)
        du_ref[...] = du_sum[...].astype(jnp.bfloat16)


def ffn(u, dy, weights):
    total, width = u.shape
    shards_in = lax.axis_size("shard")
    depth = width // shards_in
    units = weights.shape[1] // 3
    blocks = BLOCKS
    block = units // blocks
    half = blocks // 2
    whole = pl.BlockSpec((total, width), lambda j: (0, 0), pipeline_mode=pl.Buffered(1))
    low = functools.partial(jax.ShapeDtypeStruct, dtype=jnp.bfloat16)
    return pl.pallas_call(
        ffn_kernel,
        grid=(blocks,),
        in_specs=[
            whole,
            whole,
            pl.BlockSpec((width, block), lambda j: (0, j)),
            pl.BlockSpec((width, block), lambda j: (0, blocks + j)),
            pl.BlockSpec(
                (shards_in, block, depth),
                lambda j: (0, j % (depth // block), 2 * units // depth + j // (depth // block)),
            ),
        ],
        out_specs=[
            whole,
            whole,
            pl.BlockSpec((width, 3 * block), lambda j: (0, jnp.minimum(j, half - 1))),
            pl.BlockSpec((width, 3 * block), lambda j: (0, jnp.maximum(j - half, 0))),
        ],
        out_shape=[low((total, width))] * 2 + [low((width, 3 * units // 2))] * 2,
        scratch_shapes=[
            pltpu.VMEM((total, width), jnp.float32),
            pltpu.VMEM((total, width), jnp.float32),
            pltpu.VMEM((width, total), jnp.bfloat16),
            pltpu.VMEM((width, total), jnp.bfloat16),
        ],
        compiler_params=pltpu.CompilerParams(
            dimension_semantics=("arbitrary",), vmem_limit_bytes=60 << 20
        ),
        cost_estimate=cost(30),
        name="ffn",
    )(u, dy, weights, weights, weights.reshape(shards_in, depth, 3 * units))


def pack_kernel(sent, value, out):
    for i in range(value.shape[1]):
        out[0, i] = value[:, i, :]


def pack_runs(value, sent, part):
    rows_in, total, width = value.shape
    return pl.pallas_call(
        pack_kernel,
        grid_spec=pltpu.PrefetchScalarGridSpec(
            num_scalar_prefetch=1,
            grid=(sent.shape[0],),
            in_specs=[
                pl.BlockSpec((part, total, width), lambda c, first: (first[c], 0, 0)),
            ],
            out_specs=pl.BlockSpec((1, total, part, width), lambda c, first: (c, 0, 0, 0)),
        ),
        out_shape=jax.ShapeDtypeStruct((sent.shape[0], total, part, width), value.dtype),
        compiler_params=pltpu.CompilerParams(dimension_semantics=("arbitrary",)),
        cost_estimate=cost(2),
        name="pack_runs",
    )(sent, value)


def head_probs(query, key, placing, placed):
    scores = contract_cols(query, key) * HD ** (-0.5)
    allowed = (placed >= placing[:, 0:1]) & (placed <= placing[:, 1:2])
    scores = jnp.where(allowed, scores, FLOOR_SCORE)
    probs = jnp.exp(scores - jnp.max(scores, -1, keepdims=True))
    return probs / jnp.sum(probs, -1, keepdims=True)


def turn(value, turns, back):
    swung = pltpu.roll(value, HD // 2, 1) * turns[1]
    return value * turns[0] - swung if back else value * turns[0] + swung


def attend_kernel(
    u_ref, qkv_ref, out_ref, turns, placing, placed, y_ref, q_ref, k_ref, v_ref, o_ref
):
    count = q_ref.shape[1]
    u = u_ref[...]
    for first in range(0, count, HD):
        head = slice(first, first + HD)

        def lin(which):
            start = which * count + first
            return dot(u, qkv_ref[:, start : start + HD])

        query = turn(lin(0), turns, False).astype(jnp.bfloat16)
        key = turn(lin(1), turns, False).astype(jnp.bfloat16)
        value = lin(2).astype(jnp.bfloat16)
        q_ref[:, head] = query
        k_ref[:, head] = key
        v_ref[:, head] = value
        probs = head_probs(query, key, placing[...], placed[...])
        o_ref[:, head] = dot(probs.astype(jnp.bfloat16), value).astype(jnp.bfloat16)
    width = y_ref.shape[1]
    for start in range(0, width, 512):
        y_ref[:, start : start + 512] = dot(o_ref[...], out_ref[:, start : start + 512])


def attend(u, qkv, out_w, turns, placing, placed):
    total, count = u.shape[0], out_w.shape[0]
    low = jax.ShapeDtypeStruct((total, count), jnp.bfloat16)
    return pl.pallas_call(
        attend_kernel,
        out_shape=[jax.ShapeDtypeStruct((total, out_w.shape[1]), jnp.float32)] + [low] * 4,
        in_specs=[INSIDE] * 6,
        out_specs=[INSIDE] * 5,
        compiler_params=pltpu.CompilerParams(vmem_limit_bytes=60 << 20),
        cost_estimate=cost(12),
        name="attend",
    )(u, qkv, out_w, turns, placing, placed)


def attend_back_kernel(
    dy_ref,
    u_ref,
    qkv_ref,
    out_ref,
    q_ref,
    k_ref,
    v_ref,
    o_ref,
    turns,
    placing,
    placed,
    du_ref,
    grad_ref,
    lin,
):
    count = q_ref.shape[1]
    width = du_ref.shape[1]
    scale = HD ** (-0.5)
    low = jnp.bfloat16
    for first in range(0, count, HD):
        head = slice(first, first + HD)
        query, key, value = q_ref[:, head], k_ref[:, head], v_ref[:, head]
        grad_out = contract_cols(dy_ref[...], out_ref[head, :]).astype(low)
        probs = head_probs(query, key, placing[...], placed[...])
        grad_probs = contract_cols(grad_out, value)
        delta = jnp.sum(probs * grad_probs, -1, keepdims=True)
        grad_scores = (probs * (grad_probs - delta)).astype(low)
        grad_query = turn(dot(grad_scores, key) * scale, turns, True)
        grad_key = turn(contract_rows(grad_scores, query) * scale, turns, True)
        grad_value = contract_rows(probs.astype(low), grad_out)
        for which, grad in enumerate((grad_query, grad_key, grad_value)):
            start = which * count + first
            lin[:, start : start + HD] = grad.astype(low)
    tile = min(512, width)
    edge = lin.shape[1]
    for start in range(0, width, tile):
        span = slice(start, start + tile)
        du_ref[:, span] = contract_cols(lin[...], qkv_ref[span, :]).astype(low)
        grad_ref[span, :edge] = dot(u_ref[:, span].T, lin[...]).astype(low)
        grad_ref[span, edge:] = dot(dy_ref[:, span].T, o_ref[...]).astype(low)


def attend_back(dy, u, qkv, out_w, q, k, v, o, turns, placing, placed):
    total, width = u.shape
    count = q.shape[1]
    return pl.pallas_call(
        attend_back_kernel,
        out_shape=[
            jax.ShapeDtypeStruct((total, width), jnp.bfloat16),
            jax.ShapeDtypeStruct((width, 4 * count), jnp.bfloat16),
        ],
        in_specs=[INSIDE] * 11,
        out_specs=[INSIDE] * 2,
        scratch_shapes=[pltpu.VMEM((total, 3 * count), jnp.bfloat16)],
        compiler_params=pltpu.CompilerParams(vmem_limit_bytes=60 << 20),
        cost_estimate=cost(20),
        name="attend_back",
    )(dy, u, qkv, out_w, q, k, v, o, turns, placing, placed)


EXACT = functools.partial(
    lax.dot_general, precision=PRECISE, preferred_element_type=jnp.float32
)


def columns_of(pieces):
    rows_in = pieces[0].shape[0]
    lane = lax.broadcasted_iota(jnp.int32, (rows_in, 8), 1)
    out = jnp.zeros((rows_in, 8), jnp.float32)
    for k, piece in enumerate(pieces):
        out = jnp.where(lane == k, piece, out)
    return out


def tables_of(current, weight, static, table_ref, active_ref):
    branch_in = 0.0
    tables = []
    for i, stream in enumerate(current):
        normed, scaled = norm_rows(stream)
        active = jnp.tanh(EXACT(normed, weight, (((1,), (1,)), ((), ()))))
        table = active + static[i : i + 1, :]
        table_ref[i] = table
        active_ref[i] = active
        tables.append(table)
        branch_in = branch_in + table[:, 0:1] * stream
    return tables, branch_in


def norm_plain(value):
    centred = value - jnp.mean(value, -1, keepdims=True)
    scaled = lax.rsqrt(jnp.mean(centred * centred, -1, keepdims=True) + EPSILON)
    return (centred * scaled, scaled)


def mix_first(current, weight, static):
    normed, _ = norm_plain(current)
    active = jnp.tanh(jnp.einsum("tsd,dk->tsk", normed, weight, precision=PRECISE))
    table = active + static
    total = current.shape[1]
    branch_in = sum(table[:, i, 0][:, None] * current[:, i] for i in range(total))
    normed, scaled = norm_plain(branch_in)

    def by_stream(value):
        return jnp.pad(value.transpose(1, 0, 2), ((0, 0), (0, 0), (0, 8 - value.shape[2])))

    scaled = jnp.pad(scaled, ((0, 0), (0, 7)))
    return normed.astype(jnp.bfloat16), normed, scaled, by_stream(table), by_stream(active)


def mix_second_kernel(
    source,
    streams,
    branch_out,
    table_one,
    arrived,
    weight,
    static,
    middle_ref,
    low_ref,
    grad_low_ref,
    normed_ref,
    scaled_ref,
    table_ref,
    active_ref,
    top_ref,
):
    total = streams.shape[0]
    y = branch_out[...]
    first = [table_one[i] for i in range(total)]
    current = [streams[i].astype(jnp.float32) for i in range(total)]
    middle = []
    for j in range(total):
        mixed = first[j][:, total + 1 : total + 2] * y
        for i in range(total):
            mixed = mixed + first[i][:, 1 + j : 2 + j] * current[i]
        middle.append(mixed)
        middle_ref[j] = mixed
    tables, branch_in = tables_of(middle, weight[...], static[...], table_ref, active_ref)
    normed, scaled = norm_rows(branch_in)
    normed_ref[...] = normed
    low_ref[...] = normed.astype(jnp.bfloat16)
    scaled_ref[...] = columns_of([scaled])
    grad = 0.0
    for j in range(total):
        top = arrived[0, j]
        top_ref[j] = top
        grad = grad + tables[j][:, total + 1 : total + 2] * top.astype(jnp.float32)
    grad_low_ref[...] = grad.astype(jnp.bfloat16)


def connection_back(
    current, grad_top, branch_out, grad_in, normed_in, scaled_in, tables, actives, weight, sums
):
    total = len(current)
    weight_sum, static_sum = sums
    dx = scaled_in * (grad_in - mean_of(grad_in) - normed_in * mean_of(grad_in * normed_in))
    result = []
    for i, stream in enumerate(current):
        pieces = [jnp.sum(dx * stream, -1, keepdims=True)]
        pieces += [jnp.sum(stream * top, -1, keepdims=True) for top in grad_top]
        pieces.append(jnp.sum(grad_top[i] * branch_out, -1, keepdims=True))
        grad_table = columns_of(pieces)
        static_sum[i : i + 1, :] += jnp.sum(grad_table, 0, keepdims=True)
        grad_inner = grad_table * (1.0 - actives[i] * actives[i])
        normed, scaled = norm_rows(stream)
        weight_sum[...] += EXACT(grad_inner, normed, (((0,), (0,)), ((), ())))
        grad_normed = EXACT(grad_inner, weight, (((1,), (0,)), ((), ())))
        grad = tables[i][:, 0:1] * dx + norm_back(normed, scaled, grad_normed)
        for j in range(total):
            grad = grad + tables[i][:, 1 + j : 2 + j] * grad_top[j]
        result.append(grad)
    return result


def start_sums(sums):
    @pl.when(pl.program_id(0) == 0)
    def _():
        for ref in sums:
            ref[...] = jnp.zeros_like(ref)


def back_second_kernel(
    middle,
    top,
    branch_out,
    grad_in,
    normed_in,
    scaled_in,
    table,
    active,
    table_one,
    weight,
    final_ref,
    grad_ref,
    grad_low_ref,
    *sums,
):
    start_sums(sums)
    total = middle.shape[0]
    current = [middle[i] for i in range(total)]
    grad_top = [top[i].astype(jnp.float32) for i in range(total)]
    tables = [table[i] for i in range(total)]
    y = branch_out[...]
    for j in range(total):
        mixed = tables[j][:, total + 1 : total + 2] * y
        for i in range(total):
            mixed = mixed + tables[i][:, 1 + j : 2 + j] * current[i]
        final_ref[j] = mixed.astype(jnp.bfloat16)
    grads = connection_back(
        current,
        grad_top,
        y,
        grad_in[...],
        normed_in[...],
        scaled_in[:, 0:1],
        tables,
        [active[i] for i in range(total)],
        weight[...],
        sums,
    )
    low = 0.0
    for j in range(total):
        grad_ref[j] = grads[j]
        low = low + table_one[j][:, total + 1 : total + 2] * grads[j]
    grad_low_ref[...] = low.astype(jnp.bfloat16)


def back_first_kernel(
    streams,
    top,
    branch_out,
    grad_in,
    normed_in,
    scaled_in,
    table,
    active,
    weight,
    grad_ref,
    *sums,
):
    start_sums(sums)
    total = streams.shape[0]
    grads = connection_back(
        [streams[i].astype(jnp.float32) for i in range(total)],
        [top[i] for i in range(total)],
        branch_out[...],
        grad_in[...],
        normed_in[...],
        scaled_in[:, 0:1],
        [table[i] for i in range(total)],
        [active[i] for i in range(total)],
        weight[...],
        sums,
    )
    for j in range(total):
        grad_ref[j] = grads[j].astype(jnp.bfloat16)


def by_token(tile, shape, kind=jnp.float32):
    block = (*shape[:-2], tile, shape[-1])
    lead = (0,) * (len(shape) - 2)
    spec = pl.BlockSpec(block, lambda step, *_: (*lead, step, 0))
    return spec, jax.ShapeDtypeStruct(shape, kind)


def fixed(shape, kind=jnp.float32):
    spec = pl.BlockSpec(shape, lambda step, *_: (0,) * len(shape))
    return spec, jax.ShapeDtypeStruct(shape, kind)


def token_call(kernel, name, tile, ins, outs, prefetch=(), special=None):
    specs, values = [], []
    for value, tiled in ins:
        if tiled == "run":
            specs.append(special)
        else:
            specs.append(by_token(tile, value.shape)[0] if tiled else fixed(value.shape)[0])
        values.append(value)
    tokens = outs[0][1].shape[-2]
    return pl.pallas_call(
        kernel,
        grid_spec=pltpu.PrefetchScalarGridSpec(
            num_scalar_prefetch=len(prefetch),
            grid=(tokens // tile,),
            in_specs=specs,
            out_specs=[o[0] for o in outs],
        ),
        out_shape=[o[1] for o in outs],
        compiler_params=pltpu.CompilerParams(
            dimension_semantics=("arbitrary",), vmem_limit_bytes=60 << 20
        ),
        cost_estimate=cost(5),
        name=name,
    )(*prefetch, *values)


def shards(
    streams,
    lengths,
    destination,
    w_query,
    w_key,
    w_value,
    w_output,
    w_gate,
    w_up,
    w_down,
    mix_weight,
    mix_static,
    cotangent,
):
    rows_here, stream_total, width = streams.shape
    owners = lax.axis_size("ctx")
    cores = lax.axis_size("tensor")
    here = lax.axis_index("ctx")
    core = lax.axis_index("tensor")
    run_rows = rows_here // owners
    part = run_rows // cores
    mine = rows_here // cores
    group_rows = rows_here * owners
    head_cols = w_query.shape[1] // owners
    heads = head_cols // HD
    units = w_gate.shape[1] // owners
    scale = HD ** (-0.5)

    def columns(weight, count):
        return lax.dynamic_slice_in_dim(weight, here * count, count, 1)

    def rows(weight, count):
        return lax.dynamic_slice_in_dim(weight, here * count, count, 0)

    order = jnp.arange(group_rows, dtype=jnp.int32)
    within = order % mine
    placed = (
        order // rows_here * rows_here
        + within // part * run_rows
        + order % rows_here // mine * part
        + within % part
    )
    spans = lengths[0]
    count = jnp.arange(spans.shape[0], dtype=jnp.int32)
    starts = jnp.sum(jnp.where(count[None, :] < count[:, None], spans[None, :], 0), 1)
    begin = jnp.max(jnp.where(starts[None, :] <= placed[:, None], starts[None, :], 0), axis=1)
    cosine, sine = angles(placed - begin, HD)
    turns = jnp.stack(
        [jnp.concatenate([cosine, cosine], -1), jnp.concatenate([-sine, sine], -1)]
    ).reshape(2, group_rows, HD)
    placing = jnp.stack([begin, placed], 1)
    placed = placed[None]

    local_dest = destination - lax.axis_index("shard") * group_rows
    heads_of_runs = local_dest.reshape(owners, run_rows)[:, 0]
    came_from = heads_of_runs // rows_here
    note = jnp.broadcast_to(jnp.pad(heads_of_runs, (0, 128 - owners)), (8, 128))

    turned_weight = jnp.pad(mix_weight.transpose(0, 2, 1), ((0, 0), (0, 2), (0, 0)))
    static = jnp.pad(mix_static, ((0, 0), (0, 0), (0, 2)))
    split = streams.reshape(owners, cores, part, stream_total, width)
    current = lax.dynamic_index_in_dim(split, core, 1, keepdims=False)
    current = current.reshape(mine, stream_total, width)
    attn_low, attn_normed, attn_scaled, table_one, active_one = mix_first(
        current.astype(jnp.float32), mix_weight[0], mix_static[0]
    )
    current = current.transpose(1, 0, 2)
    low = jnp.bfloat16
    tile = min(16, part)
    small = by_token(tile, (stream_total, mine, 8))
    attn_input, qkv, out_w, packed, notes = open_team(
        0, attn_low, (w_query, w_key, w_value, w_output, w_gate, w_up, w_down), note
    )
    ffn_weights = lax.all_gather(packed, "shard", axis=0, tiled=True)
    every = notes[:, 0, :owners]
    sent = jnp.sum(jnp.where(every // rows_here == here, every % rows_here, 0), 1) // part + core
    packed = pack_runs(cotangent, sent, part)
    arrived = lax.all_to_all(packed, "ctx", split_axis=0, concat_axis=0, tiled=True)
    attn_part, queries, keys, values, attended = attend(
        attn_input, qkv, out_w, turns, placing, placed
    )
    [attn_out] = team_sum(1, attn_part)

    (
        middle,
        ffn_low,
        grad_ffn_low,
        ffn_normed,
        ffn_scaled,
        table_two,
        active_two,
        grad_top,
    ) = token_call(
        mix_second_kernel,
        "mix_second",
        tile,
        [
            (current, True),
            (attn_out, True),
            (table_one, True),
            (arrived, "run"),
            (turned_weight[1], False),
            (static[1], False),
        ],
        [
            by_token(tile, (stream_total, mine, width)),
            by_token(tile, (mine, width), low),
            by_token(tile, (mine, width), low),
            by_token(tile, (mine, width)),
            by_token(tile, (mine, 8)),
            small,
            small,
            by_token(tile, (stream_total, mine, width), low),
        ],
        (came_from,),
        pl.BlockSpec(
            (1, stream_total, tile, width),
            lambda step, source: (source[step * tile // part], 0, step % (part // tile), 0),
        ),
    )
    ffn_input, grad_ffn_out = team_gather(2, ffn_low, grad_ffn_low)
    ffn_part, ffn_input_part, *ffn_grads = ffn(ffn_input, grad_ffn_out, ffn_weights)

    def shard_sum(partial):
        return lax.psum_scatter(partial, "shard", scatter_dimension=0, tiled=True)

    early_sum, late_sum = [shard_sum(grads) for grads in ffn_grads]
    ffn_out, grad_ffn_input = team_sum(3, ffn_part, ffn_input_part)
    sums = [fixed((8, width)), fixed((stream_total, 8))]
    final, grad_middle, grad_attn_low, weight_two, static_two = token_call(
        back_second_kernel,
        "back_second",
        tile,
        [
            (middle, True),
            (grad_top, True),
            (ffn_out, True),
            (grad_ffn_input, True),
            (ffn_normed, True),
            (ffn_scaled, True),
            (table_two, True),
            (active_two, True),
            (table_one, True),
            (turned_weight[1], False),
        ],
        [
            by_token(tile, (stream_total, mine, width), low),
            by_token(tile, (stream_total, mine, width)),
            by_token(tile, (mine, width), low),
            *sums,
        ],
    )
    [grad_attn_out] = team_gather(4, grad_attn_low)

    attn_input_part, attn_grads = attend_back(
        grad_attn_out, attn_input, qkv, out_w, queries, keys, values, attended, turns, placing, placed
    )
    attn_sum = shard_sum(attn_grads)
    [grad_attn_input], [early_rows] = team_sum_and_rows(5, early_sum, attn_input_part)
    grad_current, weight_one, static_one = token_call(
        back_first_kernel,
        "back_first",
        tile,
        [
            (current, True),
            (grad_middle, True),
            (attn_out, True),
            (grad_attn_input, True),
            (attn_normed, True),
            (attn_scaled, True),
            (table_one, True),
            (active_one, True),
            (turned_weight[0], False),
        ],
        [by_token(tile, (stream_total, mine, width), low), *sums],
    )
    statics = jnp.stack([static_one, static_two]).reshape(1, -1)
    mixed = jnp.concatenate(
        [
            jnp.stack([weight_one, weight_two], 1).reshape(16, width),
            jnp.pad(statics, ((0, 7), (0, width - statics.size))),
        ],
        0,
    )

    def runs(value):
        return value.transpose(1, 0, 2).reshape(owners, part, stream_total, width)

    own_final, own_grad = runs(final), runs(grad_current)
    mixed, (far_final, far_grad), late_rows = close_team(
        7, late_sum, mixed, own_final, own_grad
    )
    mixed, attn_sum = lax.optimization_barrier((mixed, attn_sum))
    (
        streams_out,
        grad_streams,
        grad_gate,
        grad_up,
        grad_down,
        grad_query,
        grad_key,
        grad_value,
        grad_output,
    ) = place_all(
        (own_final, far_final, own_grad, far_grad), early_rows, late_rows, team_rows(8, attn_sum)
    )
    columns_in = mix_weight.shape[2]
    grad_mix_weight = mixed[:columns_in].transpose(1, 2, 0)
    grad_mix_static = mixed[8, 0, : statics.size].reshape(2, stream_total, 8)[:, :, :columns_in]

    return (
        streams_out.reshape(rows_here, stream_total, width),
        grad_streams.reshape(rows_here, stream_total, width),
        grad_query,
        grad_key,
        grad_value,
        grad_output,
        grad_gate,
        grad_up,
        grad_down,
        grad_mix_weight,
        grad_mix_static,
    )


def solution(mesh):
    return jax.shard_map(
        shards,
        mesh=mesh,
        in_specs=(
            P(("shard", "ctx"), None, None),
            P("shard", None),
            P(("shard", "ctx")),
            P("shard", "tensor"),
            P("shard", "tensor"),
            P("shard", "tensor"),
            P("tensor", "shard"),
            P("shard", "tensor"),
            P("shard", "tensor"),
            P("tensor", "shard"),
            P(),
            P(),
            P(("shard", "ctx"), None, None),
        ),
        out_specs=(
            P(("shard", "ctx"), None, None),
            P(("shard", "ctx"), None, None),
            P(("shard", "ctx"), "tensor"),
            P(("shard", "ctx"), "tensor"),
            P(("shard", "ctx"), "tensor"),
            P("tensor", ("shard", "ctx")),
            P(("shard", "ctx"), "tensor"),
            P(("shard", "ctx"), "tensor"),
            P("tensor", ("shard", "ctx")),
            P(),
            P(),
        ),
        check_vma=False,
    )
```

```python
import functools

import jax
import jax.numpy as jnp
import numpy as np
from jax import lax
from jax.experimental import pallas as pl
from jax.experimental.pallas import tpu as pltpu
from jax.sharding import PartitionSpec as P

HD = 128


PRECISE = lax.Precision.HIGHEST
EPSILON = 1e-05
FLOOR_SCORE = -1e30
BLOCKS = 4


def mean_of(value):
    width = value.shape[-1]
    while value.shape[-1] > 128 and value.shape[-1] % 256 == 0:
        half = value.shape[-1] // 2
        value = value[..., :half] + value[..., half:]
    return jnp.sum(value, -1, keepdims=True) * (1.0 / width)


def norm_rows(value):
    centred = value - mean_of(value)
    scaled = lax.rsqrt(mean_of(centred * centred) + EPSILON)
    return (centred * scaled, scaled)


def norm_back(normed, scaled, grad):
    return scaled * (grad - mean_of(grad) - normed * mean_of(grad * normed))


def angles(positions, head_size):
    indices = np.arange(head_size // 2, dtype=np.float64)
    frequency = (10000.0 ** (-(2.0 * indices / head_size))).astype(np.float32)
    turned = positions.astype(jnp.float32)[:, None] * frequency[None, :]
    return (jnp.cos(turned)[:, None, :], jnp.sin(turned)[:, None, :])


def dot(left, right):
    return jnp.dot(left, right, preferred_element_type=jnp.float32)


def contract_rows(left, right):
    return lax.dot_general(
        left, right, (((0,), (0,)), ((), ())), preferred_element_type=jnp.float32
    )


def contract_cols(left, right):
    return lax.dot_general(
        left, right, (((1,), (1,)), ((), ())), preferred_element_type=jnp.float32
    )


def greet(partners):
    barrier = pltpu.get_barrier_semaphore()
    for partner in partners:
        pl.semaphore_signal(
            barrier, inc=1, device_id=partner, device_id_type=pl.DeviceIdType.MESH
        )
    pl.semaphore_wait(barrier, len(partners))


def send(source, target, sent, received, device):
    pltpu.make_async_remote_copy(
        src_ref=source,
        dst_ref=target,
        send_sem=sent,
        recv_sem=received,
        device_id=device,
        device_id_type=pl.DeviceIdType.MESH,
    ).start()


def landed(block, semaphore):
    pltpu.make_async_copy(block, block, semaphore).wait()


def ring(owners, cores):
    here = lax.axis_index("ctx")
    core = lax.axis_index("tensor")
    right, left = lax.rem(here + 1, owners), lax.rem(here + owners - 1, owners)
    return here, core, cores - 1 - core, right, left


def gather_first(values, outs, sems, owners, cores):
    local, sent_right, sent_left, sent_pair, came, came_pair = sems
    here, core, pair, right, left = ring(owners, cores)
    for i, (value, out) in enumerate(zip(values, outs)):
        target = out.at[here, core]

        @pl.when(here < owners - 1)
        def _():
            send(value, target, sent_right.at[i, here], came.at[i, here], {"ctx": right})

        @pl.when(here > 0)
        def _():
            send(value, target, sent_left.at[i, here], came.at[i, here], {"ctx": left})

        send(value, target, sent_pair.at[i, here], came_pair.at[i, here], {"tensor": pair})
        pltpu.make_async_copy(value, target, local.at[i]).start()


def gather_rest(values, outs, sems, owners, cores):
    local, sent_right, sent_left, sent_pair, came, came_pair = sems
    here, core, pair, right, left = ring(owners, cores)

    def arrive(i, out, block, onward, sent, device):
        held = out.at[block, core]
        landed(held, came.at[i, block])

        @pl.when(onward)
        def _():
            send(held, held, sent.at[i, block], came.at[i, block], device)

        send(held, held, sent_pair.at[i, block], came_pair.at[i, block], {"tensor": pair})

    for step in range(1, owners):
        for i, out in enumerate(outs):

            @pl.when(here >= step)
            def _():
                arrive(i, out, here - step, here < owners - 1, sent_right, {"ctx": right})

            @pl.when(here + step < owners)
            def _():
                arrive(i, out, here + step, here > 0, sent_left, {"ctx": left})

    for i, (value, out) in enumerate(zip(values, outs)):
        pltpu.make_async_copy(value, out.at[here, core], local.at[i]).wait()
        for block in range(owners):
            landed(out.at[block, pair], came_pair.at[i, block])
            landed(out.at[block, core], sent_pair.at[i, block])

            @pl.when((here < owners - 1) & (block <= here))
            def _():
                landed(out.at[block, core], sent_right.at[i, block])

            @pl.when((here > 0) & (block >= here))
            def _():
                landed(out.at[block, core], sent_left.at[i, block])


def gather_sems(amount, owners):
    return [pltpu.SemaphoreType.DMA((amount,))] + [
        pltpu.SemaphoreType.DMA((amount, owners)) for _ in range(5)
    ]


def line_partners(owners, cores):
    here, core, pair, right, left = ring(owners, cores)
    return [{"ctx": right}, {"ctx": left}, {"tensor": pair}]


def gather_kernel(amount, owners, cores, *refs):
    values, outs, sems = refs[:amount], refs[amount : 2 * amount], refs[2 * amount :]
    greet(line_partners(owners, cores))
    gather_first(values, outs, sems, owners, cores)
    gather_rest(values, outs, sems, owners, cores)


ANY = pl.BlockSpec(memory_space=pl.ANY)
FAR = pl.BlockSpec(memory_space=pltpu.HBM)
INSIDE = pl.BlockSpec(memory_space=pltpu.VMEM)


def params(collective_id):
    return pltpu.CompilerParams(
        collective_id=collective_id, has_side_effects=True, vmem_limit_bytes=60 << 20
    )


def cost(micros):
    return pl.CostEstimate(flops=0, transcendentals=0, bytes_accessed=int(micros * 3.0e6))


def team_gather(collective_id, *values):
    owners, cores = lax.axis_size("ctx"), lax.axis_size("tensor")
    amount = len(values)
    outs = pl.pallas_call(
        functools.partial(gather_kernel, amount, owners, cores),
        out_shape=[jax.ShapeDtypeStruct((owners, cores, *v.shape), v.dtype) for v in values],
        in_specs=[INSIDE] * amount,
        out_specs=[ANY] * amount,
        scratch_shapes=gather_sems(amount, owners),
        compiler_params=params(collective_id),
        cost_estimate=cost(20 * amount),
        name="team_gather",
    )(*values)
    return [o.reshape(-1, v.shape[1]) for o, v in zip(outs, values)]


def plane(index, shards_in):
    across_x = index + 1 - 2 * lax.rem(index, 2)
    return across_x, lax.rem(index + 2, shards_in), lax.rem(across_x + 2, shards_in)


def open_kernel(shards_in, owners, cores, *refs):
    value, w_query, w_key, w_value, w_output, w_gate, w_up, w_down, note = refs[:9]
    out, qkv, out_w, packed, notes = refs[9:14]
    own_sem, sent_w, came_w, passed_w, sent_n, came_n, pack_sem, load_sem = refs[14:22]
    stage, stage_out, stage_pack = refs[22:25]
    sems = refs[25:]
    index = lax.axis_index("shard")
    here = lax.axis_index("ctx")
    depth = w_query.shape[0]
    count = w_query.shape[1] // owners
    columns = pl.ds(pl.multiple_of(here * count, count), count)
    stored = [w.at[:, columns] for w in (w_query, w_key, w_value)] + [w_output.at[columns, :]]
    sources = [stage.at[0], stage.at[1], stage.at[2], stage_out]
    for k, (slow, source) in enumerate(zip(stored, sources)):
        pltpu.make_async_copy(slow, source, load_sem.at[k]).start()

    def target(weight, block):
        if weight == 3:
            wide = w_output.shape[1]
            return out_w.at[:, pl.ds(pl.multiple_of(block * wide, wide), wide)]
        rows = pl.ds(pl.multiple_of(block * depth, depth), depth)
        return qkv.at[rows, pl.ds(weight * count, count)]

    others = [lax.rem(index + step, shards_in) for step in range(1, shards_in)]
    greet(around("shard", shards_in) + around("ctx", owners) + around("tensor", cores))
    units = w_gate.shape[1] // owners
    hidden = pl.ds(pl.multiple_of(here * units, units), units)
    wide_down = w_down.shape[1]
    pieces = [
        (w_gate.at[:, hidden], stage_pack.at[:, pl.ds(0, units)]),
        (w_up.at[:, hidden], stage_pack.at[:, pl.ds(units, units)]),
    ]
    for k in range(units // depth):
        start = pl.multiple_of(here * units + k * depth, depth)
        place = pl.ds(2 * units + k * wide_down, wide_down)
        pieces.append((w_down.at[pl.ds(start, depth), :], stage_pack.at[:, place]))
    for k, (source, place) in enumerate(pieces):
        pltpu.make_async_copy(source, place, pack_sem.at[k]).start()
    notes[here] = note[...]
    fellows = [lax.rem(here + step, owners) for step in range(1, owners)]
    for fellow in fellows:
        send(note, notes.at[here], sent_n.at[fellow], came_n.at[here], {"ctx": fellow})
    square = shards_in == 4
    near = plane(index, shards_in)[:2] if square else others
    for weight in range(4):
        pltpu.make_async_copy(stored[weight], sources[weight], load_sem.at[weight]).wait()
        for other in near:
            send(
                sources[weight],
                target(weight, index),
                sent_w.at[weight, other],
                came_w.at[weight, index],
                {"shard": other},
            )
    gather_first([value], [out], sems, owners, cores)
    for weight in range(4):
        pltpu.make_async_copy(
            sources[weight], target(weight, index), own_sem.at[weight]
        ).start()
    for k, (source, place) in enumerate(pieces):
        pltpu.make_async_copy(source, place, pack_sem.at[k]).wait()
    pltpu.make_async_copy(stage_pack, packed, load_sem.at[4]).start()
    if square:
        across_x, across_y, far = plane(index, shards_in)
        for weight, source, device in (
            (0, across_x, across_y),
            (2, across_y, across_x),
            (1, across_x, across_y),
            (3, across_y, across_x),
        ):
            held = target(weight, source)
            landed(held, came_w.at[weight, source])
            send(
                held, held, passed_w.at[weight], came_w.at[weight, source], {"shard": device}
            )
    gather_rest([value], [out], sems, owners, cores)
    for fellow in fellows:
        landed(notes.at[fellow], came_n.at[fellow])
        landed(note, sent_n.at[fellow])
    pltpu.make_async_copy(stage_pack, packed, load_sem.at[4]).wait()
    for weight in range(4):
        pltpu.make_async_copy(
            sources[weight], target(weight, index), own_sem.at[weight]
        ).wait()
        for other in near:
            landed(sources[weight], sent_w.at[weight, other])
    if square:
        for weight, source in ((0, across_y), (2, across_x), (1, across_y), (3, across_x)):
            landed(target(weight, source), came_w.at[weight, source])
        for weight in range(4):
            landed(target(weight, far), came_w.at[weight, far])
            landed(sources[weight], passed_w.at[weight])
    else:
        for weight in range(4):
            for other in others:
                landed(target(weight, other), came_w.at[weight, other])


def open_team(collective_id, value, weights, note):
    shards_in, owners, cores = [lax.axis_size(a) for a in ("shard", "ctx", "tensor")]
    depth = weights[0].shape[0]
    count = weights[0].shape[1] // owners
    units = weights[4].shape[1] // owners
    pieces = 2 + units // depth
    out, qkv, out_w, packed, notes = pl.pallas_call(
        functools.partial(open_kernel, shards_in, owners, cores),
        out_shape=[
            jax.ShapeDtypeStruct((owners, cores, *value.shape), value.dtype),
            jax.ShapeDtypeStruct((shards_in * depth, 3 * count), value.dtype),
            jax.ShapeDtypeStruct((count, shards_in * weights[3].shape[1]), value.dtype),
            jax.ShapeDtypeStruct((depth, 3 * units), value.dtype),
            jax.ShapeDtypeStruct((owners, *note.shape), note.dtype),
        ],
        in_specs=[INSIDE] + [FAR] * 7 + [INSIDE],
        out_specs=[ANY] * 3 + [FAR] + [INSIDE],
        scratch_shapes=[
            pltpu.SemaphoreType.DMA((4,)),
            pltpu.SemaphoreType.DMA((4, shards_in)),
            pltpu.SemaphoreType.DMA((4, shards_in)),
            pltpu.SemaphoreType.DMA((4,)),
            pltpu.SemaphoreType.DMA((owners,)),
            pltpu.SemaphoreType.DMA((owners,)),
            pltpu.SemaphoreType.DMA((pieces,)),
            pltpu.SemaphoreType.DMA((5,)),
            pltpu.VMEM((3, depth, count), value.dtype),
            pltpu.VMEM((count, weights[3].shape[1]), value.dtype),
            pltpu.VMEM((depth, 3 * units), value.dtype),
        ]
        + gather_sems(1, owners),
        compiler_params=params(collective_id),
        cost_estimate=cost(40),
        name="open_team",
    )(value, *weights, note)
    return out.reshape(-1, value.shape[1]), qkv, out_w, packed, notes


def scatter_kernel(amount, owners, cores, *refs):
    parts, outs, refs = refs[:amount], refs[amount : 2 * amount], refs[2 * amount :]
    greet(line_partners(owners, cores))
    scatter(amount, owners, cores, parts, outs, refs)


def scatter(amount, owners, cores, parts, outs, refs):
    pairs, halves, from_left, from_right, own = [
        refs[k * amount : (k + 1) * amount] for k in range(5)
    ]
    total, sent_pair, came_pair, sent, came_left, came_right, load = refs[5 * amount :]
    here, core, pair, right, left = ring(owners, cores)
    order = [k // 2 if k % 2 else owners - 1 - k // 2 for k in range(owners)]
    for i in range(amount):
        for block in order:
            pltpu.make_async_copy(
                parts[i].at[block, core], own[i].at[block], load.at[i, block]
            ).start()
            send(
                parts[i].at[block, pair],
                pairs[i].at[block],
                sent_pair.at[i, block],
                came_pair.at[i, block],
                {"tensor": pair},
            )

    def add_up(i, block, more, arrived, came):
        landed(pairs[i].at[block], came_pair.at[i, block])
        landed(own[i].at[block], load.at[i, block])
        total[...] = own[i][block].astype(jnp.float32) + pairs[i][block].astype(jnp.float32)

        @pl.when(more)
        def _():
            landed(arrived[i].at[block], came.at[i, block])
            total[...] += arrived[i][block].astype(jnp.float32)

    def pass_on(i, block, more, arrived, came, device):
        add_up(i, block, more, arrived, came)
        halves[i][block] = total[...].astype(halves[i].dtype)
        send(
            halves[i].at[block],
            arrived[i].at[block],
            sent.at[i, block],
            came.at[i, block],
            {"ctx": device},
        )

    for step in range(2 * owners - 2):
        for i in range(amount):
            rightward = owners - 1 - (step - here)
            leftward = step - (owners - 1 - here)

            @pl.when((rightward > here) & (step >= here))
            def _():
                pass_on(i, rightward, here > 0, from_left, came_left, right)

            @pl.when((leftward >= 0) & (leftward < here))
            def _():
                pass_on(i, leftward, here < owners - 1, from_right, came_right, left)

    for i in range(amount):
        add_up(i, here, here > 0, from_left, came_left)

        @pl.when(here < owners - 1)
        def _():
            landed(from_right[i].at[here], came_right.at[i, here])
            total[...] += from_right[i][here].astype(jnp.float32)

        outs[i][...] = total[...]
    for i in range(amount):
        for block in range(owners):
            landed(pairs[i].at[block], sent_pair.at[i, block])

            @pl.when(block != here)
            def _():
                landed(halves[i].at[block], sent.at[i, block])


def scatter_scratch(amount, owners, block, kind):
    held = [pltpu.VMEM((owners, *block), kind)] * amount
    sems = [pltpu.SemaphoreType.DMA((amount, owners)) for _ in range(6)]
    return held * 5 + [pltpu.VMEM(block, jnp.float32)] + sems


def team_sum(collective_id, *values):
    owners, cores = lax.axis_size("ctx"), lax.axis_size("tensor")
    amount = len(values)
    width = values[0].shape[1]
    mine = values[0].shape[0] // (owners * cores)
    return pl.pallas_call(
        functools.partial(scatter_kernel, amount, owners, cores),
        out_shape=[jax.ShapeDtypeStruct((mine, width), jnp.float32)] * amount,
        in_specs=[ANY] * amount,
        out_specs=[INSIDE] * amount,
        scratch_shapes=scatter_scratch(amount, owners, (mine, width), values[0].dtype),
        compiler_params=params(collective_id),
        cost_estimate=cost(20 * amount),
        name="team_sum",
    )(*[v.reshape(owners, cores, mine, width) for v in values])


def swap_first(summed, held, local, sent, came, owners):
    here = lax.axis_index("ctx")
    count = summed.shape[0] // owners

    def rows(owner):
        return summed.at[pl.ds(pl.multiple_of(owner * count, count), count), :]

    for step in range(1, owners):
        other = lax.rem(here + step, owners)
        send(rows(other), held.at[here], sent.at[other], came.at[here], {"ctx": other})
    pltpu.make_async_copy(rows(here), held.at[here], local).start()


def put_rows(rows, outs, block, half, halves):
    amount = len(outs)
    units = rows.shape[1] // amount
    for j in range(units // block):
        start = half * units + j * block
        for i, out in enumerate(outs):
            first = (j * amount + i) * block
            piece = rows[:, first : first + block].astype(jnp.float32)
            if i < amount - 1:
                out[:, start : start + block] = piece
            else:
                out[start : start + block, :] = piece.T


def place_kernel(block, where, own_a, far_a, own_b, far_b, early, late, attn, *outs):
    core = where[0]
    for own, far, out in ((own_a, far_a, outs[0]), (own_b, far_b, outs[1])):
        out[0, core] = own[0]
        out[0, out.shape[1] - 1 - core] = far[0]
    put_rows(early[0], outs[2:5], block, 0, 2)
    put_rows(late[0], outs[2:5], block, 1, 2)
    put_rows(attn[0], outs[5:], outs[5].shape[1], 0, 1)


def place_all(streams, early, late, attn):
    owners, cores = lax.axis_size("ctx"), lax.axis_size("tensor")
    run = streams[0].shape
    block = late.shape[2] // (3 * BLOCKS // 2)

    def lead(shape):
        return pl.BlockSpec((1, *shape[1:]), lambda c, _: (c,) + (0,) * (len(shape) - 1))

    both = (run[0], cores, *run[1:])
    specs, shapes = [lead(both)] * 2, [jax.ShapeDtypeStruct(both, streams[0].dtype)] * 2
    for amount, units in ((3, 2 * late.shape[2] // 3), (4, attn.shape[2] // 4)):
        count = late.shape[1]
        specs += [pl.BlockSpec((count, units), lambda c, _: (0, c))] * (amount - 1)
        specs.append(pl.BlockSpec((units, count), lambda c, _: (c, 0)))
        wide = jax.ShapeDtypeStruct((count, owners * units), jnp.float32)
        shapes += [wide] * (amount - 1)
        shapes.append(jax.ShapeDtypeStruct((owners * units, count), jnp.float32))
    return pl.pallas_call(
        functools.partial(place_kernel, block),
        grid_spec=pltpu.PrefetchScalarGridSpec(
            num_scalar_prefetch=1,
            grid=(owners,),
            in_specs=[lead(v.shape) for v in (*streams, early, late, attn)],
            out_specs=specs,
        ),
        out_shape=shapes,
        compiler_params=pltpu.CompilerParams(
            dimension_semantics=("arbitrary",), vmem_limit_bytes=60 << 20
        ),
        cost_estimate=cost(7),
        name="place_all",
    )(lax.axis_index("tensor")[None].astype(jnp.int32), *streams, early, late, attn)


def swap_rest(summed, held, local, sent, came, owners):
    here = lax.axis_index("ctx")
    count = summed.shape[0] // owners
    own = summed.at[pl.ds(pl.multiple_of(here * count, count), count), :]
    for step in range(owners):
        source = lax.rem(here + owners - step, owners)
        if step == 0:
            pltpu.make_async_copy(own, held.at[here], local).wait()
        else:
            landed(held.at[source], came.at[source])
    for step in range(1, owners):
        other = lax.rem(here + step, owners)
        landed(held.at[other], sent.at[other])


def held_shape(summed, owners):
    return (owners, summed.shape[0] // owners, summed.shape[1])


def swap_sems(owners):
    return [
        pltpu.SemaphoreType.DMA,
        pltpu.SemaphoreType.DMA((owners,)),
        pltpu.SemaphoreType.DMA((owners,)),
    ]


def around(axis, size):
    index = lax.axis_index(axis)
    return [{axis: lax.rem(index + step, size)} for step in range(1, size)]


def swap_kernel_alone(owners, summed, held, *sems):
    greet(around("ctx", owners))
    swap_first(summed, held, *sems, owners)
    swap_rest(summed, held, *sems, owners)


def team_rows(collective_id, summed):
    owners = lax.axis_size("ctx")
    return pl.pallas_call(
        functools.partial(swap_kernel_alone, owners),
        out_shape=jax.ShapeDtypeStruct(held_shape(summed, owners), summed.dtype),
        in_specs=[INSIDE],
        out_specs=ANY,
        scratch_shapes=swap_sems(owners),
        compiler_params=params(collective_id),
        cost_estimate=cost(20),
        name="team_rows",
    )(summed)


def close_kernel(amount, shards_in, owners, cores, *refs):
    values, mixed, grads = refs[:amount], refs[amount], refs[amount + 1]
    refs = refs[amount + 2 :]
    outs, mix_out, late = refs[:amount], refs[amount], refs[amount + 1]
    summed, refs = refs[amount + 2], refs[amount + 3 :]
    pairs, half, quarters, blocks, sent, came = refs[:6]
    sent_c, came_c, sent_s, came_s, sent_b, came_b = refs[6:12]
    swap = refs[12:]
    here, core, pair, right, left = ring(owners, cores)
    index = lax.axis_index("shard")
    near = [lax.rem(here + step, owners) for step in range(1, owners)]
    others = [lax.rem(index + step, shards_in) for step in range(1, shards_in)]
    greet([{"tensor": pair}] + around("ctx", owners) + around("shard", shards_in))
    wide = mixed.shape[1] // cores
    thin = wide // owners
    send(
        mixed.at[:, pl.ds(pl.multiple_of(pair * wide, wide), wide)],
        pairs,
        sent.at[amount],
        came.at[amount],
        {"tensor": pair},
    )
    for i in range(amount):
        send(values[i], outs[i], sent.at[i], came.at[i], {"tensor": pair})
    landed(pairs, came.at[amount])
    half[...] = mixed[:, pl.ds(pl.multiple_of(core * wide, wide), wide)] + pairs[...]
    for other in near:
        send(
            half.at[:, pl.ds(pl.multiple_of(other * thin, thin), thin)],
            quarters.at[here],
            sent_c.at[other],
            came_c.at[here],
            {"ctx": other},
        )
    swap_first(grads, late, *swap, owners)
    total = half[:, pl.ds(pl.multiple_of(here * thin, thin), thin)]
    for other in near:
        landed(quarters.at[other], came_c.at[other])
        total += quarters[other]
    blocks[index] = total
    for other in others:
        send(
            blocks.at[index], blocks.at[index], sent_s.at[other], came_s.at[index], {"shard": other}
        )
    for other in others:
        landed(blocks.at[other], came_s.at[other])
    total = blocks[0]
    for block in range(1, shards_in):
        total += blocks[block]

    def place(owner, half_of):
        return summed.at[half_of * owners + owner]

    summed[core * owners + here] = total
    for other in near:
        send(place(here, core), place(here, core), sent_b.at[other], came_b.at[here, core], {"ctx": other})
    send(place(here, core), place(here, core), sent_b.at[here], came_b.at[here, core], {"tensor": pair})
    for other in near:
        landed(place(other, core), came_b.at[other, core])
        send(
            place(other, core),
            place(other, core),
            sent_b.at[owners + other],
            came_b.at[other, core],
            {"tensor": pair},
        )
    for owner in range(owners):
        landed(place(owner, pair), came_b.at[owner, pair])
        landed(place(owner, core), sent_b.at[owner])
    for owner in range(owners):
        for half_of in range(cores):
            found = summed[half_of * owners + owner]
            start = (half_of * owners + owner) * thin
            for row in range(mix_out.shape[0] * mix_out.shape[1]):
                k, h = row // mix_out.shape[1], row % mix_out.shape[1]
                mix_out[k, h : h + 1, start : start + thin] = found[row : row + 1, :]
    for other in near:
        landed(place(other, core), sent_b.at[owners + other])
        landed(quarters.at[other], sent_c.at[other])
    for other in others:
        landed(blocks.at[other], sent_s.at[other])
    landed(pairs, sent.at[amount])
    swap_rest(grads, late, *swap, owners)
    for i in range(amount):
        landed(outs[i], came.at[i])
        landed(values[i], sent.at[i])


def close_team(collective_id, grads, mixed, *values):
    shards_in, owners, cores = [lax.axis_size(a) for a in ("shard", "ctx", "tensor")]
    amount = len(values)
    height, width = mixed.shape
    thin = width // (cores * owners)
    out = pl.pallas_call(
        functools.partial(close_kernel, amount, shards_in, owners, cores),
        out_shape=[
            jax.ShapeDtypeStruct(v.shape, v.dtype) for v in values
        ]
        + [jax.ShapeDtypeStruct((height // 2, 2, width), jnp.float32)]
        + [jax.ShapeDtypeStruct(held_shape(grads, owners), grads.dtype)],
        in_specs=[INSIDE] * (amount + 2),
        out_specs=[ANY] * amount + [INSIDE, ANY],
        scratch_shapes=[
            pltpu.VMEM((cores * owners, height, thin), jnp.float32),
            pltpu.VMEM((height, width // cores), jnp.float32),
            pltpu.VMEM((height, width // cores), jnp.float32),
            pltpu.VMEM((owners, height, thin), jnp.float32),
            pltpu.VMEM((shards_in, height, thin), jnp.float32),
            pltpu.SemaphoreType.DMA((amount + 1,)),
            pltpu.SemaphoreType.DMA((amount + 1,)),
            pltpu.SemaphoreType.DMA((owners,)),
            pltpu.SemaphoreType.DMA((owners,)),
            pltpu.SemaphoreType.DMA((shards_in,)),
            pltpu.SemaphoreType.DMA((shards_in,)),
            pltpu.SemaphoreType.DMA((2 * owners,)),
            pltpu.SemaphoreType.DMA((owners, cores)),
        ]
        + swap_sems(owners),
        compiler_params=params(collective_id),
        cost_estimate=cost(60),
        name="close_team",
    )(*values, mixed, grads)
    return out[amount], out[:amount], out[amount + 1]


def ffn_kernel(
    u_ref,
    dy_ref,
    gate_ref,
    up_ref,
    down_ref,
    y_ref,
    du_ref,
    early_ref,
    late_ref,
    y_sum,
    du_sum,
    u_t,
    dy_t,
):
    step = pl.program_id(0)
    early = step < pl.num_programs(0) // 2
    total, width = u_ref.shape
    block = gate_ref.shape[1]
    tile = down_ref.shape[2]

    @pl.when(step == 0)
    def _():
        y_sum[...] = jnp.zeros_like(y_sum)
        du_sum[...] = jnp.zeros_like(du_sum)
        for start in range(0, width, tile):
            u_t[start : start + tile, :] = u_ref[:, start : start + tile].T
            dy_t[start : start + tile, :] = dy_ref[:, start : start + tile].T

    gate = dot(u_ref[...], gate_ref[...])
    upward = dot(u_ref[...], up_ref[...])
    shards_in = down_ref.shape[0]
    grad_hidden = 0.0
    for k in range(shards_in):
        grad_hidden = grad_hidden + contract_cols(
            dy_ref[:, k * tile : (k + 1) * tile], down_ref[k]
        )
    sigma = jax.nn.sigmoid(gate)
    swish = gate * sigma
    hidden = (swish * upward).astype(jnp.bfloat16)
    grad_gate = (grad_hidden * upward * (sigma + swish * (1.0 - sigma))).astype(jnp.bfloat16)
    grad_up = (grad_hidden * swish).astype(jnp.bfloat16)
    for k in range(shards_in):
        span = slice(k * tile, (k + 1) * tile)
        y_sum[:, span] += dot(hidden, down_ref[k])
        du_sum[:, span] += contract_cols(grad_gate, gate_ref[span, :]) + contract_cols(
            grad_up, up_ref[span, :]
        )

    def weights_back(grad_ref):
        for start in range(0, width, tile):
            span = slice(start, start + tile)
            grad_ref[span, :block] = dot(u_t[span, :], grad_gate).astype(jnp.bfloat16)
            grad_ref[span, block : 2 * block] = dot(u_t[span, :], grad_up).astype(jnp.bfloat16)
            grad_ref[span, 2 * block :] = dot(dy_t[span, :], hidden).astype(jnp.bfloat16)

    @pl.when(early)
    def _():
        weights_back(early_ref)

    @pl.when(jnp.logical_not(early))
    def _():
        weights_back(late_ref)

    @pl.when(step == pl.num_programs(0) - 1)
    def _():
        y_ref[...] = y_sum[...].astype(jnp.bfloat16)
        du_ref[...] = du_sum[...].astype(jnp.bfloat16)


def ffn(u, dy, weights):
    total, width = u.shape
    shards_in = lax.axis_size("shard")
    depth = width // shards_in
    units = weights.shape[1] // 3
    blocks = BLOCKS
    block = units // blocks
    half = blocks // 2
    whole = pl.BlockSpec((total, width), lambda j: (0, 0), pipeline_mode=pl.Buffered(1))
    low = functools.partial(jax.ShapeDtypeStruct, dtype=jnp.bfloat16)
    return pl.pallas_call(
        ffn_kernel,
        grid=(blocks,),
        in_specs=[
            whole,
            whole,
            pl.BlockSpec((width, block), lambda j: (0, j)),
            pl.BlockSpec((width, block), lambda j: (0, blocks + j)),
            pl.BlockSpec(
                (shards_in, block, depth),
                lambda j: (0, j % (depth // block), 2 * units // depth + j // (depth // block)),
            ),
        ],
        out_specs=[
            whole,
            whole,
            pl.BlockSpec((width, 3 * block), lambda j: (0, jnp.minimum(j, half - 1))),
            pl.BlockSpec((width, 3 * block), lambda j: (0, jnp.maximum(j - half, 0))),
        ],
        out_shape=[low((total, width))] * 2 + [low((width, 3 * units // 2))] * 2,
        scratch_shapes=[
            pltpu.VMEM((total, width), jnp.float32),
            pltpu.VMEM((total, width), jnp.float32),
            pltpu.VMEM((width, total), jnp.bfloat16),
            pltpu.VMEM((width, total), jnp.bfloat16),
        ],
        compiler_params=pltpu.CompilerParams(
            dimension_semantics=("arbitrary",), vmem_limit_bytes=60 << 20
        ),
        cost_estimate=cost(30),
        name="ffn",
    )(u, dy, weights, weights, weights.reshape(shards_in, depth, 3 * units))


def pack_kernel(sent, value, out):
    for i in range(value.shape[1]):
        out[0, i] = value[:, i, :]


def pack_runs(value, sent, part):
    rows_in, total, width = value.shape
    return pl.pallas_call(
        pack_kernel,
        grid_spec=pltpu.PrefetchScalarGridSpec(
            num_scalar_prefetch=1,
            grid=(sent.shape[0],),
            in_specs=[
                pl.BlockSpec((part, total, width), lambda c, first: (first[c], 0, 0)),
            ],
            out_specs=pl.BlockSpec((1, total, part, width), lambda c, first: (c, 0, 0, 0)),
        ),
        out_shape=jax.ShapeDtypeStruct((sent.shape[0], total, part, width), value.dtype),
        compiler_params=pltpu.CompilerParams(dimension_semantics=("arbitrary",)),
        cost_estimate=cost(2),
        name="pack_runs",
    )(sent, value)


def head_probs(query, key, placing, placed):
    scores = contract_cols(query, key) * HD ** (-0.5)
    allowed = (placed >= placing[:, 0:1]) & (placed <= placing[:, 1:2])
    scores = jnp.where(allowed, scores, FLOOR_SCORE)
    probs = jnp.exp(scores - jnp.max(scores, -1, keepdims=True))
    return probs / jnp.sum(probs, -1, keepdims=True)


def turn(value, turns, back):
    swung = pltpu.roll(value, HD // 2, 1) * turns[1]
    return value * turns[0] - swung if back else value * turns[0] + swung


def attend_kernel(
    u_ref, qkv_ref, out_ref, turns, placing, placed, y_ref, q_ref, k_ref, v_ref, o_ref
):
    count = q_ref.shape[1]
    u = u_ref[...]
    for first in range(0, count, HD):
        head = slice(first, first + HD)

        def lin(which):
            start = which * count + first
            return dot(u, qkv_ref[:, start : start + HD])

        query = turn(lin(0), turns, False).astype(jnp.bfloat16)
        key = turn(lin(1), turns, False).astype(jnp.bfloat16)
        value = lin(2).astype(jnp.bfloat16)
        q_ref[:, head] = query
        k_ref[:, head] = key
        v_ref[:, head] = value
        probs = head_probs(query, key, placing[...], placed[...])
        o_ref[:, head] = dot(probs.astype(jnp.bfloat16), value).astype(jnp.bfloat16)
    width = y_ref.shape[1]
    for start in range(0, width, 512):
        y_ref[:, start : start + 512] = dot(o_ref[...], out_ref[:, start : start + 512])


def attend(u, qkv, out_w, turns, placing, placed):
    total, count = u.shape[0], out_w.shape[0]
    low = jax.ShapeDtypeStruct((total, count), jnp.bfloat16)
    return pl.pallas_call(
        attend_kernel,
        out_shape=[jax.ShapeDtypeStruct((total, out_w.shape[1]), jnp.float32)] + [low] * 4,
        in_specs=[INSIDE] * 6,
        out_specs=[INSIDE] * 5,
        compiler_params=pltpu.CompilerParams(vmem_limit_bytes=60 << 20),
        cost_estimate=cost(12),
        name="attend",
    )(u, qkv, out_w, turns, placing, placed)


def attend_back_kernel(
    owners,
    cores,
    dy_ref,
    u_ref,
    qkv_ref,
    out_ref,
    q_ref,
    k_ref,
    v_ref,
    o_ref,
    turns,
    placing,
    placed,
    summed,
    grad_ref,
    sum_ref,
    rows,
    lin,
    du_ref,
    *refs,
):
    greet(around("ctx", owners) + around("tensor", cores))
    swap, refs = refs[:3], refs[3:]
    swap_first(summed, rows, *swap, owners)
    count = q_ref.shape[1]
    width = dy_ref.shape[1]
    scale = HD ** (-0.5)
    low = jnp.bfloat16
    for first in range(0, count, HD):
        head = slice(first, first + HD)
        query, key, value = q_ref[:, head], k_ref[:, head], v_ref[:, head]
        grad_out = contract_cols(dy_ref[...], out_ref[head, :]).astype(low)
        probs = head_probs(query, key, placing[...], placed[...])
        grad_probs = contract_cols(grad_out, value)
        delta = jnp.sum(probs * grad_probs, -1, keepdims=True)
        grad_scores = (probs * (grad_probs - delta)).astype(low)
        grad_query = turn(dot(grad_scores, key) * scale, turns, True)
        grad_key = turn(contract_rows(grad_scores, query) * scale, turns, True)
        grad_value = contract_rows(probs.astype(low), grad_out)
        for which, grad in enumerate((grad_query, grad_key, grad_value)):
            start = which * count + first
            lin[:, start : start + HD] = grad.astype(low)
    tile = min(512, width)
    edge = lin.shape[1]
    for start in range(0, width, tile):
        span = slice(start, start + tile)
        du_part = contract_cols(lin[...], qkv_ref[span, :]).astype(low)
        du_ref[:, :, :, span] = du_part.reshape(*du_ref.shape[:3], tile)
    for start in range(0, width, tile):
        span = slice(start, start + tile)
        grad_ref[span, :edge] = dot(u_ref[:, span].T, lin[...]).astype(low)
        grad_ref[span, edge:] = dot(dy_ref[:, span].T, o_ref[...]).astype(low)
    scatter(1, owners, cores, [du_ref], [sum_ref], refs)
    swap_rest(summed, rows, *swap, owners)


def attend_back(collective_id, dy, u, qkv, out_w, q, k, v, o, turns, placing, placed, summed):
    owners, cores = lax.axis_size("ctx"), lax.axis_size("tensor")
    total, width = u.shape
    count = q.shape[1]
    mine = total // (owners * cores)
    return pl.pallas_call(
        functools.partial(attend_back_kernel, owners, cores),
        out_shape=[
            jax.ShapeDtypeStruct((width, 4 * count), jnp.bfloat16),
            jax.ShapeDtypeStruct((mine, width), jnp.float32),
            jax.ShapeDtypeStruct(held_shape(summed, owners), summed.dtype),
        ],
        in_specs=[INSIDE] * 11 + [ANY],
        out_specs=[INSIDE] * 2 + [ANY],
        scratch_shapes=[
            pltpu.VMEM((total, 3 * count), jnp.bfloat16),
            pltpu.VMEM((owners, cores, mine, width), jnp.bfloat16),
        ]
        + swap_sems(owners)
        + scatter_scratch(1, owners, (mine, width), jnp.bfloat16),
        compiler_params=params(collective_id),
        cost_estimate=cost(50),
        name="attend_back",
    )(dy, u, qkv, out_w, q, k, v, o, turns, placing, placed, summed)


EXACT = functools.partial(
    lax.dot_general, precision=PRECISE, preferred_element_type=jnp.float32
)


def columns_of(pieces):
    rows_in = pieces[0].shape[0]
    lane = lax.broadcasted_iota(jnp.int32, (rows_in, 8), 1)
    out = jnp.zeros((rows_in, 8), jnp.float32)
    for k, piece in enumerate(pieces):
        out = jnp.where(lane == k, piece, out)
    return out


def tables_of(current, weight, static, table_ref, active_ref):
    branch_in = 0.0
    tables = []
    for i, stream in enumerate(current):
        normed, scaled = norm_rows(stream)
        active = jnp.tanh(EXACT(normed, weight, (((1,), (1,)), ((), ()))))
        table = active + static[i : i + 1, :]
        table_ref[i] = table
        active_ref[i] = active
        tables.append(table)
        branch_in = branch_in + table[:, 0:1] * stream
    return tables, branch_in


def norm_plain(value):
    centred = value - jnp.mean(value, -1, keepdims=True)
    scaled = lax.rsqrt(jnp.mean(centred * centred, -1, keepdims=True) + EPSILON)
    return (centred * scaled, scaled)


def mix_first(current, weight, static):
    normed, _ = norm_plain(current)
    active = jnp.tanh(jnp.einsum("tsd,dk->tsk", normed, weight, precision=PRECISE))
    table = active + static
    total = current.shape[1]
    branch_in = sum(table[:, i, 0][:, None] * current[:, i] for i in range(total))
    normed, scaled = norm_plain(branch_in)

    def by_stream(value):
        return jnp.pad(value.transpose(1, 0, 2), ((0, 0), (0, 0), (0, 8 - value.shape[2])))

    scaled = jnp.pad(scaled, ((0, 0), (0, 7)))
    return normed.astype(jnp.bfloat16), normed, scaled, by_stream(table), by_stream(active)


def mix_second_kernel(
    source,
    streams,
    branch_out,
    table_one,
    arrived,
    weight,
    static,
    middle_ref,
    low_ref,
    grad_low_ref,
    normed_ref,
    scaled_ref,
    table_ref,
    active_ref,
    top_ref,
):
    total = streams.shape[0]
    y = branch_out[...]
    first = [table_one[i] for i in range(total)]
    current = [streams[i].astype(jnp.float32) for i in range(total)]
    middle = []
    for j in range(total):
        mixed = first[j][:, total + 1 : total + 2] * y
        for i in range(total):
            mixed = mixed + first[i][:, 1 + j : 2 + j] * current[i]
        middle.append(mixed)
        middle_ref[j] = mixed
    tables, branch_in = tables_of(middle, weight[...], static[...], table_ref, active_ref)
    normed, scaled = norm_rows(branch_in)
    normed_ref[...] = normed
    low_ref[...] = normed.astype(jnp.bfloat16)
    scaled_ref[...] = columns_of([scaled])
    grad = 0.0
    for j in range(total):
        top = arrived[0, j]
        top_ref[j] = top
        grad = grad + tables[j][:, total + 1 : total + 2] * top.astype(jnp.float32)
    grad_low_ref[...] = grad.astype(jnp.bfloat16)


def connection_back(
    current, grad_top, branch_out, grad_in, normed_in, scaled_in, tables, actives, weight, sums
):
    total = len(current)
    weight_sum, static_sum = sums
    dx = scaled_in * (grad_in - mean_of(grad_in) - normed_in * mean_of(grad_in * normed_in))
    result = []
    for i, stream in enumerate(current):
        pieces = [jnp.sum(dx * stream, -1, keepdims=True)]
        pieces += [jnp.sum(stream * top, -1, keepdims=True) for top in grad_top]
        pieces.append(jnp.sum(grad_top[i] * branch_out, -1, keepdims=True))
        grad_table = columns_of(pieces)
        static_sum[i : i + 1, :] += jnp.sum(grad_table, 0, keepdims=True)
        grad_inner = grad_table * (1.0 - actives[i] * actives[i])
        normed, scaled = norm_rows(stream)
        weight_sum[...] += EXACT(grad_inner, normed, (((0,), (0,)), ((), ())))
        grad_normed = EXACT(grad_inner, weight, (((1,), (0,)), ((), ())))
        grad = tables[i][:, 0:1] * dx + norm_back(normed, scaled, grad_normed)
        for j in range(total):
            grad = grad + tables[i][:, 1 + j : 2 + j] * grad_top[j]
        result.append(grad)
    return result


def start_sums(sums):
    @pl.when(pl.program_id(0) == 0)
    def _():
        for ref in sums:
            ref[...] = jnp.zeros_like(ref)


def back_second_kernel(
    middle,
    top,
    branch_out,
    grad_in,
    normed_in,
    scaled_in,
    table,
    active,
    table_one,
    weight,
    final_ref,
    grad_ref,
    grad_low_ref,
    *sums,
):
    start_sums(sums)
    total = middle.shape[0]
    current = [middle[i] for i in range(total)]
    grad_top = [top[i].astype(jnp.float32) for i in range(total)]
    tables = [table[i] for i in range(total)]
    y = branch_out[...]
    for j in range(total):
        mixed = tables[j][:, total + 1 : total + 2] * y
        for i in range(total):
            mixed = mixed + tables[i][:, 1 + j : 2 + j] * current[i]
        final_ref[0, :, j, :] = mixed.astype(jnp.bfloat16)
    grads = connection_back(
        current,
        grad_top,
        y,
        grad_in[...],
        normed_in[...],
        scaled_in[:, 0:1],
        tables,
        [active[i] for i in range(total)],
        weight[...],
        sums,
    )
    low = 0.0
    for j in range(total):
        grad_ref[j] = grads[j]
        low = low + table_one[j][:, total + 1 : total + 2] * grads[j]
    grad_low_ref[...] = low.astype(jnp.bfloat16)


def back_first_kernel(
    streams,
    top,
    branch_out,
    grad_in,
    normed_in,
    scaled_in,
    table,
    active,
    weight,
    grad_ref,
    *sums,
):
    start_sums(sums)
    total = streams.shape[0]
    grads = connection_back(
        [streams[i].astype(jnp.float32) for i in range(total)],
        [top[i] for i in range(total)],
        branch_out[...],
        grad_in[...],
        normed_in[...],
        scaled_in[:, 0:1],
        [table[i] for i in range(total)],
        [active[i] for i in range(total)],
        weight[...],
        sums,
    )
    for j in range(total):
        grad_ref[0, :, j, :] = grads[j].astype(jnp.bfloat16)


def by_token(tile, shape, kind=jnp.float32):
    block = (*shape[:-2], tile, shape[-1])
    lead = (0,) * (len(shape) - 2)
    spec = pl.BlockSpec(block, lambda step, *_: (*lead, step, 0))
    return spec, jax.ShapeDtypeStruct(shape, kind)


def fixed(shape, kind=jnp.float32):
    spec = pl.BlockSpec(shape, lambda step, *_: (0,) * len(shape))
    return spec, jax.ShapeDtypeStruct(shape, kind)


def token_call(kernel, name, tile, ins, outs, prefetch=(), special=None):
    specs, values = [], []
    for value, tiled in ins:
        if tiled == "run":
            specs.append(special)
        else:
            specs.append(by_token(tile, value.shape)[0] if tiled else fixed(value.shape)[0])
        values.append(value)
    tokens = ins[0][0].shape[-2]
    return pl.pallas_call(
        kernel,
        grid_spec=pltpu.PrefetchScalarGridSpec(
            num_scalar_prefetch=len(prefetch),
            grid=(tokens // tile,),
            in_specs=specs,
            out_specs=[o[0] for o in outs],
        ),
        out_shape=[o[1] for o in outs],
        compiler_params=pltpu.CompilerParams(
            dimension_semantics=("arbitrary",), vmem_limit_bytes=60 << 20
        ),
        cost_estimate=cost(5),
        name=name,
    )(*prefetch, *values)


def shards(
    streams,
    lengths,
    destination,
    w_query,
    w_key,
    w_value,
    w_output,
    w_gate,
    w_up,
    w_down,
    mix_weight,
    mix_static,
    cotangent,
):
    rows_here, stream_total, width = streams.shape
    owners = lax.axis_size("ctx")
    cores = lax.axis_size("tensor")
    here = lax.axis_index("ctx")
    core = lax.axis_index("tensor")
    run_rows = rows_here // owners
    part = run_rows // cores
    mine = rows_here // cores
    group_rows = rows_here * owners
    head_cols = w_query.shape[1] // owners
    heads = head_cols // HD
    units = w_gate.shape[1] // owners
    scale = HD ** (-0.5)

    def columns(weight, count):
        return lax.dynamic_slice_in_dim(weight, here * count, count, 1)

    def rows(weight, count):
        return lax.dynamic_slice_in_dim(weight, here * count, count, 0)

    order = jnp.arange(group_rows, dtype=jnp.int32)
    within = order % mine
    placed = (
        order // rows_here * rows_here
        + within // part * run_rows
        + order % rows_here // mine * part
        + within % part
    )
    spans = lengths[0]
    count = jnp.arange(spans.shape[0], dtype=jnp.int32)
    starts = jnp.sum(jnp.where(count[None, :] < count[:, None], spans[None, :], 0), 1)
    begin = jnp.max(jnp.where(starts[None, :] <= placed[:, None], starts[None, :], 0), axis=1)
    cosine, sine = angles(placed - begin, HD)
    turns = jnp.stack(
        [jnp.concatenate([cosine, cosine], -1), jnp.concatenate([-sine, sine], -1)]
    ).reshape(2, group_rows, HD)
    placing = jnp.stack([begin, placed], 1)
    placed = placed[None]

    local_dest = destination - lax.axis_index("shard") * group_rows
    heads_of_runs = local_dest.reshape(owners, run_rows)[:, 0]
    came_from = heads_of_runs // rows_here
    note = jnp.broadcast_to(jnp.pad(heads_of_runs, (0, 128 - owners)), (8, 128))

    turned_weight = jnp.pad(mix_weight.transpose(0, 2, 1), ((0, 0), (0, 2), (0, 0)))
    static = jnp.pad(mix_static, ((0, 0), (0, 0), (0, 2)))
    split = streams.reshape(owners, cores, part, stream_total, width)
    current = lax.dynamic_index_in_dim(split, core, 1, keepdims=False)
    current = current.reshape(mine, stream_total, width)
    attn_low, attn_normed, attn_scaled, table_one, active_one = mix_first(
        current.astype(jnp.float32), mix_weight[0], mix_static[0]
    )
    current = current.transpose(1, 0, 2)
    low = jnp.bfloat16
    tile = min(16, part)
    small = by_token(tile, (stream_total, mine, 8))
    attn_input, qkv, out_w, packed, notes = open_team(
        0, attn_low, (w_query, w_key, w_value, w_output, w_gate, w_up, w_down), note
    )
    ffn_weights = lax.all_gather(packed, "shard", axis=0, tiled=True)
    every = notes[:, 0, :owners]
    sent = jnp.sum(jnp.where(every // rows_here == here, every % rows_here, 0), 1) // part + core
    packed = pack_runs(cotangent, sent, part)
    arrived = lax.all_to_all(packed, "ctx", split_axis=0, concat_axis=0, tiled=True)
    attn_part, queries, keys, values, attended = attend(
        attn_input, qkv, out_w, turns, placing, placed
    )
    [attn_out] = team_sum(1, attn_part)

    (
        middle,
        ffn_low,
        grad_ffn_low,
        ffn_normed,
        ffn_scaled,
        table_two,
        active_two,
        grad_top,
    ) = token_call(
        mix_second_kernel,
        "mix_second",
        tile,
        [
            (current, True),
            (attn_out, True),
            (table_one, True),
            (arrived, "run"),
            (turned_weight[1], False),
            (static[1], False),
        ],
        [
            by_token(tile, (stream_total, mine, width)),
            by_token(tile, (mine, width), low),
            by_token(tile, (mine, width), low),
            by_token(tile, (mine, width)),
            by_token(tile, (mine, 8)),
            small,
            small,
            by_token(tile, (stream_total, mine, width), low),
        ],
        (came_from,),
        pl.BlockSpec(
            (1, stream_total, tile, width),
            lambda step, source: (source[step * tile // part], 0, step % (part // tile), 0),
        ),
    )
    ffn_input, grad_ffn_out = team_gather(2, ffn_low, grad_ffn_low)
    ffn_part, ffn_input_part, *ffn_grads = ffn(ffn_input, grad_ffn_out, ffn_weights)

    def shard_sum(partial):
        return lax.psum_scatter(partial, "shard", scatter_dimension=0, tiled=True)

    early_sum, late_sum = [shard_sum(grads) for grads in ffn_grads]
    ffn_out, grad_ffn_input = team_sum(3, ffn_part, ffn_input_part)
    sums = [fixed((8, width)), fixed((stream_total, 8))]
    runs = (
        pl.BlockSpec(
            (1, tile, stream_total, width),
            lambda step, *_: (step * tile // part, step % (part // tile), 0, 0),
        ),
        jax.ShapeDtypeStruct((owners, part, stream_total, width), low),
    )
    final, grad_middle, grad_attn_low, weight_two, static_two = token_call(
        back_second_kernel,
        "back_second",
        tile,
        [
            (middle, True),
            (grad_top, True),
            (ffn_out, True),
            (grad_ffn_input, True),
            (ffn_normed, True),
            (ffn_scaled, True),
            (table_two, True),
            (active_two, True),
            (table_one, True),
            (turned_weight[1], False),
        ],
        [
            runs,
            by_token(tile, (stream_total, mine, width)),
            by_token(tile, (mine, width), low),
            *sums,
        ],
    )
    [grad_attn_out] = team_gather(4, grad_attn_low)

    attn_grads, grad_attn_input, early_rows = attend_back(
        5,
        grad_attn_out,
        attn_input,
        qkv,
        out_w,
        queries,
        keys,
        values,
        attended,
        turns,
        placing,
        placed,
        early_sum,
    )
    attn_sum = shard_sum(attn_grads)

    grad_current, weight_one, static_one = token_call(
        back_first_kernel,
        "back_first",
        tile,
        [
            (current, True),
            (grad_middle, True),
            (attn_out, True),
            (grad_attn_input, True),
            (attn_normed, True),
            (attn_scaled, True),
            (table_one, True),
            (active_one, True),
            (turned_weight[0], False),
        ],
        [runs, *sums],
    )
    statics = jnp.stack([static_one, static_two]).reshape(1, -1)
    mixed = jnp.concatenate(
        [
            jnp.stack([weight_one, weight_two], 1).reshape(16, width),
            jnp.pad(statics, ((0, 7), (0, width - statics.size))),
        ],
        0,
    )

    mixed, (far_final, far_grad), late_rows = close_team(
        7, late_sum, mixed, final, grad_current
    )
    mixed, attn_sum = lax.optimization_barrier((mixed, attn_sum))
    (
        streams_out,
        grad_streams,
        grad_gate,
        grad_up,
        grad_down,
        grad_query,
        grad_key,
        grad_value,
        grad_output,
    ) = place_all(
        (final, far_final, grad_current, far_grad), early_rows, late_rows, team_rows(8, attn_sum)
    )
    columns_in = mix_weight.shape[2]
    grad_mix_weight = mixed[:columns_in].transpose(1, 2, 0)
    grad_mix_static = mixed[8, 0, : statics.size].reshape(2, stream_total, 8)[:, :, :columns_in]

    return (
        streams_out.reshape(rows_here, stream_total, width),
        grad_streams.reshape(rows_here, stream_total, width),
        grad_query,
        grad_key,
        grad_value,
        grad_output,
        grad_gate,
        grad_up,
        grad_down,
        grad_mix_weight,
        grad_mix_static,
    )


def solution(mesh):
    return jax.shard_map(
        shards,
        mesh=mesh,
        in_specs=(
            P(("shard", "ctx"), None, None),
            P("shard", None),
            P(("shard", "ctx")),
            P("shard", "tensor"),
            P("shard", "tensor"),
            P("shard", "tensor"),
            P("tensor", "shard"),
            P("shard", "tensor"),
            P("shard", "tensor"),
            P("tensor", "shard"),
            P(),
            P(),
            P(("shard", "ctx"), None, None),
        ),
        out_specs=(
            P(("shard", "ctx"), None, None),
            P(("shard", "ctx"), None, None),
            P(("shard", "ctx"), "tensor"),
            P(("shard", "ctx"), "tensor"),
            P(("shard", "ctx"), "tensor"),
            P("tensor", ("shard", "ctx")),
            P(("shard", "ctx"), "tensor"),
            P(("shard", "ctx"), "tensor"),
            P("tensor", ("shard", "ctx")),
            P(),
            P(),
        ),
        check_vma=False,
    )
```

```python
import functools

import jax
import jax.numpy as jnp
import numpy as np
from jax import lax
from jax.experimental import pallas as pl
from jax.experimental.pallas import tpu as pltpu
from jax.sharding import PartitionSpec as P

HD = 128


PRECISE = lax.Precision.HIGHEST
EPSILON = 1e-05
FLOOR_SCORE = -1e30
BLOCKS = 4


def mean_of(value):
    width = value.shape[-1]
    while value.shape[-1] > 128 and value.shape[-1] % 256 == 0:
        half = value.shape[-1] // 2
        value = value[..., :half] + value[..., half:]
    return jnp.sum(value, -1, keepdims=True) * (1.0 / width)


def norm_rows(value):
    centred = value - mean_of(value)
    scaled = lax.rsqrt(mean_of(centred * centred) + EPSILON)
    return (centred * scaled, scaled)


def norm_back(normed, scaled, grad):
    return scaled * (grad - mean_of(grad) - normed * mean_of(grad * normed))


def angles(positions, head_size):
    indices = np.arange(head_size // 2, dtype=np.float64)
    frequency = (10000.0 ** (-(2.0 * indices / head_size))).astype(np.float32)
    turned = positions.astype(jnp.float32)[:, None] * frequency[None, :]
    return (jnp.cos(turned)[:, None, :], jnp.sin(turned)[:, None, :])


def dot(left, right):
    return jnp.dot(left, right, preferred_element_type=jnp.float32)


def contract_rows(left, right):
    return lax.dot_general(
        left, right, (((0,), (0,)), ((), ())), preferred_element_type=jnp.float32
    )


def contract_cols(left, right):
    return lax.dot_general(
        left, right, (((1,), (1,)), ((), ())), preferred_element_type=jnp.float32
    )


def greet(partners):
    barrier = pltpu.get_barrier_semaphore()
    for partner in partners:
        pl.semaphore_signal(
            barrier, inc=1, device_id=partner, device_id_type=pl.DeviceIdType.MESH
        )
    pl.semaphore_wait(barrier, len(partners))


def send(source, target, sent, received, device):
    pltpu.make_async_remote_copy(
        src_ref=source,
        dst_ref=target,
        send_sem=sent,
        recv_sem=received,
        device_id=device,
        device_id_type=pl.DeviceIdType.MESH,
    ).start()


def landed(block, semaphore):
    pltpu.make_async_copy(block, block, semaphore).wait()


def ring(owners, cores):
    here = lax.axis_index("ctx")
    core = lax.axis_index("tensor")
    right, left = lax.rem(here + 1, owners), lax.rem(here + owners - 1, owners)
    return here, core, cores - 1 - core, right, left


def gather_first(values, outs, sems, owners, cores):
    local, sent_right, sent_left, sent_pair, came, came_pair = sems
    here, core, pair, right, left = ring(owners, cores)
    for i, (value, out) in enumerate(zip(values, outs)):
        target = out.at[here, core]

        @pl.when(here < owners - 1)
        def _():
            send(value, target, sent_right.at[i, here], came.at[i, here], {"ctx": right})

        @pl.when(here > 0)
        def _():
            send(value, target, sent_left.at[i, here], came.at[i, here], {"ctx": left})

        send(value, target, sent_pair.at[i, here], came_pair.at[i, here], {"tensor": pair})
        pltpu.make_async_copy(value, target, local.at[i]).start()


def gather_rest(values, outs, sems, owners, cores):
    local, sent_right, sent_left, sent_pair, came, came_pair = sems
    here, core, pair, right, left = ring(owners, cores)

    def arrive(i, out, block, onward, sent, device):
        held = out.at[block, core]
        landed(held, came.at[i, block])

        @pl.when(onward)
        def _():
            send(held, held, sent.at[i, block], came.at[i, block], device)

        send(held, held, sent_pair.at[i, block], came_pair.at[i, block], {"tensor": pair})

    for step in range(1, owners):
        for i, out in enumerate(outs):

            @pl.when(here >= step)
            def _():
                arrive(i, out, here - step, here < owners - 1, sent_right, {"ctx": right})

            @pl.when(here + step < owners)
            def _():
                arrive(i, out, here + step, here > 0, sent_left, {"ctx": left})

    for i, (value, out) in enumerate(zip(values, outs)):
        pltpu.make_async_copy(value, out.at[here, core], local.at[i]).wait()
        for block in range(owners):
            landed(out.at[block, pair], came_pair.at[i, block])
            landed(out.at[block, core], sent_pair.at[i, block])

            @pl.when((here < owners - 1) & (block <= here))
            def _():
                landed(out.at[block, core], sent_right.at[i, block])

            @pl.when((here > 0) & (block >= here))
            def _():
                landed(out.at[block, core], sent_left.at[i, block])


def gather_sems(amount, owners):
    return [pltpu.SemaphoreType.DMA((amount,))] + [
        pltpu.SemaphoreType.DMA((amount, owners)) for _ in range(5)
    ]


def line_partners(owners, cores):
    here, core, pair, right, left = ring(owners, cores)
    return [{"ctx": right}, {"ctx": left}, {"tensor": pair}]


def gather_kernel(amount, owners, cores, *refs):
    values, outs, sems = refs[:amount], refs[amount : 2 * amount], refs[2 * amount :]
    greet(line_partners(owners, cores))
    gather_first(values, outs, sems, owners, cores)
    gather_rest(values, outs, sems, owners, cores)


ANY = pl.BlockSpec(memory_space=pl.ANY)
FAR = pl.BlockSpec(memory_space=pltpu.HBM)
INSIDE = pl.BlockSpec(memory_space=pltpu.VMEM)


def params(collective_id):
    return pltpu.CompilerParams(
        collective_id=collective_id, has_side_effects=True, vmem_limit_bytes=60 << 20
    )


def cost(micros):
    return pl.CostEstimate(flops=0, transcendentals=0, bytes_accessed=int(micros * 3.0e6))


def team_gather(collective_id, *values):
    owners, cores = lax.axis_size("ctx"), lax.axis_size("tensor")
    amount = len(values)
    outs = pl.pallas_call(
        functools.partial(gather_kernel, amount, owners, cores),
        out_shape=[jax.ShapeDtypeStruct((owners, cores, *v.shape), v.dtype) for v in values],
        in_specs=[INSIDE] * amount,
        out_specs=[ANY] * amount,
        scratch_shapes=gather_sems(amount, owners),
        compiler_params=params(collective_id),
        cost_estimate=cost(20 * amount),
        name="team_gather",
    )(*values)
    return [o.reshape(-1, v.shape[1]) for o, v in zip(outs, values)]


def plane(index, shards_in):
    across_x = index + 1 - 2 * lax.rem(index, 2)
    return across_x, lax.rem(index + 2, shards_in), lax.rem(across_x + 2, shards_in)


def open_kernel(shards_in, owners, cores, *refs):
    value, w_query, w_key, w_value, w_output, w_gate, w_up, w_down, note = refs[:9]
    out, qkv, out_w, packed, notes = refs[9:14]
    own_sem, sent_w, came_w, passed_w, sent_n, came_n, pack_sem, load_sem = refs[14:22]
    stage, stage_out, stage_pack = refs[22:25]
    sems = refs[25:]
    index = lax.axis_index("shard")
    here = lax.axis_index("ctx")
    depth = w_query.shape[0]
    count = w_query.shape[1] // owners
    columns = pl.ds(pl.multiple_of(here * count, count), count)
    stored = [w.at[:, columns] for w in (w_query, w_key, w_value)] + [w_output.at[columns, :]]
    sources = [stage.at[0], stage.at[1], stage.at[2], stage_out]
    for k, (slow, source) in enumerate(zip(stored, sources)):
        pltpu.make_async_copy(slow, source, load_sem.at[k]).start()

    def target(weight, block):
        if weight == 3:
            wide = w_output.shape[1]
            return out_w.at[:, pl.ds(pl.multiple_of(block * wide, wide), wide)]
        rows = pl.ds(pl.multiple_of(block * depth, depth), depth)
        return qkv.at[rows, pl.ds(weight * count, count)]

    others = [lax.rem(index + step, shards_in) for step in range(1, shards_in)]
    greet(around("shard", shards_in) + around("ctx", owners) + around("tensor", cores))
    units = w_gate.shape[1] // owners
    hidden = pl.ds(pl.multiple_of(here * units, units), units)
    wide_down = w_down.shape[1]
    pieces = [
        (w_gate.at[:, hidden], stage_pack.at[:, pl.ds(0, units)]),
        (w_up.at[:, hidden], stage_pack.at[:, pl.ds(units, units)]),
    ]
    for k in range(units // depth):
        start = pl.multiple_of(here * units + k * depth, depth)
        place = pl.ds(2 * units + k * wide_down, wide_down)
        pieces.append((w_down.at[pl.ds(start, depth), :], stage_pack.at[:, place]))
    for k, (source, place) in enumerate(pieces):
        pltpu.make_async_copy(source, place, pack_sem.at[k]).start()
    notes[here] = note[...]
    fellows = [lax.rem(here + step, owners) for step in range(1, owners)]
    for fellow in fellows:
        send(note, notes.at[here], sent_n.at[fellow], came_n.at[here], {"ctx": fellow})
    square = shards_in == 4
    near = plane(index, shards_in)[:2] if square else others
    for weight in range(4):
        pltpu.make_async_copy(stored[weight], sources[weight], load_sem.at[weight]).wait()
        for other in near:
            send(
                sources[weight],
                target(weight, index),
                sent_w.at[weight, other],
                came_w.at[weight, index],
                {"shard": other},
            )
    gather_first([value], [out], sems, owners, cores)
    for weight in range(4):
        pltpu.make_async_copy(
            sources[weight], target(weight, index), own_sem.at[weight]
        ).start()
    for k, (source, place) in enumerate(pieces):
        pltpu.make_async_copy(source, place, pack_sem.at[k]).wait()
    pltpu.make_async_copy(stage_pack, packed, load_sem.at[4]).start()
    if square:
        across_x, across_y, far = plane(index, shards_in)
        for weight, source, device in (
            (0, across_x, across_y),
            (2, across_y, across_x),
            (1, across_x, across_y),
            (3, across_y, across_x),
        ):
            held = target(weight, source)
            landed(held, came_w.at[weight, source])
            send(
                held, held, passed_w.at[weight], came_w.at[weight, source], {"shard": device}
            )
    gather_rest([value], [out], sems, owners, cores)
    for fellow in fellows:
        landed(notes.at[fellow], came_n.at[fellow])
        landed(note, sent_n.at[fellow])
    pltpu.make_async_copy(stage_pack, packed, load_sem.at[4]).wait()
    for weight in range(4):
        pltpu.make_async_copy(
            sources[weight], target(weight, index), own_sem.at[weight]
        ).wait()
        for other in near:
            landed(sources[weight], sent_w.at[weight, other])
    if square:
        for weight, source in ((0, across_y), (2, across_x), (1, across_y), (3, across_x)):
            landed(target(weight, source), came_w.at[weight, source])
        for weight in range(4):
            landed(target(weight, far), came_w.at[weight, far])
            landed(sources[weight], passed_w.at[weight])
    else:
        for weight in range(4):
            for other in others:
                landed(target(weight, other), came_w.at[weight, other])


def open_team(collective_id, value, weights, note):
    shards_in, owners, cores = [lax.axis_size(a) for a in ("shard", "ctx", "tensor")]
    depth = weights[0].shape[0]
    count = weights[0].shape[1] // owners
    units = weights[4].shape[1] // owners
    pieces = 2 + units // depth
    out, qkv, out_w, packed, notes = pl.pallas_call(
        functools.partial(open_kernel, shards_in, owners, cores),
        out_shape=[
            jax.ShapeDtypeStruct((owners, cores, *value.shape), value.dtype),
            jax.ShapeDtypeStruct((shards_in * depth, 3 * count), value.dtype),
            jax.ShapeDtypeStruct((count, shards_in * weights[3].shape[1]), value.dtype),
            jax.ShapeDtypeStruct((depth, 3 * units), value.dtype),
            jax.ShapeDtypeStruct((owners, *note.shape), note.dtype),
        ],
        in_specs=[INSIDE] + [FAR] * 7 + [INSIDE],
        out_specs=[ANY] * 3 + [FAR] + [INSIDE],
        scratch_shapes=[
            pltpu.SemaphoreType.DMA((4,)),
            pltpu.SemaphoreType.DMA((4, shards_in)),
            pltpu.SemaphoreType.DMA((4, shards_in)),
            pltpu.SemaphoreType.DMA((4,)),
            pltpu.SemaphoreType.DMA((owners,)),
            pltpu.SemaphoreType.DMA((owners,)),
            pltpu.SemaphoreType.DMA((pieces,)),
            pltpu.SemaphoreType.DMA((5,)),
            pltpu.VMEM((3, depth, count), value.dtype),
            pltpu.VMEM((count, weights[3].shape[1]), value.dtype),
            pltpu.VMEM((depth, 3 * units), value.dtype),
        ]
        + gather_sems(1, owners),
        compiler_params=params(collective_id),
        cost_estimate=cost(40),
        name="open_team",
    )(value, *weights, note)
    return out.reshape(-1, value.shape[1]), qkv, out_w, packed, notes


def scatter_kernel(amount, owners, cores, *refs):
    parts, outs, refs = refs[:amount], refs[amount : 2 * amount], refs[2 * amount :]
    greet(line_partners(owners, cores))
    scatter(amount, owners, cores, parts, outs, refs)


def scatter(amount, owners, cores, parts, outs, refs):
    pairs, halves, from_left, from_right, own = [
        refs[k * amount : (k + 1) * amount] for k in range(5)
    ]
    total, sent_pair, came_pair, sent, came_left, came_right, load = refs[5 * amount :]
    here, core, pair, right, left = ring(owners, cores)
    order = [k // 2 if k % 2 else owners - 1 - k // 2 for k in range(owners)]
    for i in range(amount):
        for block in order:
            pltpu.make_async_copy(
                parts[i].at[block, core], own[i].at[block], load.at[i, block]
            ).start()
            send(
                parts[i].at[block, pair],
                pairs[i].at[block],
                sent_pair.at[i, block],
                came_pair.at[i, block],
                {"tensor": pair},
            )

    def add_up(i, block, more, arrived, came):
        landed(pairs[i].at[block], came_pair.at[i, block])
        landed(own[i].at[block], load.at[i, block])
        total[...] = own[i][block].astype(jnp.float32) + pairs[i][block].astype(jnp.float32)

        @pl.when(more)
        def _():
            landed(arrived[i].at[block], came.at[i, block])
            total[...] += arrived[i][block].astype(jnp.float32)

    def pass_on(i, block, more, arrived, came, device):
        add_up(i, block, more, arrived, came)
        halves[i][block] = total[...].astype(halves[i].dtype)
        send(
            halves[i].at[block],
            arrived[i].at[block],
            sent.at[i, block],
            came.at[i, block],
            {"ctx": device},
        )

    for step in range(2 * owners - 2):
        for i in range(amount):
            rightward = owners - 1 - (step - here)
            leftward = step - (owners - 1 - here)

            @pl.when((rightward > here) & (step >= here))
            def _():
                pass_on(i, rightward, here > 0, from_left, came_left, right)

            @pl.when((leftward >= 0) & (leftward < here))
            def _():
                pass_on(i, leftward, here < owners - 1, from_right, came_right, left)

    for i in range(amount):
        add_up(i, here, here > 0, from_left, came_left)

        @pl.when(here < owners - 1)
        def _():
            landed(from_right[i].at[here], came_right.at[i, here])
            total[...] += from_right[i][here].astype(jnp.float32)

        outs[i][...] = total[...]
    for i in range(amount):
        for block in range(owners):
            landed(pairs[i].at[block], sent_pair.at[i, block])

            @pl.when(block != here)
            def _():
                landed(halves[i].at[block], sent.at[i, block])


def scatter_scratch(amount, owners, block, kind):
    held = [pltpu.VMEM((owners, *block), kind)] * amount
    sems = [pltpu.SemaphoreType.DMA((amount, owners)) for _ in range(6)]
    return held * 5 + [pltpu.VMEM(block, jnp.float32)] + sems


def team_sum(collective_id, *values):
    owners, cores = lax.axis_size("ctx"), lax.axis_size("tensor")
    amount = len(values)
    width = values[0].shape[1]
    mine = values[0].shape[0] // (owners * cores)
    return pl.pallas_call(
        functools.partial(scatter_kernel, amount, owners, cores),
        out_shape=[jax.ShapeDtypeStruct((mine, width), jnp.float32)] * amount,
        in_specs=[ANY] * amount,
        out_specs=[INSIDE] * amount,
        scratch_shapes=scatter_scratch(amount, owners, (mine, width), values[0].dtype),
        compiler_params=params(collective_id),
        cost_estimate=cost(20 * amount),
        name="team_sum",
    )(*[v.reshape(owners, cores, mine, width) for v in values])


def swap_first(summed, held, local, sent, came, owners):
    here = lax.axis_index("ctx")
    count = summed.shape[0] // owners

    def rows(owner):
        return summed.at[pl.ds(pl.multiple_of(owner * count, count), count), :]

    for step in range(1, owners):
        other = lax.rem(here + step, owners)
        send(rows(other), held.at[here], sent.at[other], came.at[here], {"ctx": other})
    pltpu.make_async_copy(rows(here), held.at[here], local).start()


def put_rows(rows, outs, block, half, halves):
    amount = len(outs)
    units = rows.shape[1] // amount
    for j in range(units // block):
        start = half * units + j * block
        for i, out in enumerate(outs):
            first = (j * amount + i) * block
            piece = rows[:, first : first + block].astype(jnp.float32)
            if i < amount - 1:
                out[:, start : start + block] = piece
            else:
                out[start : start + block, :] = piece.T


def place_attn_kernel(attn, *outs):
    put_rows(attn[0], outs, outs[0].shape[1], 0, 1)


def place_kernel(block, where, own_a, far_a, own_b, far_b, early, late, *outs):
    core = where[0]
    for own, far, out in ((own_a, far_a, outs[0]), (own_b, far_b, outs[1])):
        out[0, core] = own[0]
        out[0, out.shape[1] - 1 - core] = far[0]
    put_rows(early[0], outs[2:], block, 0, 2)
    put_rows(late[0], outs[2:], block, 1, 2)


def placed_rows(owners, count, units, amount):
    specs = [pl.BlockSpec((count, units), lambda c, *_: (0, c))] * (amount - 1)
    specs.append(pl.BlockSpec((units, count), lambda c, *_: (c, 0)))
    shapes = [jax.ShapeDtypeStruct((count, owners * units), jnp.float32)] * (amount - 1)
    shapes.append(jax.ShapeDtypeStruct((owners * units, count), jnp.float32))
    return specs, shapes


def place_attn(attn):
    owners, count, wide = attn.shape
    specs, shapes = placed_rows(owners, count, wide // 4, 4)
    return pl.pallas_call(
        place_attn_kernel,
        grid=(owners,),
        in_specs=[pl.BlockSpec((1, count, wide), lambda c: (c, 0, 0))],
        out_specs=specs,
        out_shape=shapes,
        compiler_params=pltpu.CompilerParams(
            dimension_semantics=("arbitrary",), vmem_limit_bytes=60 << 20
        ),
        cost_estimate=cost(2),
        name="place_attn",
    )(attn)


def place_all(streams, early, late):
    owners, cores = lax.axis_size("ctx"), lax.axis_size("tensor")
    run = streams[0].shape
    block = late.shape[2] // (3 * BLOCKS // 2)

    def lead(shape):
        return pl.BlockSpec((1, *shape[1:]), lambda c, _: (c,) + (0,) * (len(shape) - 1))

    both = (run[0], cores, *run[1:])
    specs, shapes = [lead(both)] * 2, [jax.ShapeDtypeStruct(both, streams[0].dtype)] * 2
    more, wide = placed_rows(owners, late.shape[1], 2 * late.shape[2] // 3, 3)
    specs, shapes = specs + more, shapes + wide
    return pl.pallas_call(
        functools.partial(place_kernel, block),
        grid_spec=pltpu.PrefetchScalarGridSpec(
            num_scalar_prefetch=1,
            grid=(owners,),
            in_specs=[lead(v.shape) for v in (*streams, early, late)],
            out_specs=specs,
        ),
        out_shape=shapes,
        compiler_params=pltpu.CompilerParams(
            dimension_semantics=("arbitrary",), vmem_limit_bytes=60 << 20
        ),
        cost_estimate=cost(7),
        name="place_all",
    )(lax.axis_index("tensor")[None].astype(jnp.int32), *streams, early, late)


def swap_rest(summed, held, local, sent, came, owners):
    here = lax.axis_index("ctx")
    count = summed.shape[0] // owners
    own = summed.at[pl.ds(pl.multiple_of(here * count, count), count), :]
    for step in range(owners):
        source = lax.rem(here + owners - step, owners)
        if step == 0:
            pltpu.make_async_copy(own, held.at[here], local).wait()
        else:
            landed(held.at[source], came.at[source])
    for step in range(1, owners):
        other = lax.rem(here + step, owners)
        landed(held.at[other], sent.at[other])


def held_shape(summed, owners):
    return (owners, summed.shape[0] // owners, summed.shape[1])


def swap_sems(owners):
    return [
        pltpu.SemaphoreType.DMA,
        pltpu.SemaphoreType.DMA((owners,)),
        pltpu.SemaphoreType.DMA((owners,)),
    ]


def around(axis, size):
    index = lax.axis_index(axis)
    return [{axis: lax.rem(index + step, size)} for step in range(1, size)]


def swap_kernel_alone(owners, summed, held, *sems):
    greet(around("ctx", owners))
    swap_first(summed, held, *sems, owners)
    swap_rest(summed, held, *sems, owners)


def team_rows(collective_id, summed):
    owners = lax.axis_size("ctx")
    return pl.pallas_call(
        functools.partial(swap_kernel_alone, owners),
        out_shape=jax.ShapeDtypeStruct(held_shape(summed, owners), summed.dtype),
        in_specs=[INSIDE],
        out_specs=ANY,
        scratch_shapes=swap_sems(owners),
        compiler_params=params(collective_id),
        cost_estimate=cost(20),
        name="team_rows",
    )(summed)


def close_kernel(amount, shards_in, owners, cores, *refs):
    values, mixed, grads = refs[:amount], refs[amount], refs[amount + 1]
    refs = refs[amount + 2 :]
    outs, mix_out, late = refs[:amount], refs[amount], refs[amount + 1]
    summed, refs = refs[amount + 2], refs[amount + 3 :]
    pairs, half, quarters, blocks, sent, came = refs[:6]
    sent_c, came_c, sent_s, came_s, sent_b, came_b = refs[6:12]
    swap = refs[12:]
    here, core, pair, right, left = ring(owners, cores)
    index = lax.axis_index("shard")
    near = [lax.rem(here + step, owners) for step in range(1, owners)]
    others = [lax.rem(index + step, shards_in) for step in range(1, shards_in)]
    greet([{"tensor": pair}] + around("ctx", owners) + around("shard", shards_in))
    wide = mixed.shape[1] // cores
    thin = wide // owners
    send(
        mixed.at[:, pl.ds(pl.multiple_of(pair * wide, wide), wide)],
        pairs,
        sent.at[amount],
        came.at[amount],
        {"tensor": pair},
    )
    for i in range(amount):
        send(values[i], outs[i], sent.at[i], came.at[i], {"tensor": pair})
    landed(pairs, came.at[amount])
    half[...] = mixed[:, pl.ds(pl.multiple_of(core * wide, wide), wide)] + pairs[...]
    for other in near:
        send(
            half.at[:, pl.ds(pl.multiple_of(other * thin, thin), thin)],
            quarters.at[here],
            sent_c.at[other],
            came_c.at[here],
            {"ctx": other},
        )
    swap_first(grads, late, *swap, owners)
    total = half[:, pl.ds(pl.multiple_of(here * thin, thin), thin)]
    for other in near:
        landed(quarters.at[other], came_c.at[other])
        total += quarters[other]
    blocks[index] = total
    for other in others:
        send(
            blocks.at[index], blocks.at[index], sent_s.at[other], came_s.at[index], {"shard": other}
        )
    for other in others:
        landed(blocks.at[other], came_s.at[other])
    total = blocks[0]
    for block in range(1, shards_in):
        total += blocks[block]

    def place(owner, half_of):
        return summed.at[half_of * owners + owner]

    summed[core * owners + here] = total
    for other in near:
        send(place(here, core), place(here, core), sent_b.at[other], came_b.at[here, core], {"ctx": other})
    send(place(here, core), place(here, core), sent_b.at[here], came_b.at[here, core], {"tensor": pair})
    for other in near:
        landed(place(other, core), came_b.at[other, core])
        send(
            place(other, core),
            place(other, core),
            sent_b.at[owners + other],
            came_b.at[other, core],
            {"tensor": pair},
        )
    for owner in range(owners):
        landed(place(owner, pair), came_b.at[owner, pair])
        landed(place(owner, core), sent_b.at[owner])
    for owner in range(owners):
        for half_of in range(cores):
            found = summed[half_of * owners + owner]
            start = (half_of * owners + owner) * thin
            for row in range(mix_out.shape[0] * mix_out.shape[1]):
                k, h = row // mix_out.shape[1], row % mix_out.shape[1]
                mix_out[k, h : h + 1, start : start + thin] = found[row : row + 1, :]
    for other in near:
        landed(place(other, core), sent_b.at[owners + other])
        landed(quarters.at[other], sent_c.at[other])
    for other in others:
        landed(blocks.at[other], sent_s.at[other])
    landed(pairs, sent.at[amount])
    swap_rest(grads, late, *swap, owners)
    for i in range(amount):
        landed(outs[i], came.at[i])
        landed(values[i], sent.at[i])


def close_team(collective_id, grads, mixed, *values):
    shards_in, owners, cores = [lax.axis_size(a) for a in ("shard", "ctx", "tensor")]
    amount = len(values)
    height, width = mixed.shape
    thin = width // (cores * owners)
    out = pl.pallas_call(
        functools.partial(close_kernel, amount, shards_in, owners, cores),
        out_shape=[
            jax.ShapeDtypeStruct(v.shape, v.dtype) for v in values
        ]
        + [jax.ShapeDtypeStruct((height // 2, 2, width), jnp.float32)]
        + [jax.ShapeDtypeStruct(held_shape(grads, owners), grads.dtype)],
        in_specs=[INSIDE] * (amount + 2),
        out_specs=[ANY] * amount + [INSIDE, ANY],
        scratch_shapes=[
            pltpu.VMEM((cores * owners, height, thin), jnp.float32),
            pltpu.VMEM((height, width // cores), jnp.float32),
            pltpu.VMEM((height, width // cores), jnp.float32),
            pltpu.VMEM((owners, height, thin), jnp.float32),
            pltpu.VMEM((shards_in, height, thin), jnp.float32),
            pltpu.SemaphoreType.DMA((amount + 1,)),
            pltpu.SemaphoreType.DMA((amount + 1,)),
            pltpu.SemaphoreType.DMA((owners,)),
            pltpu.SemaphoreType.DMA((owners,)),
            pltpu.SemaphoreType.DMA((shards_in,)),
            pltpu.SemaphoreType.DMA((shards_in,)),
            pltpu.SemaphoreType.DMA((2 * owners,)),
            pltpu.SemaphoreType.DMA((owners, cores)),
        ]
        + swap_sems(owners),
        compiler_params=params(collective_id),
        cost_estimate=cost(60),
        name="close_team",
    )(*values, mixed, grads)
    return out[amount], out[:amount], out[amount + 1]


def ffn_kernel(
    u_ref,
    dy_ref,
    gate_ref,
    up_ref,
    down_ref,
    y_ref,
    du_ref,
    early_ref,
    late_ref,
    y_sum,
    du_sum,
    u_t,
    dy_t,
):
    step = pl.program_id(0)
    early = step < pl.num_programs(0) // 2
    total, width = u_ref.shape
    block = gate_ref.shape[1]
    tile = down_ref.shape[2]

    @pl.when(step == 0)
    def _():
        y_sum[...] = jnp.zeros_like(y_sum)
        du_sum[...] = jnp.zeros_like(du_sum)
        for start in range(0, width, tile):
            u_t[start : start + tile, :] = u_ref[:, start : start + tile].T
            dy_t[start : start + tile, :] = dy_ref[:, start : start + tile].T

    gate = dot(u_ref[...], gate_ref[...])
    upward = dot(u_ref[...], up_ref[...])
    shards_in = down_ref.shape[0]
    grad_hidden = 0.0
    for k in range(shards_in):
        grad_hidden = grad_hidden + contract_cols(
            dy_ref[:, k * tile : (k + 1) * tile], down_ref[k]
        )
    sigma = jax.nn.sigmoid(gate)
    swish = gate * sigma
    hidden = (swish * upward).astype(jnp.bfloat16)
    grad_gate = (grad_hidden * upward * (sigma + swish * (1.0 - sigma))).astype(jnp.bfloat16)
    grad_up = (grad_hidden * swish).astype(jnp.bfloat16)
    for k in range(shards_in):
        span = slice(k * tile, (k + 1) * tile)
        y_sum[:, span] += dot(hidden, down_ref[k])
        du_sum[:, span] += contract_cols(grad_gate, gate_ref[span, :]) + contract_cols(
            grad_up, up_ref[span, :]
        )

    def weights_back(grad_ref):
        for start in range(0, width, tile):
            span = slice(start, start + tile)
            grad_ref[span, :block] = dot(u_t[span, :], grad_gate).astype(jnp.bfloat16)
            grad_ref[span, block : 2 * block] = dot(u_t[span, :], grad_up).astype(jnp.bfloat16)
            grad_ref[span, 2 * block :] = dot(dy_t[span, :], hidden).astype(jnp.bfloat16)

    @pl.when(early)
    def _():
        weights_back(early_ref)

    @pl.when(jnp.logical_not(early))
    def _():
        weights_back(late_ref)

    @pl.when(step == pl.num_programs(0) - 1)
    def _():
        y_ref[...] = y_sum[...].astype(jnp.bfloat16)
        du_ref[...] = du_sum[...].astype(jnp.bfloat16)


def ffn(u, dy, weights):
    total, width = u.shape
    shards_in = lax.axis_size("shard")
    depth = width // shards_in
    units = weights.shape[1] // 3
    blocks = BLOCKS
    block = units // blocks
    half = blocks // 2
    whole = pl.BlockSpec((total, width), lambda j: (0, 0), pipeline_mode=pl.Buffered(1))
    low = functools.partial(jax.ShapeDtypeStruct, dtype=jnp.bfloat16)
    return pl.pallas_call(
        ffn_kernel,
        grid=(blocks,),
        in_specs=[
            whole,
            whole,
            pl.BlockSpec((width, block), lambda j: (0, j)),
            pl.BlockSpec((width, block), lambda j: (0, blocks + j)),
            pl.BlockSpec(
                (shards_in, block, depth),
                lambda j: (0, j % (depth // block), 2 * units // depth + j // (depth // block)),
            ),
        ],
        out_specs=[
            whole,
            whole,
            pl.BlockSpec((width, 3 * block), lambda j: (0, jnp.minimum(j, half - 1))),
            pl.BlockSpec((width, 3 * block), lambda j: (0, jnp.maximum(j - half, 0))),
        ],
        out_shape=[low((total, width))] * 2 + [low((width, 3 * units // 2))] * 2,
        scratch_shapes=[
            pltpu.VMEM((total, width), jnp.float32),
            pltpu.VMEM((total, width), jnp.float32),
            pltpu.VMEM((width, total), jnp.bfloat16),
            pltpu.VMEM((width, total), jnp.bfloat16),
        ],
        compiler_params=pltpu.CompilerParams(
            dimension_semantics=("arbitrary",), vmem_limit_bytes=60 << 20
        ),
        cost_estimate=cost(30),
        name="ffn",
    )(u, dy, weights, weights, weights.reshape(shards_in, depth, 3 * units))


def pack_kernel(sent, value, out):
    for i in range(value.shape[1]):
        out[0, i] = value[:, i, :]


def pack_runs(value, sent, part):
    rows_in, total, width = value.shape
    return pl.pallas_call(
        pack_kernel,
        grid_spec=pltpu.PrefetchScalarGridSpec(
            num_scalar_prefetch=1,
            grid=(sent.shape[0],),
            in_specs=[
                pl.BlockSpec((part, total, width), lambda c, first: (first[c], 0, 0)),
            ],
            out_specs=pl.BlockSpec((1, total, part, width), lambda c, first: (c, 0, 0, 0)),
        ),
        out_shape=jax.ShapeDtypeStruct((sent.shape[0], total, part, width), value.dtype),
        compiler_params=pltpu.CompilerParams(dimension_semantics=("arbitrary",)),
        cost_estimate=cost(2),
        name="pack_runs",
    )(sent, value)


def head_probs(query, key, placing, placed):
    scores = contract_cols(query, key) * HD ** (-0.5)
    allowed = (placed >= placing[:, 0:1]) & (placed <= placing[:, 1:2])
    scores = jnp.where(allowed, scores, FLOOR_SCORE)
    probs = jnp.exp(scores - jnp.max(scores, -1, keepdims=True))
    return probs / jnp.sum(probs, -1, keepdims=True)


def turn(value, turns, back):
    swung = pltpu.roll(value, HD // 2, 1) * turns[1]
    return value * turns[0] - swung if back else value * turns[0] + swung


def attend_kernel(
    u_ref, qkv_ref, out_ref, turns, placing, placed, y_ref, q_ref, k_ref, v_ref, o_ref
):
    count = q_ref.shape[1]
    u = u_ref[...]
    for first in range(0, count, HD):
        head = slice(first, first + HD)

        def lin(which):
            start = which * count + first
            return dot(u, qkv_ref[:, start : start + HD])

        query = turn(lin(0), turns, False).astype(jnp.bfloat16)
        key = turn(lin(1), turns, False).astype(jnp.bfloat16)
        value = lin(2).astype(jnp.bfloat16)
        q_ref[:, head] = query
        k_ref[:, head] = key
        v_ref[:, head] = value
        probs = head_probs(query, key, placing[...], placed[...])
        o_ref[:, head] = dot(probs.astype(jnp.bfloat16), value).astype(jnp.bfloat16)
    width = y_ref.shape[1]
    for start in range(0, width, 512):
        y_ref[:, start : start + 512] = dot(o_ref[...], out_ref[:, start : start + 512])


def attend(u, qkv, out_w, turns, placing, placed):
    total, count = u.shape[0], out_w.shape[0]
    low = jax.ShapeDtypeStruct((total, count), jnp.bfloat16)
    return pl.pallas_call(
        attend_kernel,
        out_shape=[jax.ShapeDtypeStruct((total, out_w.shape[1]), jnp.float32)] + [low] * 4,
        in_specs=[INSIDE] * 6,
        out_specs=[INSIDE] * 5,
        compiler_params=pltpu.CompilerParams(vmem_limit_bytes=60 << 20),
        cost_estimate=cost(12),
        name="attend",
    )(u, qkv, out_w, turns, placing, placed)


def attend_back_kernel(
    owners,
    cores,
    dy_ref,
    u_ref,
    qkv_ref,
    out_ref,
    q_ref,
    k_ref,
    v_ref,
    o_ref,
    turns,
    placing,
    placed,
    summed,
    grad_ref,
    sum_ref,
    rows,
    lin,
    du_ref,
    *refs,
):
    greet(around("ctx", owners) + around("tensor", cores))
    swap, refs = refs[:3], refs[3:]
    swap_first(summed, rows, *swap, owners)
    count = q_ref.shape[1]
    width = dy_ref.shape[1]
    scale = HD ** (-0.5)
    low = jnp.bfloat16
    for first in range(0, count, HD):
        head = slice(first, first + HD)
        query, key, value = q_ref[:, head], k_ref[:, head], v_ref[:, head]
        grad_out = contract_cols(dy_ref[...], out_ref[head, :]).astype(low)
        probs = head_probs(query, key, placing[...], placed[...])
        grad_probs = contract_cols(grad_out, value)
        delta = jnp.sum(probs * grad_probs, -1, keepdims=True)
        grad_scores = (probs * (grad_probs - delta)).astype(low)
        grad_query = turn(dot(grad_scores, key) * scale, turns, True)
        grad_key = turn(contract_rows(grad_scores, query) * scale, turns, True)
        grad_value = contract_rows(probs.astype(low), grad_out)
        for which, grad in enumerate((grad_query, grad_key, grad_value)):
            start = which * count + first
            lin[:, start : start + HD] = grad.astype(low)
    tile = min(512, width)
    edge = lin.shape[1]
    for start in range(0, width, tile):
        span = slice(start, start + tile)
        du_part = contract_cols(lin[...], qkv_ref[span, :]).astype(low)
        du_ref[:, :, :, span] = du_part.reshape(*du_ref.shape[:3], tile)
    for start in range(0, width, tile):
        span = slice(start, start + tile)
        grad_ref[span, :edge] = dot(u_ref[:, span].T, lin[...]).astype(low)
        grad_ref[span, edge:] = dot(dy_ref[:, span].T, o_ref[...]).astype(low)
    scatter(1, owners, cores, [du_ref], [sum_ref], refs)
    swap_rest(summed, rows, *swap, owners)


def attend_back(collective_id, dy, u, qkv, out_w, q, k, v, o, turns, placing, placed, summed):
    owners, cores = lax.axis_size("ctx"), lax.axis_size("tensor")
    total, width = u.shape
    count = q.shape[1]
    mine = total // (owners * cores)
    return pl.pallas_call(
        functools.partial(attend_back_kernel, owners, cores),
        out_shape=[
            jax.ShapeDtypeStruct((width, 4 * count), jnp.bfloat16),
            jax.ShapeDtypeStruct((mine, width), jnp.float32),
            jax.ShapeDtypeStruct(held_shape(summed, owners), summed.dtype),
        ],
        in_specs=[INSIDE] * 11 + [ANY],
        out_specs=[INSIDE] * 2 + [ANY],
        scratch_shapes=[
            pltpu.VMEM((total, 3 * count), jnp.bfloat16),
            pltpu.VMEM((owners, cores, mine, width), jnp.bfloat16),
        ]
        + swap_sems(owners)
        + scatter_scratch(1, owners, (mine, width), jnp.bfloat16),
        compiler_params=params(collective_id),
        cost_estimate=cost(50),
        name="attend_back",
    )(dy, u, qkv, out_w, q, k, v, o, turns, placing, placed, summed)


EXACT = functools.partial(
    lax.dot_general, precision=PRECISE, preferred_element_type=jnp.float32
)


def columns_of(pieces):
    rows_in = pieces[0].shape[0]
    lane = lax.broadcasted_iota(jnp.int32, (rows_in, 8), 1)
    out = jnp.zeros((rows_in, 8), jnp.float32)
    for k, piece in enumerate(pieces):
        out = jnp.where(lane == k, piece, out)
    return out


def tables_of(current, weight, static, table_ref, active_ref):
    branch_in = 0.0
    tables = []
    for i, stream in enumerate(current):
        normed, scaled = norm_rows(stream)
        active = jnp.tanh(EXACT(normed, weight, (((1,), (1,)), ((), ()))))
        table = active + static[i : i + 1, :]
        table_ref[i] = table
        active_ref[i] = active
        tables.append(table)
        branch_in = branch_in + table[:, 0:1] * stream
    return tables, branch_in


def norm_plain(value):
    centred = value - jnp.mean(value, -1, keepdims=True)
    scaled = lax.rsqrt(jnp.mean(centred * centred, -1, keepdims=True) + EPSILON)
    return (centred * scaled, scaled)


def mix_first(current, weight, static):
    normed, _ = norm_plain(current)
    active = jnp.tanh(jnp.einsum("tsd,dk->tsk", normed, weight, precision=PRECISE))
    table = active + static
    total = current.shape[1]
    branch_in = sum(table[:, i, 0][:, None] * current[:, i] for i in range(total))
    normed, scaled = norm_plain(branch_in)

    def by_stream(value):
        return jnp.pad(value.transpose(1, 0, 2), ((0, 0), (0, 0), (0, 8 - value.shape[2])))

    scaled = jnp.pad(scaled, ((0, 0), (0, 7)))
    return normed.astype(jnp.bfloat16), normed, scaled, by_stream(table), by_stream(active)


def mix_second_kernel(
    source,
    streams,
    branch_out,
    table_one,
    arrived,
    weight,
    static,
    middle_ref,
    low_ref,
    grad_low_ref,
    normed_ref,
    scaled_ref,
    table_ref,
    active_ref,
    top_ref,
):
    total = streams.shape[0]
    y = branch_out[...]
    first = [table_one[i] for i in range(total)]
    current = [streams[i].astype(jnp.float32) for i in range(total)]
    middle = []
    for j in range(total):
        mixed = first[j][:, total + 1 : total + 2] * y
        for i in range(total):
            mixed = mixed + first[i][:, 1 + j : 2 + j] * current[i]
        middle.append(mixed)
        middle_ref[j] = mixed
    tables, branch_in = tables_of(middle, weight[...], static[...], table_ref, active_ref)
    normed, scaled = norm_rows(branch_in)
    normed_ref[...] = normed
    low_ref[...] = normed.astype(jnp.bfloat16)
    scaled_ref[...] = columns_of([scaled])
    grad = 0.0
    for j in range(total):
        top = arrived[0, j]
        top_ref[j] = top
        grad = grad + tables[j][:, total + 1 : total + 2] * top.astype(jnp.float32)
    grad_low_ref[...] = grad.astype(jnp.bfloat16)


def connection_back(
    current, grad_top, branch_out, grad_in, normed_in, scaled_in, tables, actives, weight, sums
):
    total = len(current)
    weight_sum, static_sum = sums
    dx = scaled_in * (grad_in - mean_of(grad_in) - normed_in * mean_of(grad_in * normed_in))
    result = []
    for i, stream in enumerate(current):
        pieces = [jnp.sum(dx * stream, -1, keepdims=True)]
        pieces += [jnp.sum(stream * top, -1, keepdims=True) for top in grad_top]
        pieces.append(jnp.sum(grad_top[i] * branch_out, -1, keepdims=True))
        grad_table = columns_of(pieces)
        static_sum[i : i + 1, :] += jnp.sum(grad_table, 0, keepdims=True)
        grad_inner = grad_table * (1.0 - actives[i] * actives[i])
        normed, scaled = norm_rows(stream)
        weight_sum[...] += EXACT(grad_inner, normed, (((0,), (0,)), ((), ())))
        grad_normed = EXACT(grad_inner, weight, (((1,), (0,)), ((), ())))
        grad = tables[i][:, 0:1] * dx + norm_back(normed, scaled, grad_normed)
        for j in range(total):
            grad = grad + tables[i][:, 1 + j : 2 + j] * grad_top[j]
        result.append(grad)
    return result


def start_sums(sums):
    @pl.when(pl.program_id(0) == 0)
    def _():
        for ref in sums:
            ref[...] = jnp.zeros_like(ref)


def back_second_kernel(
    middle,
    top,
    branch_out,
    grad_in,
    normed_in,
    scaled_in,
    table,
    active,
    table_one,
    weight,
    final_ref,
    grad_ref,
    grad_low_ref,
    *sums,
):
    start_sums(sums)
    total = middle.shape[0]
    current = [middle[i] for i in range(total)]
    grad_top = [top[i].astype(jnp.float32) for i in range(total)]
    tables = [table[i] for i in range(total)]
    y = branch_out[...]
    for j in range(total):
        mixed = tables[j][:, total + 1 : total + 2] * y
        for i in range(total):
            mixed = mixed + tables[i][:, 1 + j : 2 + j] * current[i]
        final_ref[0, :, j, :] = mixed.astype(jnp.bfloat16)
    grads = connection_back(
        current,
        grad_top,
        y,
        grad_in[...],
        normed_in[...],
        scaled_in[:, 0:1],
        tables,
        [active[i] for i in range(total)],
        weight[...],
        sums,
    )
    low = 0.0
    for j in range(total):
        grad_ref[j] = grads[j]
        low = low + table_one[j][:, total + 1 : total + 2] * grads[j]
    grad_low_ref[...] = low.astype(jnp.bfloat16)


def back_first_kernel(
    streams,
    top,
    branch_out,
    grad_in,
    normed_in,
    scaled_in,
    table,
    active,
    weight,
    grad_ref,
    *sums,
):
    start_sums(sums)
    total = streams.shape[0]
    grads = connection_back(
        [streams[i].astype(jnp.float32) for i in range(total)],
        [top[i] for i in range(total)],
        branch_out[...],
        grad_in[...],
        normed_in[...],
        scaled_in[:, 0:1],
        [table[i] for i in range(total)],
        [active[i] for i in range(total)],
        weight[...],
        sums,
    )
    for j in range(total):
        grad_ref[0, :, j, :] = grads[j].astype(jnp.bfloat16)


def by_token(tile, shape, kind=jnp.float32):
    block = (*shape[:-2], tile, shape[-1])
    lead = (0,) * (len(shape) - 2)
    spec = pl.BlockSpec(block, lambda step, *_: (*lead, step, 0))
    return spec, jax.ShapeDtypeStruct(shape, kind)


def fixed(shape, kind=jnp.float32):
    spec = pl.BlockSpec(shape, lambda step, *_: (0,) * len(shape))
    return spec, jax.ShapeDtypeStruct(shape, kind)


def token_call(kernel, name, tile, ins, outs, prefetch=(), special=None):
    specs, values = [], []
    for value, tiled in ins:
        if tiled == "run":
            specs.append(special)
        else:
            specs.append(by_token(tile, value.shape)[0] if tiled else fixed(value.shape)[0])
        values.append(value)
    tokens = ins[0][0].shape[-2]
    return pl.pallas_call(
        kernel,
        grid_spec=pltpu.PrefetchScalarGridSpec(
            num_scalar_prefetch=len(prefetch),
            grid=(tokens // tile,),
            in_specs=specs,
            out_specs=[o[0] for o in outs],
        ),
        out_shape=[o[1] for o in outs],
        compiler_params=pltpu.CompilerParams(
            dimension_semantics=("arbitrary",), vmem_limit_bytes=60 << 20
        ),
        cost_estimate=cost(5),
        name=name,
    )(*prefetch, *values)


def shards(
    streams,
    lengths,
    destination,
    w_query,
    w_key,
    w_value,
    w_output,
    w_gate,
    w_up,
    w_down,
    mix_weight,
    mix_static,
    cotangent,
):
    rows_here, stream_total, width = streams.shape
    owners = lax.axis_size("ctx")
    cores = lax.axis_size("tensor")
    here = lax.axis_index("ctx")
    core = lax.axis_index("tensor")
    run_rows = rows_here // owners
    part = run_rows // cores
    mine = rows_here // cores
    group_rows = rows_here * owners
    head_cols = w_query.shape[1] // owners
    heads = head_cols // HD
    units = w_gate.shape[1] // owners
    scale = HD ** (-0.5)

    def columns(weight, count):
        return lax.dynamic_slice_in_dim(weight, here * count, count, 1)

    def rows(weight, count):
        return lax.dynamic_slice_in_dim(weight, here * count, count, 0)

    order = jnp.arange(group_rows, dtype=jnp.int32)
    within = order % mine
    placed = (
        order // rows_here * rows_here
        + within // part * run_rows
        + order % rows_here // mine * part
        + within % part
    )
    spans = lengths[0]
    count = jnp.arange(spans.shape[0], dtype=jnp.int32)
    starts = jnp.sum(jnp.where(count[None, :] < count[:, None], spans[None, :], 0), 1)
    begin = jnp.max(jnp.where(starts[None, :] <= placed[:, None], starts[None, :], 0), axis=1)
    cosine, sine = angles(placed - begin, HD)
    turns = jnp.stack(
        [jnp.concatenate([cosine, cosine], -1), jnp.concatenate([-sine, sine], -1)]
    ).reshape(2, group_rows, HD)
    placing = jnp.stack([begin, placed], 1)
    placed = placed[None]

    local_dest = destination - lax.axis_index("shard") * group_rows
    heads_of_runs = local_dest.reshape(owners, run_rows)[:, 0]
    came_from = heads_of_runs // rows_here
    note = jnp.broadcast_to(jnp.pad(heads_of_runs, (0, 128 - owners)), (8, 128))

    turned_weight = jnp.pad(mix_weight.transpose(0, 2, 1), ((0, 0), (0, 2), (0, 0)))
    static = jnp.pad(mix_static, ((0, 0), (0, 0), (0, 2)))
    split = streams.reshape(owners, cores, part, stream_total, width)
    current = lax.dynamic_index_in_dim(split, core, 1, keepdims=False)
    current = current.reshape(mine, stream_total, width)
    attn_low, attn_normed, attn_scaled, table_one, active_one = mix_first(
        current.astype(jnp.float32), mix_weight[0], mix_static[0]
    )
    current = current.transpose(1, 0, 2)
    low = jnp.bfloat16
    tile = min(16, part)
    small = by_token(tile, (stream_total, mine, 8))
    attn_input, qkv, out_w, packed, notes = open_team(
        0, attn_low, (w_query, w_key, w_value, w_output, w_gate, w_up, w_down), note
    )
    ffn_weights = lax.all_gather(packed, "shard", axis=0, tiled=True)
    every = notes[:, 0, :owners]
    sent = jnp.sum(jnp.where(every // rows_here == here, every % rows_here, 0), 1) // part + core
    packed = pack_runs(cotangent, sent, part)
    arrived = lax.all_to_all(packed, "ctx", split_axis=0, concat_axis=0, tiled=True)
    attn_part, queries, keys, values, attended = attend(
        attn_input, qkv, out_w, turns, placing, placed
    )
    [attn_out] = team_sum(1, attn_part)

    (
        middle,
        ffn_low,
        grad_ffn_low,
        ffn_normed,
        ffn_scaled,
        table_two,
        active_two,
        grad_top,
    ) = token_call(
        mix_second_kernel,
        "mix_second",
        tile,
        [
            (current, True),
            (attn_out, True),
            (table_one, True),
            (arrived, "run"),
            (turned_weight[1], False),
            (static[1], False),
        ],
        [
            by_token(tile, (stream_total, mine, width)),
            by_token(tile, (mine, width), low),
            by_token(tile, (mine, width), low),
            by_token(tile, (mine, width)),
            by_token(tile, (mine, 8)),
            small,
            small,
            by_token(tile, (stream_total, mine, width), low),
        ],
        (came_from,),
        pl.BlockSpec(
            (1, stream_total, tile, width),
            lambda step, source: (source[step * tile // part], 0, step % (part // tile), 0),
        ),
    )
    ffn_input, grad_ffn_out = team_gather(2, ffn_low, grad_ffn_low)
    ffn_part, ffn_input_part, *ffn_grads = ffn(ffn_input, grad_ffn_out, ffn_weights)

    def shard_sum(partial):
        return lax.psum_scatter(partial, "shard", scatter_dimension=0, tiled=True)

    early_sum, late_sum = [shard_sum(grads) for grads in ffn_grads]
    ffn_out, grad_ffn_input = team_sum(3, ffn_part, ffn_input_part)
    sums = [fixed((8, width)), fixed((stream_total, 8))]
    runs = (
        pl.BlockSpec(
            (1, tile, stream_total, width),
            lambda step, *_: (step * tile // part, step % (part // tile), 0, 0),
        ),
        jax.ShapeDtypeStruct((owners, part, stream_total, width), low),
    )
    final, grad_middle, grad_attn_low, weight_two, static_two = token_call(
        back_second_kernel,
        "back_second",
        tile,
        [
            (middle, True),
            (grad_top, True),
            (ffn_out, True),
            (grad_ffn_input, True),
            (ffn_normed, True),
            (ffn_scaled, True),
            (table_two, True),
            (active_two, True),
            (table_one, True),
            (turned_weight[1], False),
        ],
        [
            runs,
            by_token(tile, (stream_total, mine, width)),
            by_token(tile, (mine, width), low),
            *sums,
        ],
    )
    [grad_attn_out] = team_gather(4, grad_attn_low)

    attn_grads, grad_attn_input, early_rows = attend_back(
        5,
        grad_attn_out,
        attn_input,
        qkv,
        out_w,
        queries,
        keys,
        values,
        attended,
        turns,
        placing,
        placed,
        early_sum,
    )
    attn_sum = shard_sum(attn_grads)

    grad_current, weight_one, static_one = token_call(
        back_first_kernel,
        "back_first",
        tile,
        [
            (current, True),
            (grad_middle, True),
            (attn_out, True),
            (grad_attn_input, True),
            (attn_normed, True),
            (attn_scaled, True),
            (table_one, True),
            (active_one, True),
            (turned_weight[0], False),
        ],
        [runs, *sums],
    )
    statics = jnp.stack([static_one, static_two]).reshape(1, -1)
    mixed = jnp.concatenate(
        [
            jnp.stack([weight_one, weight_two], 1).reshape(16, width),
            jnp.pad(statics, ((0, 7), (0, width - statics.size))),
        ],
        0,
    )

    mixed, (far_final, far_grad), late_rows = close_team(
        7, late_sum, mixed, final, grad_current
    )
    streams_out, grad_streams, grad_gate, grad_up, grad_down = place_all(
        (final, far_final, grad_current, far_grad), early_rows, late_rows
    )
    mixed, attn_sum, grad_gate = lax.optimization_barrier((mixed, attn_sum, grad_gate))
    grad_query, grad_key, grad_value, grad_output = place_attn(team_rows(8, attn_sum))
    columns_in = mix_weight.shape[2]
    grad_mix_weight = mixed[:columns_in].transpose(1, 2, 0)
    grad_mix_static = mixed[8, 0, : statics.size].reshape(2, stream_total, 8)[:, :, :columns_in]

    return (
        streams_out.reshape(rows_here, stream_total, width),
        grad_streams.reshape(rows_here, stream_total, width),
        grad_query,
        grad_key,
        grad_value,
        grad_output,
        grad_gate,
        grad_up,
        grad_down,
        grad_mix_weight,
        grad_mix_static,
    )


def solution(mesh):
    return jax.shard_map(
        shards,
        mesh=mesh,
        in_specs=(
            P(("shard", "ctx"), None, None),
            P("shard", None),
            P(("shard", "ctx")),
            P("shard", "tensor"),
            P("shard", "tensor"),
            P("shard", "tensor"),
            P("tensor", "shard"),
            P("shard", "tensor"),
            P("shard", "tensor"),
            P("tensor", "shard"),
            P(),
            P(),
            P(("shard", "ctx"), None, None),
        ),
        out_specs=(
            P(("shard", "ctx"), None, None),
            P(("shard", "ctx"), None, None),
            P(("shard", "ctx"), "tensor"),
            P(("shard", "ctx"), "tensor"),
            P(("shard", "ctx"), "tensor"),
            P("tensor", ("shard", "ctx")),
            P(("shard", "ctx"), "tensor"),
            P(("shard", "ctx"), "tensor"),
            P("tensor", ("shard", "ctx")),
            P(),
            P(),
        ),
        check_vma=False,
    )
```

```python
import functools

import jax
import jax.numpy as jnp
import numpy as np
from jax import lax
from jax.experimental import pallas as pl
from jax.experimental.pallas import tpu as pltpu
from jax.sharding import PartitionSpec as P

HD = 128


PRECISE = lax.Precision.HIGHEST
EPSILON = 1e-05
FLOOR_SCORE = -1e30
BLOCKS = 4


def mean_of(value):
    width = value.shape[-1]
    while value.shape[-1] > 128 and value.shape[-1] % 256 == 0:
        half = value.shape[-1] // 2
        value = value[..., :half] + value[..., half:]
    return jnp.sum(value, -1, keepdims=True) * (1.0 / width)


def norm_rows(value):
    centred = value - mean_of(value)
    scaled = lax.rsqrt(mean_of(centred * centred) + EPSILON)
    return (centred * scaled, scaled)


def norm_back(normed, scaled, grad):
    return scaled * (grad - mean_of(grad) - normed * mean_of(grad * normed))


def angles(positions, head_size):
    indices = np.arange(head_size // 2, dtype=np.float64)
    frequency = (10000.0 ** (-(2.0 * indices / head_size))).astype(np.float32)
    turned = positions.astype(jnp.float32)[:, None] * frequency[None, :]
    return (jnp.cos(turned)[:, None, :], jnp.sin(turned)[:, None, :])


def dot(left, right):
    return jnp.dot(left, right, preferred_element_type=jnp.float32)


def contract_rows(left, right):
    return lax.dot_general(
        left, right, (((0,), (0,)), ((), ())), preferred_element_type=jnp.float32
    )


def contract_cols(left, right):
    return lax.dot_general(
        left, right, (((1,), (1,)), ((), ())), preferred_element_type=jnp.float32
    )


def greet(partners):
    barrier = pltpu.get_barrier_semaphore()
    for partner in partners:
        pl.semaphore_signal(
            barrier, inc=1, device_id=partner, device_id_type=pl.DeviceIdType.MESH
        )
    pl.semaphore_wait(barrier, len(partners))


def send(source, target, sent, received, device):
    pltpu.make_async_remote_copy(
        src_ref=source,
        dst_ref=target,
        send_sem=sent,
        recv_sem=received,
        device_id=device,
        device_id_type=pl.DeviceIdType.MESH,
    ).start()


def landed(block, semaphore):
    pltpu.make_async_copy(block, block, semaphore).wait()


def ring(owners, cores):
    here = lax.axis_index("ctx")
    core = lax.axis_index("tensor")
    right, left = lax.rem(here + 1, owners), lax.rem(here + owners - 1, owners)
    return here, core, cores - 1 - core, right, left


def gather_first(values, outs, sems, owners, cores):
    local, sent_right, sent_left, sent_pair, came, came_pair = sems
    here, core, pair, right, left = ring(owners, cores)
    for i, (value, out) in enumerate(zip(values, outs)):
        target = out.at[here, core]

        @pl.when(here < owners - 1)
        def _():
            send(value, target, sent_right.at[i, here], came.at[i, here], {"ctx": right})

        @pl.when(here > 0)
        def _():
            send(value, target, sent_left.at[i, here], came.at[i, here], {"ctx": left})

        send(value, target, sent_pair.at[i, here], came_pair.at[i, here], {"tensor": pair})
        pltpu.make_async_copy(value, target, local.at[i]).start()


def gather_rest(values, outs, sems, owners, cores):
    local, sent_right, sent_left, sent_pair, came, came_pair = sems
    here, core, pair, right, left = ring(owners, cores)

    def arrive(i, out, block, onward, sent, device):
        held = out.at[block, core]
        landed(held, came.at[i, block])

        @pl.when(onward)
        def _():
            send(held, held, sent.at[i, block], came.at[i, block], device)

        send(held, held, sent_pair.at[i, block], came_pair.at[i, block], {"tensor": pair})

    for step in range(1, owners):
        for i, out in enumerate(outs):

            @pl.when(here >= step)
            def _():
                arrive(i, out, here - step, here < owners - 1, sent_right, {"ctx": right})

            @pl.when(here + step < owners)
            def _():
                arrive(i, out, here + step, here > 0, sent_left, {"ctx": left})

    for i, (value, out) in enumerate(zip(values, outs)):
        pltpu.make_async_copy(value, out.at[here, core], local.at[i]).wait()
        for block in range(owners):
            landed(out.at[block, pair], came_pair.at[i, block])
            landed(out.at[block, core], sent_pair.at[i, block])

            @pl.when((here < owners - 1) & (block <= here))
            def _():
                landed(out.at[block, core], sent_right.at[i, block])

            @pl.when((here > 0) & (block >= here))
            def _():
                landed(out.at[block, core], sent_left.at[i, block])


def gather_sems(amount, owners):
    return [pltpu.SemaphoreType.DMA((amount,))] + [
        pltpu.SemaphoreType.DMA((amount, owners)) for _ in range(5)
    ]


def line_partners(owners, cores):
    here, core, pair, right, left = ring(owners, cores)
    return [{"ctx": right}, {"ctx": left}, {"tensor": pair}]


def gather_kernel(amount, owners, cores, *refs):
    values, outs, sems = refs[:amount], refs[amount : 2 * amount], refs[2 * amount :]
    greet(line_partners(owners, cores))
    gather_first(values, outs, sems, owners, cores)
    gather_rest(values, outs, sems, owners, cores)


ANY = pl.BlockSpec(memory_space=pl.ANY)
FAR = pl.BlockSpec(memory_space=pltpu.HBM)
INSIDE = pl.BlockSpec(memory_space=pltpu.VMEM)


def params(collective_id):
    return pltpu.CompilerParams(
        collective_id=collective_id, has_side_effects=True, vmem_limit_bytes=60 << 20
    )


def cost(micros):
    return pl.CostEstimate(flops=0, transcendentals=0, bytes_accessed=int(micros * 3.0e6))


def team_gather(collective_id, *values):
    owners, cores = lax.axis_size("ctx"), lax.axis_size("tensor")
    amount = len(values)
    outs = pl.pallas_call(
        functools.partial(gather_kernel, amount, owners, cores),
        out_shape=[jax.ShapeDtypeStruct((owners, cores, *v.shape), v.dtype) for v in values],
        in_specs=[INSIDE] * amount,
        out_specs=[ANY] * amount,
        scratch_shapes=gather_sems(amount, owners),
        compiler_params=params(collective_id),
        cost_estimate=cost(20 * amount),
        name="team_gather",
    )(*values)
    return [o.reshape(-1, v.shape[1]) for o, v in zip(outs, values)]


def plane(index, shards_in):
    across_x = index + 1 - 2 * lax.rem(index, 2)
    return across_x, lax.rem(index + 2, shards_in), lax.rem(across_x + 2, shards_in)


def open_kernel(shards_in, owners, cores, *refs):
    value, w_query, w_key, w_value, w_output, w_gate, w_up, w_down, note = refs[:9]
    out, qkv, out_w, packed, notes = refs[9:14]
    own_sem, sent_w, came_w, passed_w, sent_n, came_n, pack_sem, load_sem = refs[14:22]
    stage, stage_out, stage_pack = refs[22:25]
    sems = refs[25:]
    index = lax.axis_index("shard")
    here = lax.axis_index("ctx")
    depth = w_query.shape[0]
    count = w_query.shape[1] // owners
    columns = pl.ds(pl.multiple_of(here * count, count), count)
    stored = [w.at[:, columns] for w in (w_query, w_key, w_value)] + [w_output.at[columns, :]]
    sources = [stage.at[0], stage.at[1], stage.at[2], stage_out]
    for k, (slow, source) in enumerate(zip(stored, sources)):
        pltpu.make_async_copy(slow, source, load_sem.at[k]).start()

    def target(weight, block):
        if weight == 3:
            wide = w_output.shape[1]
            return out_w.at[:, pl.ds(pl.multiple_of(block * wide, wide), wide)]
        rows = pl.ds(pl.multiple_of(block * depth, depth), depth)
        return qkv.at[rows, pl.ds(weight * count, count)]

    others = [lax.rem(index + step, shards_in) for step in range(1, shards_in)]
    greet(around("shard", shards_in) + around("ctx", owners) + around("tensor", cores))
    units = w_gate.shape[1] // owners
    hidden = pl.ds(pl.multiple_of(here * units, units), units)
    wide_down = w_down.shape[1]
    pieces = [
        (w_gate.at[:, hidden], stage_pack.at[:, pl.ds(0, units)]),
        (w_up.at[:, hidden], stage_pack.at[:, pl.ds(units, units)]),
    ]
    for k in range(units // depth):
        start = pl.multiple_of(here * units + k * depth, depth)
        place = pl.ds(2 * units + k * wide_down, wide_down)
        pieces.append((w_down.at[pl.ds(start, depth), :], stage_pack.at[:, place]))
    for k, (source, place) in enumerate(pieces):
        pltpu.make_async_copy(source, place, pack_sem.at[k]).start()
    notes[here] = note[...]
    fellows = [lax.rem(here + step, owners) for step in range(1, owners)]
    for fellow in fellows:
        send(note, notes.at[here], sent_n.at[fellow], came_n.at[here], {"ctx": fellow})
    square = shards_in == 4
    near = plane(index, shards_in)[:2] if square else others
    for weight in range(4):
        pltpu.make_async_copy(stored[weight], sources[weight], load_sem.at[weight]).wait()
        for other in near:
            send(
                sources[weight],
                target(weight, index),
                sent_w.at[weight, other],
                came_w.at[weight, index],
                {"shard": other},
            )
    gather_first([value], [out], sems, owners, cores)
    for weight in range(4):
        pltpu.make_async_copy(
            sources[weight], target(weight, index), own_sem.at[weight]
        ).start()
    for k, (source, place) in enumerate(pieces):
        pltpu.make_async_copy(source, place, pack_sem.at[k]).wait()
    pltpu.make_async_copy(stage_pack, packed, load_sem.at[4]).start()
    if square:
        across_x, across_y, far = plane(index, shards_in)
        for weight, source, device in (
            (0, across_x, across_y),
            (2, across_y, across_x),
            (1, across_x, across_y),
            (3, across_y, across_x),
        ):
            held = target(weight, source)
            landed(held, came_w.at[weight, source])
            send(
                held, held, passed_w.at[weight], came_w.at[weight, source], {"shard": device}
            )
    gather_rest([value], [out], sems, owners, cores)
    for fellow in fellows:
        landed(notes.at[fellow], came_n.at[fellow])
        landed(note, sent_n.at[fellow])
    pltpu.make_async_copy(stage_pack, packed, load_sem.at[4]).wait()
    for weight in range(4):
        pltpu.make_async_copy(
            sources[weight], target(weight, index), own_sem.at[weight]
        ).wait()
        for other in near:
            landed(sources[weight], sent_w.at[weight, other])
    if square:
        for weight, source in ((0, across_y), (2, across_x), (1, across_y), (3, across_x)):
            landed(target(weight, source), came_w.at[weight, source])
        for weight in range(4):
            landed(target(weight, far), came_w.at[weight, far])
            landed(sources[weight], passed_w.at[weight])
    else:
        for weight in range(4):
            for other in others:
                landed(target(weight, other), came_w.at[weight, other])


def open_team(collective_id, value, weights, note):
    shards_in, owners, cores = [lax.axis_size(a) for a in ("shard", "ctx", "tensor")]
    depth = weights[0].shape[0]
    count = weights[0].shape[1] // owners
    units = weights[4].shape[1] // owners
    pieces = 2 + units // depth
    out, qkv, out_w, packed, notes = pl.pallas_call(
        functools.partial(open_kernel, shards_in, owners, cores),
        out_shape=[
            jax.ShapeDtypeStruct((owners, cores, *value.shape), value.dtype),
            jax.ShapeDtypeStruct((shards_in * depth, 3 * count), value.dtype),
            jax.ShapeDtypeStruct((count, shards_in * weights[3].shape[1]), value.dtype),
            jax.ShapeDtypeStruct((depth, 3 * units), value.dtype),
            jax.ShapeDtypeStruct((owners, *note.shape), note.dtype),
        ],
        in_specs=[INSIDE] + [FAR] * 7 + [INSIDE],
        out_specs=[ANY] * 3 + [FAR] + [INSIDE],
        scratch_shapes=[
            pltpu.SemaphoreType.DMA((4,)),
            pltpu.SemaphoreType.DMA((4, shards_in)),
            pltpu.SemaphoreType.DMA((4, shards_in)),
            pltpu.SemaphoreType.DMA((4,)),
            pltpu.SemaphoreType.DMA((owners,)),
            pltpu.SemaphoreType.DMA((owners,)),
            pltpu.SemaphoreType.DMA((pieces,)),
            pltpu.SemaphoreType.DMA((5,)),
            pltpu.VMEM((3, depth, count), value.dtype),
            pltpu.VMEM((count, weights[3].shape[1]), value.dtype),
            pltpu.VMEM((depth, 3 * units), value.dtype),
        ]
        + gather_sems(1, owners),
        compiler_params=params(collective_id),
        cost_estimate=cost(40),
        name="open_team",
    )(value, *weights, note)
    return out.reshape(-1, value.shape[1]), qkv, out_w, packed, notes


def scatter_kernel(amount, owners, cores, *refs):
    parts, outs, refs = refs[:amount], refs[amount : 2 * amount], refs[2 * amount :]
    greet(line_partners(owners, cores))
    scatter(amount, owners, cores, parts, outs, refs)


def scatter(amount, owners, cores, parts, outs, refs):
    pairs, halves, from_left, from_right, own = [
        refs[k * amount : (k + 1) * amount] for k in range(5)
    ]
    total, sent_pair, came_pair, sent, came_left, came_right, load = refs[5 * amount :]
    here, core, pair, right, left = ring(owners, cores)
    order = [k // 2 if k % 2 else owners - 1 - k // 2 for k in range(owners)]
    for i in range(amount):
        for block in order:
            pltpu.make_async_copy(
                parts[i].at[block, core], own[i].at[block], load.at[i, block]
            ).start()
            send(
                parts[i].at[block, pair],
                pairs[i].at[block],
                sent_pair.at[i, block],
                came_pair.at[i, block],
                {"tensor": pair},
            )

    def add_up(i, block, more, arrived, came):
        landed(pairs[i].at[block], came_pair.at[i, block])
        landed(own[i].at[block], load.at[i, block])
        total[...] = own[i][block].astype(jnp.float32) + pairs[i][block].astype(jnp.float32)

        @pl.when(more)
        def _():
            landed(arrived[i].at[block], came.at[i, block])
            total[...] += arrived[i][block].astype(jnp.float32)

    def pass_on(i, block, more, arrived, came, device):
        add_up(i, block, more, arrived, came)
        halves[i][block] = total[...].astype(halves[i].dtype)
        send(
            halves[i].at[block],
            arrived[i].at[block],
            sent.at[i, block],
            came.at[i, block],
            {"ctx": device},
        )

    for step in range(2 * owners - 2):
        for i in range(amount):
            rightward = owners - 1 - (step - here)
            leftward = step - (owners - 1 - here)

            @pl.when((rightward > here) & (step >= here))
            def _():
                pass_on(i, rightward, here > 0, from_left, came_left, right)

            @pl.when((leftward >= 0) & (leftward < here))
            def _():
                pass_on(i, leftward, here < owners - 1, from_right, came_right, left)

    for i in range(amount):
        add_up(i, here, here > 0, from_left, came_left)

        @pl.when(here < owners - 1)
        def _():
            landed(from_right[i].at[here], came_right.at[i, here])
            total[...] += from_right[i][here].astype(jnp.float32)

        outs[i][...] = total[...]
    for i in range(amount):
        for block in range(owners):
            landed(pairs[i].at[block], sent_pair.at[i, block])

            @pl.when(block != here)
            def _():
                landed(halves[i].at[block], sent.at[i, block])


def scatter_scratch(amount, owners, block, kind):
    held = [pltpu.VMEM((owners, *block), kind)] * amount
    sems = [pltpu.SemaphoreType.DMA((amount, owners)) for _ in range(6)]
    return held * 5 + [pltpu.VMEM(block, jnp.float32)] + sems


def team_sum(collective_id, *values):
    owners, cores = lax.axis_size("ctx"), lax.axis_size("tensor")
    amount = len(values)
    width = values[0].shape[1]
    mine = values[0].shape[0] // (owners * cores)
    return pl.pallas_call(
        functools.partial(scatter_kernel, amount, owners, cores),
        out_shape=[jax.ShapeDtypeStruct((mine, width), jnp.float32)] * amount,
        in_specs=[ANY] * amount,
        out_specs=[INSIDE] * amount,
        scratch_shapes=scatter_scratch(amount, owners, (mine, width), values[0].dtype),
        compiler_params=params(collective_id),
        cost_estimate=cost(20 * amount),
        name="team_sum",
    )(*[v.reshape(owners, cores, mine, width) for v in values])


def swap_first(summed, held, local, sent, came, owners):
    here = lax.axis_index("ctx")
    count = summed.shape[0] // owners

    def rows(owner):
        return summed.at[pl.ds(pl.multiple_of(owner * count, count), count), :]

    for step in range(1, owners):
        other = lax.rem(here + step, owners)
        send(rows(other), held.at[here], sent.at[other], came.at[here], {"ctx": other})
    pltpu.make_async_copy(rows(here), held.at[here], local).start()


def put_rows(rows, outs, block, half, halves):
    amount = len(outs)
    units = rows.shape[1] // amount
    for j in range(units // block):
        start = half * units + j * block
        for i, out in enumerate(outs):
            first = (j * amount + i) * block
            piece = rows[:, first : first + block].astype(jnp.float32)
            if i < amount - 1:
                out[:, start : start + block] = piece
            else:
                out[start : start + block, :] = piece.T


def place_attn_kernel(attn, *outs):
    put_rows(attn[0], outs, outs[0].shape[1], 0, 1)


def place_kernel(block, where, own_a, far_a, own_b, far_b, early, late, *outs):
    core = where[0]
    for own, far, out in ((own_a, far_a, outs[0]), (own_b, far_b, outs[1])):
        out[0, core] = own[0]
        out[0, out.shape[1] - 1 - core] = far[0]
    put_rows(early[0], outs[2:], block, 0, 2)
    put_rows(late[0], outs[2:], block, 1, 2)


def placed_rows(owners, count, units, amount):
    specs = [pl.BlockSpec((count, units), lambda c, *_: (0, c))] * (amount - 1)
    specs.append(pl.BlockSpec((units, count), lambda c, *_: (c, 0)))
    shapes = [jax.ShapeDtypeStruct((count, owners * units), jnp.float32)] * (amount - 1)
    shapes.append(jax.ShapeDtypeStruct((owners * units, count), jnp.float32))
    return specs, shapes


def place_attn(attn):
    owners, count, wide = attn.shape
    specs, shapes = placed_rows(owners, count, wide // 4, 4)
    return pl.pallas_call(
        place_attn_kernel,
        grid=(owners,),
        in_specs=[pl.BlockSpec((1, count, wide), lambda c: (c, 0, 0))],
        out_specs=specs,
        out_shape=shapes,
        compiler_params=pltpu.CompilerParams(
            dimension_semantics=("arbitrary",), vmem_limit_bytes=60 << 20
        ),
        cost_estimate=cost(2),
        name="place_attn",
    )(attn)


def place_all(streams, early, late):
    owners, cores = lax.axis_size("ctx"), lax.axis_size("tensor")
    run = streams[0].shape
    block = late.shape[2] // (3 * BLOCKS // 2)

    def lead(shape):
        return pl.BlockSpec((1, *shape[1:]), lambda c, _: (c,) + (0,) * (len(shape) - 1))

    both = (run[0], cores, *run[1:])
    specs, shapes = [lead(both)] * 2, [jax.ShapeDtypeStruct(both, streams[0].dtype)] * 2
    more, wide = placed_rows(owners, late.shape[1], 2 * late.shape[2] // 3, 3)
    specs, shapes = specs + more, shapes + wide
    return pl.pallas_call(
        functools.partial(place_kernel, block),
        grid_spec=pltpu.PrefetchScalarGridSpec(
            num_scalar_prefetch=1,
            grid=(owners,),
            in_specs=[lead(v.shape) for v in (*streams, early, late)],
            out_specs=specs,
        ),
        out_shape=shapes,
        compiler_params=pltpu.CompilerParams(
            dimension_semantics=("arbitrary",), vmem_limit_bytes=60 << 20
        ),
        cost_estimate=cost(7),
        name="place_all",
    )(lax.axis_index("tensor")[None].astype(jnp.int32), *streams, early, late)


def swap_rest(summed, held, local, sent, came, owners):
    here = lax.axis_index("ctx")
    count = summed.shape[0] // owners
    own = summed.at[pl.ds(pl.multiple_of(here * count, count), count), :]
    for step in range(owners):
        source = lax.rem(here + owners - step, owners)
        if step == 0:
            pltpu.make_async_copy(own, held.at[here], local).wait()
        else:
            landed(held.at[source], came.at[source])
    for step in range(1, owners):
        other = lax.rem(here + step, owners)
        landed(held.at[other], sent.at[other])


def held_shape(summed, owners):
    return (owners, summed.shape[0] // owners, summed.shape[1])


def swap_sems(owners):
    return [
        pltpu.SemaphoreType.DMA,
        pltpu.SemaphoreType.DMA((owners,)),
        pltpu.SemaphoreType.DMA((owners,)),
    ]


def around(axis, size):
    index = lax.axis_index(axis)
    return [{axis: lax.rem(index + step, size)} for step in range(1, size)]


def swap_kernel_alone(owners, summed, held, *sems):
    greet(around("ctx", owners))
    swap_first(summed, held, *sems, owners)
    swap_rest(summed, held, *sems, owners)


def team_rows(collective_id, summed):
    owners = lax.axis_size("ctx")
    return pl.pallas_call(
        functools.partial(swap_kernel_alone, owners),
        out_shape=jax.ShapeDtypeStruct(held_shape(summed, owners), summed.dtype),
        in_specs=[INSIDE],
        out_specs=ANY,
        scratch_shapes=swap_sems(owners),
        compiler_params=params(collective_id),
        cost_estimate=cost(20),
        name="team_rows",
    )(summed)


def close_kernel(amount, shards_in, owners, cores, *refs):
    values, mixed, grads = refs[:amount], refs[amount], refs[amount + 1]
    refs = refs[amount + 2 :]
    outs, mix_out, late = refs[:amount], refs[amount], refs[amount + 1]
    summed, refs = refs[amount + 2], refs[amount + 3 :]
    pairs, half, quarters, blocks, sent, came = refs[:6]
    sent_c, came_c, sent_s, came_s, sent_b, came_b = refs[6:12]
    swap = refs[12:]
    here, core, pair, right, left = ring(owners, cores)
    index = lax.axis_index("shard")
    near = [lax.rem(here + step, owners) for step in range(1, owners)]
    others = [lax.rem(index + step, shards_in) for step in range(1, shards_in)]
    greet([{"tensor": pair}] + around("ctx", owners) + around("shard", shards_in))
    wide = mixed.shape[1] // cores
    thin = wide // owners
    send(
        mixed.at[:, pl.ds(pl.multiple_of(pair * wide, wide), wide)],
        pairs,
        sent.at[amount],
        came.at[amount],
        {"tensor": pair},
    )
    for i in range(amount):
        send(values[i], outs[i], sent.at[i], came.at[i], {"tensor": pair})
    landed(pairs, came.at[amount])
    half[...] = mixed[:, pl.ds(pl.multiple_of(core * wide, wide), wide)] + pairs[...]
    for other in near:
        send(
            half.at[:, pl.ds(pl.multiple_of(other * thin, thin), thin)],
            quarters.at[here],
            sent_c.at[other],
            came_c.at[here],
            {"ctx": other},
        )
    swap_first(grads, late, *swap, owners)
    total = half[:, pl.ds(pl.multiple_of(here * thin, thin), thin)]
    for other in near:
        landed(quarters.at[other], came_c.at[other])
        total += quarters[other]
    blocks[index] = total
    for other in others:
        send(
            blocks.at[index], blocks.at[index], sent_s.at[other], came_s.at[index], {"shard": other}
        )
    for other in others:
        landed(blocks.at[other], came_s.at[other])
    total = blocks[0]
    for block in range(1, shards_in):
        total += blocks[block]

    def place(owner, half_of):
        return summed.at[half_of * owners + owner]

    summed[core * owners + here] = total
    for other in near:
        send(place(here, core), place(here, core), sent_b.at[other], came_b.at[here, core], {"ctx": other})
    send(place(here, core), place(here, core), sent_b.at[here], came_b.at[here, core], {"tensor": pair})
    for other in near:
        landed(place(other, core), came_b.at[other, core])
        send(
            place(other, core),
            place(other, core),
            sent_b.at[owners + other],
            came_b.at[other, core],
            {"tensor": pair},
        )
    for owner in range(owners):
        landed(place(owner, pair), came_b.at[owner, pair])
        landed(place(owner, core), sent_b.at[owner])
    for owner in range(owners):
        for half_of in range(cores):
            found = summed[half_of * owners + owner]
            start = (half_of * owners + owner) * thin
            for row in range(mix_out.shape[0] * mix_out.shape[1]):
                k, h = row // mix_out.shape[1], row % mix_out.shape[1]
                mix_out[k, h : h + 1, start : start + thin] = found[row : row + 1, :]
    for other in near:
        landed(place(other, core), sent_b.at[owners + other])
        landed(quarters.at[other], sent_c.at[other])
    for other in others:
        landed(blocks.at[other], sent_s.at[other])
    landed(pairs, sent.at[amount])
    swap_rest(grads, late, *swap, owners)
    for i in range(amount):
        landed(outs[i], came.at[i])
        landed(values[i], sent.at[i])


def close_team(collective_id, grads, mixed, *values):
    shards_in, owners, cores = [lax.axis_size(a) for a in ("shard", "ctx", "tensor")]
    amount = len(values)
    height, width = mixed.shape
    thin = width // (cores * owners)
    out = pl.pallas_call(
        functools.partial(close_kernel, amount, shards_in, owners, cores),
        out_shape=[
            jax.ShapeDtypeStruct(v.shape, v.dtype) for v in values
        ]
        + [jax.ShapeDtypeStruct((height // 2, 2, width), jnp.float32)]
        + [jax.ShapeDtypeStruct(held_shape(grads, owners), grads.dtype)],
        in_specs=[INSIDE] * (amount + 2),
        out_specs=[ANY] * amount + [INSIDE, ANY],
        scratch_shapes=[
            pltpu.VMEM((cores * owners, height, thin), jnp.float32),
            pltpu.VMEM((height, width // cores), jnp.float32),
            pltpu.VMEM((height, width // cores), jnp.float32),
            pltpu.VMEM((owners, height, thin), jnp.float32),
            pltpu.VMEM((shards_in, height, thin), jnp.float32),
            pltpu.SemaphoreType.DMA((amount + 1,)),
            pltpu.SemaphoreType.DMA((amount + 1,)),
            pltpu.SemaphoreType.DMA((owners,)),
            pltpu.SemaphoreType.DMA((owners,)),
            pltpu.SemaphoreType.DMA((shards_in,)),
            pltpu.SemaphoreType.DMA((shards_in,)),
            pltpu.SemaphoreType.DMA((2 * owners,)),
            pltpu.SemaphoreType.DMA((owners, cores)),
        ]
        + swap_sems(owners),
        compiler_params=params(collective_id),
        cost_estimate=cost(60),
        name="close_team",
    )(*values, mixed, grads)
    return out[amount], out[:amount], out[amount + 1]


def ffn_kernel(
    u_ref,
    dy_ref,
    gate_ref,
    up_ref,
    down_ref,
    y_ref,
    du_ref,
    early_ref,
    late_ref,
    y_sum,
    du_sum,
    u_t,
    dy_t,
):
    step = pl.program_id(0)
    early = step < pl.num_programs(0) // 2
    total, width = u_ref.shape
    block = gate_ref.shape[1]
    tile = down_ref.shape[2]

    @pl.when(step == 0)
    def _():
        y_sum[...] = jnp.zeros_like(y_sum)
        du_sum[...] = jnp.zeros_like(du_sum)
        for start in range(0, width, tile):
            u_t[start : start + tile, :] = u_ref[:, start : start + tile].T
            dy_t[start : start + tile, :] = dy_ref[:, start : start + tile].T

    gate = dot(u_ref[...], gate_ref[...])
    upward = dot(u_ref[...], up_ref[...])
    shards_in = down_ref.shape[0]
    grad_hidden = 0.0
    for k in range(shards_in):
        grad_hidden = grad_hidden + contract_cols(
            dy_ref[:, k * tile : (k + 1) * tile], down_ref[k]
        )
    sigma = jax.nn.sigmoid(gate)
    swish = gate * sigma
    hidden = (swish * upward).astype(jnp.bfloat16)
    grad_gate = (grad_hidden * upward * (sigma + swish * (1.0 - sigma))).astype(jnp.bfloat16)
    grad_up = (grad_hidden * swish).astype(jnp.bfloat16)
    for k in range(shards_in):
        span = slice(k * tile, (k + 1) * tile)
        y_sum[:, span] += dot(hidden, down_ref[k])
        du_sum[:, span] += contract_cols(grad_gate, gate_ref[span, :]) + contract_cols(
            grad_up, up_ref[span, :]
        )

    def weights_back(grad_ref):
        for start in range(0, width, tile):
            span = slice(start, start + tile)
            grad_ref[span, :block] = dot(u_t[span, :], grad_gate).astype(jnp.bfloat16)
            grad_ref[span, block : 2 * block] = dot(u_t[span, :], grad_up).astype(jnp.bfloat16)
            grad_ref[span, 2 * block :] = dot(dy_t[span, :], hidden).astype(jnp.bfloat16)

    @pl.when(early)
    def _():
        weights_back(early_ref)

    @pl.when(jnp.logical_not(early))
    def _():
        weights_back(late_ref)

    @pl.when(step == pl.num_programs(0) - 1)
    def _():
        y_ref[...] = y_sum[...].astype(jnp.bfloat16)
        du_ref[...] = du_sum[...].astype(jnp.bfloat16)


def ffn(u, dy, weights):
    total, width = u.shape
    shards_in = lax.axis_size("shard")
    depth = width // shards_in
    units = weights.shape[1] // 3
    blocks = BLOCKS
    block = units // blocks
    half = blocks // 2
    whole = pl.BlockSpec((total, width), lambda j: (0, 0), pipeline_mode=pl.Buffered(1))
    low = functools.partial(jax.ShapeDtypeStruct, dtype=jnp.bfloat16)
    return pl.pallas_call(
        ffn_kernel,
        grid=(blocks,),
        in_specs=[
            whole,
            whole,
            pl.BlockSpec((width, block), lambda j: (0, j)),
            pl.BlockSpec((width, block), lambda j: (0, blocks + j)),
            pl.BlockSpec(
                (shards_in, block, depth),
                lambda j: (0, j % (depth // block), 2 * units // depth + j // (depth // block)),
            ),
        ],
        out_specs=[
            whole,
            whole,
            pl.BlockSpec((width, 3 * block), lambda j: (0, jnp.minimum(j, half - 1))),
            pl.BlockSpec((width, 3 * block), lambda j: (0, jnp.maximum(j - half, 0))),
        ],
        out_shape=[low((total, width))] * 2 + [low((width, 3 * units // 2))] * 2,
        scratch_shapes=[
            pltpu.VMEM((total, width), jnp.float32),
            pltpu.VMEM((total, width), jnp.float32),
            pltpu.VMEM((width, total), jnp.bfloat16),
            pltpu.VMEM((width, total), jnp.bfloat16),
        ],
        compiler_params=pltpu.CompilerParams(
            dimension_semantics=("arbitrary",), vmem_limit_bytes=60 << 20
        ),
        cost_estimate=cost(30),
        name="ffn",
    )(u, dy, weights, weights, weights.reshape(shards_in, depth, 3 * units))


def pack_kernel(sent, value, out):
    for i in range(value.shape[1]):
        out[0, i] = value[:, i, :]


def pack_runs(value, sent, part):
    rows_in, total, width = value.shape
    return pl.pallas_call(
        pack_kernel,
        grid_spec=pltpu.PrefetchScalarGridSpec(
            num_scalar_prefetch=1,
            grid=(sent.shape[0],),
            in_specs=[
                pl.BlockSpec((part, total, width), lambda c, first: (first[c], 0, 0)),
            ],
            out_specs=pl.BlockSpec((1, total, part, width), lambda c, first: (c, 0, 0, 0)),
        ),
        out_shape=jax.ShapeDtypeStruct((sent.shape[0], total, part, width), value.dtype),
        compiler_params=pltpu.CompilerParams(dimension_semantics=("arbitrary",)),
        cost_estimate=cost(2),
        name="pack_runs",
    )(sent, value)


def head_probs(query, key, placing, placed):
    scores = contract_cols(query, key) * HD ** (-0.5)
    allowed = (placed >= placing[:, 0:1]) & (placed <= placing[:, 1:2])
    scores = jnp.where(allowed, scores, FLOOR_SCORE)
    probs = jnp.exp(scores - jnp.max(scores, -1, keepdims=True))
    return probs / jnp.sum(probs, -1, keepdims=True)


def turn(value, turns, back):
    swung = pltpu.roll(value, HD // 2, 1) * turns[1]
    return value * turns[0] - swung if back else value * turns[0] + swung


def attend_kernel(
    u_ref, qkv_ref, out_ref, turns, placing, placed, y_low, y_high, q_ref, k_ref, v_ref, o_ref
):
    count = q_ref.shape[1]
    u = u_ref[...]
    for first in range(0, count, HD):
        head = slice(first, first + HD)

        def lin(which):
            start = which * count + first
            return dot(u, qkv_ref[:, start : start + HD])

        query = turn(lin(0), turns, False).astype(jnp.bfloat16)
        key = turn(lin(1), turns, False).astype(jnp.bfloat16)
        value = lin(2).astype(jnp.bfloat16)
        q_ref[:, head] = query
        k_ref[:, head] = key
        v_ref[:, head] = value
        probs = head_probs(query, key, placing[...], placed[...])
        o_ref[:, head] = dot(probs.astype(jnp.bfloat16), value).astype(jnp.bfloat16)
    half = y_low.shape[1]
    for start in range(0, half, 512):
        y_low[:, start : start + 512] = dot(o_ref[...], out_ref[:, start : start + 512])
    for start in range(0, half, 512):
        y_high[:, start : start + 512] = dot(
            o_ref[...], out_ref[:, half + start : half + start + 512]
        )


def attend(u, qkv, out_w, turns, placing, placed):
    total, count = u.shape[0], out_w.shape[0]
    low = jax.ShapeDtypeStruct((total, count), jnp.bfloat16)
    return pl.pallas_call(
        attend_kernel,
        out_shape=[jax.ShapeDtypeStruct((total, out_w.shape[1] // 2), jnp.float32)] * 2 + [low] * 4,
        in_specs=[INSIDE] * 6,
        out_specs=[INSIDE] * 6,
        compiler_params=pltpu.CompilerParams(vmem_limit_bytes=60 << 20),
        cost_estimate=cost(12),
        name="attend",
    )(u, qkv, out_w, turns, placing, placed)


def attend_back_kernel(
    owners,
    cores,
    dy_ref,
    u_ref,
    qkv_ref,
    out_ref,
    q_ref,
    k_ref,
    v_ref,
    o_ref,
    turns,
    placing,
    placed,
    summed,
    grad_ref,
    sum_ref,
    rows,
    lin,
    du_ref,
    *refs,
):
    greet(around("ctx", owners) + around("tensor", cores))
    swap, refs = refs[:3], refs[3:]
    swap_first(summed, rows, *swap, owners)
    count = q_ref.shape[1]
    width = dy_ref.shape[1]
    scale = HD ** (-0.5)
    low = jnp.bfloat16
    for first in range(0, count, HD):
        head = slice(first, first + HD)
        query, key, value = q_ref[:, head], k_ref[:, head], v_ref[:, head]
        grad_out = contract_cols(dy_ref[...], out_ref[head, :]).astype(low)
        probs = head_probs(query, key, placing[...], placed[...])
        grad_probs = contract_cols(grad_out, value)
        delta = jnp.sum(probs * grad_probs, -1, keepdims=True)
        grad_scores = (probs * (grad_probs - delta)).astype(low)
        grad_query = turn(dot(grad_scores, key) * scale, turns, True)
        grad_key = turn(contract_rows(grad_scores, query) * scale, turns, True)
        grad_value = contract_rows(probs.astype(low), grad_out)
        for which, grad in enumerate((grad_query, grad_key, grad_value)):
            start = which * count + first
            lin[:, start : start + HD] = grad.astype(low)
    tile = min(512, width)
    edge = lin.shape[1]
    for start in range(0, width, tile):
        span = slice(start, start + tile)
        du_part = contract_cols(lin[...], qkv_ref[span, :]).astype(low)
        du_ref[:, :, :, span] = du_part.reshape(*du_ref.shape[:3], tile)
    for start in range(0, width, tile):
        span = slice(start, start + tile)
        grad_ref[span, :edge] = dot(u_ref[:, span].T, lin[...]).astype(low)
        grad_ref[span, edge:] = dot(dy_ref[:, span].T, o_ref[...]).astype(low)
    scatter(1, owners, cores, [du_ref], [sum_ref], refs)
    swap_rest(summed, rows, *swap, owners)


def attend_back(collective_id, dy, u, qkv, out_w, q, k, v, o, turns, placing, placed, summed):
    owners, cores = lax.axis_size("ctx"), lax.axis_size("tensor")
    total, width = u.shape
    count = q.shape[1]
    mine = total // (owners * cores)
    return pl.pallas_call(
        functools.partial(attend_back_kernel, owners, cores),
        out_shape=[
            jax.ShapeDtypeStruct((width, 4 * count), jnp.bfloat16),
            jax.ShapeDtypeStruct((mine, width), jnp.float32),
            jax.ShapeDtypeStruct(held_shape(summed, owners), summed.dtype),
        ],
        in_specs=[INSIDE] * 11 + [ANY],
        out_specs=[INSIDE] * 2 + [ANY],
        scratch_shapes=[
            pltpu.VMEM((total, 3 * count), jnp.bfloat16),
            pltpu.VMEM((owners, cores, mine, width), jnp.bfloat16),
        ]
        + swap_sems(owners)
        + scatter_scratch(1, owners, (mine, width), jnp.bfloat16),
        compiler_params=params(collective_id),
        cost_estimate=cost(50),
        name="attend_back",
    )(dy, u, qkv, out_w, q, k, v, o, turns, placing, placed, summed)


EXACT = functools.partial(
    lax.dot_general, precision=PRECISE, preferred_element_type=jnp.float32
)


def columns_of(pieces):
    rows_in = pieces[0].shape[0]
    lane = lax.broadcasted_iota(jnp.int32, (rows_in, 8), 1)
    out = jnp.zeros((rows_in, 8), jnp.float32)
    for k, piece in enumerate(pieces):
        out = jnp.where(lane == k, piece, out)
    return out


def tables_of(current, weight, static, table_ref, active_ref):
    branch_in = 0.0
    tables = []
    for i, stream in enumerate(current):
        normed, scaled = norm_rows(stream)
        active = jnp.tanh(EXACT(normed, weight, (((1,), (1,)), ((), ()))))
        table = active + static[i : i + 1, :]
        table_ref[i] = table
        active_ref[i] = active
        tables.append(table)
        branch_in = branch_in + table[:, 0:1] * stream
    return tables, branch_in


def norm_plain(value):
    centred = value - jnp.mean(value, -1, keepdims=True)
    scaled = lax.rsqrt(jnp.mean(centred * centred, -1, keepdims=True) + EPSILON)
    return (centred * scaled, scaled)


def mix_first(current, weight, static):
    normed, _ = norm_plain(current)
    active = jnp.tanh(jnp.einsum("tsd,dk->tsk", normed, weight, precision=PRECISE))
    table = active + static
    total = current.shape[1]
    branch_in = sum(table[:, i, 0][:, None] * current[:, i] for i in range(total))
    normed, scaled = norm_plain(branch_in)

    def by_stream(value):
        return jnp.pad(value.transpose(1, 0, 2), ((0, 0), (0, 0), (0, 8 - value.shape[2])))

    scaled = jnp.pad(scaled, ((0, 0), (0, 7)))
    return normed.astype(jnp.bfloat16), normed, scaled, by_stream(table), by_stream(active)


def mix_second_kernel(
    source,
    streams,
    branch_out,
    table_one,
    arrived,
    weight,
    static,
    middle_ref,
    low_ref,
    grad_low_ref,
    normed_ref,
    scaled_ref,
    table_ref,
    active_ref,
    top_ref,
):
    total = streams.shape[0]
    y = branch_out[...]
    first = [table_one[i] for i in range(total)]
    current = [streams[i].astype(jnp.float32) for i in range(total)]
    middle = []
    for j in range(total):
        mixed = first[j][:, total + 1 : total + 2] * y
        for i in range(total):
            mixed = mixed + first[i][:, 1 + j : 2 + j] * current[i]
        middle.append(mixed)
        middle_ref[j] = mixed
    tables, branch_in = tables_of(middle, weight[...], static[...], table_ref, active_ref)
    normed, scaled = norm_rows(branch_in)
    normed_ref[...] = normed
    low_ref[...] = normed.astype(jnp.bfloat16)
    scaled_ref[...] = columns_of([scaled])
    grad = 0.0
    for j in range(total):
        top = arrived[0, j]
        top_ref[j] = top
        grad = grad + tables[j][:, total + 1 : total + 2] * top.astype(jnp.float32)
    grad_low_ref[...] = grad.astype(jnp.bfloat16)


def connection_back(
    current, grad_top, branch_out, grad_in, normed_in, scaled_in, tables, actives, weight, sums
):
    total = len(current)
    weight_sum, static_sum = sums
    dx = scaled_in * (grad_in - mean_of(grad_in) - normed_in * mean_of(grad_in * normed_in))
    result = []
    for i, stream in enumerate(current):
        pieces = [jnp.sum(dx * stream, -1, keepdims=True)]
        pieces += [jnp.sum(stream * top, -1, keepdims=True) for top in grad_top]
        pieces.append(jnp.sum(grad_top[i] * branch_out, -1, keepdims=True))
        grad_table = columns_of(pieces)
        static_sum[i : i + 1, :] += jnp.sum(grad_table, 0, keepdims=True)
        grad_inner = grad_table * (1.0 - actives[i] * actives[i])
        normed, scaled = norm_rows(stream)
        weight_sum[...] += EXACT(grad_inner, normed, (((0,), (0,)), ((), ())))
        grad_normed = EXACT(grad_inner, weight, (((1,), (0,)), ((), ())))
        grad = tables[i][:, 0:1] * dx + norm_back(normed, scaled, grad_normed)
        for j in range(total):
            grad = grad + tables[i][:, 1 + j : 2 + j] * grad_top[j]
        result.append(grad)
    return result


def start_sums(sums):
    @pl.when(pl.program_id(0) == 0)
    def _():
        for ref in sums:
            ref[...] = jnp.zeros_like(ref)


def back_second_kernel(
    middle,
    top,
    branch_out,
    grad_in,
    normed_in,
    scaled_in,
    table,
    active,
    table_one,
    weight,
    final_ref,
    grad_ref,
    grad_low_ref,
    *sums,
):
    start_sums(sums)
    total = middle.shape[0]
    current = [middle[i] for i in range(total)]
    grad_top = [top[i].astype(jnp.float32) for i in range(total)]
    tables = [table[i] for i in range(total)]
    y = branch_out[...]
    for j in range(total):
        mixed = tables[j][:, total + 1 : total + 2] * y
        for i in range(total):
            mixed = mixed + tables[i][:, 1 + j : 2 + j] * current[i]
        final_ref[0, :, j, :] = mixed.astype(jnp.bfloat16)
    grads = connection_back(
        current,
        grad_top,
        y,
        grad_in[...],
        normed_in[...],
        scaled_in[:, 0:1],
        tables,
        [active[i] for i in range(total)],
        weight[...],
        sums,
    )
    low = 0.0
    for j in range(total):
        grad_ref[j] = grads[j]
        low = low + table_one[j][:, total + 1 : total + 2] * grads[j]
    grad_low_ref[...] = low.astype(jnp.bfloat16)


def back_first_kernel(
    streams,
    top,
    branch_out,
    grad_in,
    normed_in,
    scaled_in,
    table,
    active,
    weight,
    grad_ref,
    *sums,
):
    start_sums(sums)
    total = streams.shape[0]
    grads = connection_back(
        [streams[i].astype(jnp.float32) for i in range(total)],
        [top[i] for i in range(total)],
        branch_out[...],
        grad_in[...],
        normed_in[...],
        scaled_in[:, 0:1],
        [table[i] for i in range(total)],
        [active[i] for i in range(total)],
        weight[...],
        sums,
    )
    for j in range(total):
        grad_ref[0, :, j, :] = grads[j].astype(jnp.bfloat16)


def by_token(tile, shape, kind=jnp.float32):
    block = (*shape[:-2], tile, shape[-1])
    lead = (0,) * (len(shape) - 2)
    spec = pl.BlockSpec(block, lambda step, *_: (*lead, step, 0))
    return spec, jax.ShapeDtypeStruct(shape, kind)


def fixed(shape, kind=jnp.float32):
    spec = pl.BlockSpec(shape, lambda step, *_: (0,) * len(shape))
    return spec, jax.ShapeDtypeStruct(shape, kind)


def token_call(kernel, name, tile, ins, outs, prefetch=(), special=None):
    specs, values = [], []
    for value, tiled in ins:
        if tiled == "run":
            specs.append(special)
        else:
            specs.append(by_token(tile, value.shape)[0] if tiled else fixed(value.shape)[0])
        values.append(value)
    tokens = ins[0][0].shape[-2]
    return pl.pallas_call(
        kernel,
        grid_spec=pltpu.PrefetchScalarGridSpec(
            num_scalar_prefetch=len(prefetch),
            grid=(tokens // tile,),
            in_specs=specs,
            out_specs=[o[0] for o in outs],
        ),
        out_shape=[o[1] for o in outs],
        compiler_params=pltpu.CompilerParams(
            dimension_semantics=("arbitrary",), vmem_limit_bytes=60 << 20
        ),
        cost_estimate=cost(5),
        name=name,
    )(*prefetch, *values)


def shards(
    streams,
    lengths,
    destination,
    w_query,
    w_key,
    w_value,
    w_output,
    w_gate,
    w_up,
    w_down,
    mix_weight,
    mix_static,
    cotangent,
):
    rows_here, stream_total, width = streams.shape
    owners = lax.axis_size("ctx")
    cores = lax.axis_size("tensor")
    here = lax.axis_index("ctx")
    core = lax.axis_index("tensor")
    run_rows = rows_here // owners
    part = run_rows // cores
    mine = rows_here // cores
    group_rows = rows_here * owners
    head_cols = w_query.shape[1] // owners
    heads = head_cols // HD
    units = w_gate.shape[1] // owners
    scale = HD ** (-0.5)

    def columns(weight, count):
        return lax.dynamic_slice_in_dim(weight, here * count, count, 1)

    def rows(weight, count):
        return lax.dynamic_slice_in_dim(weight, here * count, count, 0)

    order = jnp.arange(group_rows, dtype=jnp.int32)
    within = order % mine
    placed = (
        order // rows_here * rows_here
        + within // part * run_rows
        + order % rows_here // mine * part
        + within % part
    )
    spans = lengths[0]
    count = jnp.arange(spans.shape[0], dtype=jnp.int32)
    starts = jnp.sum(jnp.where(count[None, :] < count[:, None], spans[None, :], 0), 1)
    begin = jnp.max(jnp.where(starts[None, :] <= placed[:, None], starts[None, :], 0), axis=1)
    cosine, sine = angles(placed - begin, HD)
    turns = jnp.stack(
        [jnp.concatenate([cosine, cosine], -1), jnp.concatenate([-sine, sine], -1)]
    ).reshape(2, group_rows, HD)
    placing = jnp.stack([begin, placed], 1)
    placed = placed[None]

    local_dest = destination - lax.axis_index("shard") * group_rows
    heads_of_runs = local_dest.reshape(owners, run_rows)[:, 0]
    came_from = heads_of_runs // rows_here
    note = jnp.broadcast_to(jnp.pad(heads_of_runs, (0, 128 - owners)), (8, 128))

    turned_weight = jnp.pad(mix_weight.transpose(0, 2, 1), ((0, 0), (0, 2), (0, 0)))
    static = jnp.pad(mix_static, ((0, 0), (0, 0), (0, 2)))
    split = streams.reshape(owners, cores, part, stream_total, width)
    current = lax.dynamic_index_in_dim(split, core, 1, keepdims=False)
    current = current.reshape(mine, stream_total, width)
    attn_low, attn_normed, attn_scaled, table_one, active_one = mix_first(
        current.astype(jnp.float32), mix_weight[0], mix_static[0]
    )
    current = current.transpose(1, 0, 2)
    low = jnp.bfloat16
    tile = min(16, part)
    small = by_token(tile, (stream_total, mine, 8))
    attn_input, qkv, out_w, packed, notes = open_team(
        0, attn_low, (w_query, w_key, w_value, w_output, w_gate, w_up, w_down), note
    )
    ffn_weights = lax.all_gather(packed, "shard", axis=0, tiled=True)
    every = notes[:, 0, :owners]
    sent = jnp.sum(jnp.where(every // rows_here == here, every % rows_here, 0), 1) // part + core
    packed = pack_runs(cotangent, sent, part)
    arrived = lax.all_to_all(packed, "ctx", split_axis=0, concat_axis=0, tiled=True)
    *attn_parts, queries, keys, values, attended = attend(
        attn_input, qkv, out_w, turns, placing, placed
    )
    attn_out = jnp.concatenate(team_sum(1, *attn_parts), 1)

    (
        middle,
        ffn_low,
        grad_ffn_low,
        ffn_normed,
        ffn_scaled,
        table_two,
        active_two,
        grad_top,
    ) = token_call(
        mix_second_kernel,
        "mix_second",
        tile,
        [
            (current, True),
            (attn_out, True),
            (table_one, True),
            (arrived, "run"),
            (turned_weight[1], False),
            (static[1], False),
        ],
        [
            by_token(tile, (stream_total, mine, width)),
            by_token(tile, (mine, width), low),
            by_token(tile, (mine, width), low),
            by_token(tile, (mine, width)),
            by_token(tile, (mine, 8)),
            small,
            small,
            by_token(tile, (stream_total, mine, width), low),
        ],
        (came_from,),
        pl.BlockSpec(
            (1, stream_total, tile, width),
            lambda step, source: (source[step * tile // part], 0, step % (part // tile), 0),
        ),
    )
    ffn_input, grad_ffn_out = team_gather(2, ffn_low, grad_ffn_low)
    ffn_part, ffn_input_part, *ffn_grads = ffn(ffn_input, grad_ffn_out, ffn_weights)

    def shard_sum(partial):
        return lax.psum_scatter(partial, "shard", scatter_dimension=0, tiled=True)

    early_sum, late_sum = [shard_sum(grads) for grads in ffn_grads]
    ffn_out, grad_ffn_input = team_sum(3, ffn_part, ffn_input_part)
    sums = [fixed((8, width)), fixed((stream_total, 8))]
    runs = (
        pl.BlockSpec(
            (1, tile, stream_total, width),
            lambda step, *_: (step * tile // part, step % (part // tile), 0, 0),
        ),
        jax.ShapeDtypeStruct((owners, part, stream_total, width), low),
    )
    final, grad_middle, grad_attn_low, weight_two, static_two = token_call(
        back_second_kernel,
        "back_second",
        tile,
        [
            (middle, True),
            (grad_top, True),
            (ffn_out, True),
            (grad_ffn_input, True),
            (ffn_normed, True),
            (ffn_scaled, True),
            (table_two, True),
            (active_two, True),
            (table_one, True),
            (turned_weight[1], False),
        ],
        [
            runs,
            by_token(tile, (stream_total, mine, width)),
            by_token(tile, (mine, width), low),
            *sums,
        ],
    )
    [grad_attn_out] = team_gather(4, grad_attn_low)

    attn_grads, grad_attn_input, early_rows = attend_back(
        5,
        grad_attn_out,
        attn_input,
        qkv,
        out_w,
        queries,
        keys,
        values,
        attended,
        turns,
        placing,
        placed,
        early_sum,
    )
    attn_sum = shard_sum(attn_grads)

    grad_current, weight_one, static_one = token_call(
        back_first_kernel,
        "back_first",
        tile,
        [
            (current, True),
            (grad_middle, True),
            (attn_out, True),
            (grad_attn_input, True),
            (attn_normed, True),
            (attn_scaled, True),
            (table_one, True),
            (active_one, True),
            (turned_weight[0], False),
        ],
        [runs, *sums],
    )
    statics = jnp.stack([static_one, static_two]).reshape(1, -1)
    mixed = jnp.concatenate(
        [
            jnp.stack([weight_one, weight_two], 1).reshape(16, width),
            jnp.pad(statics, ((0, 7), (0, width - statics.size))),
        ],
        0,
    )

    mixed, (far_final, far_grad), late_rows = close_team(
        7, late_sum, mixed, final, grad_current
    )
    streams_out, grad_streams, grad_gate, grad_up, grad_down = place_all(
        (final, far_final, grad_current, far_grad), early_rows, late_rows
    )
    mixed, attn_sum, grad_gate = lax.optimization_barrier((mixed, attn_sum, grad_gate))
    grad_query, grad_key, grad_value, grad_output = place_attn(team_rows(8, attn_sum))
    columns_in = mix_weight.shape[2]
    grad_mix_weight = mixed[:columns_in].transpose(1, 2, 0)
    grad_mix_static = mixed[8, 0, : statics.size].reshape(2, stream_total, 8)[:, :, :columns_in]

    return (
        streams_out.reshape(rows_here, stream_total, width),
        grad_streams.reshape(rows_here, stream_total, width),
        grad_query,
        grad_key,
        grad_value,
        grad_output,
        grad_gate,
        grad_up,
        grad_down,
        grad_mix_weight,
        grad_mix_static,
    )


def solution(mesh):
    return jax.shard_map(
        shards,
        mesh=mesh,
        in_specs=(
            P(("shard", "ctx"), None, None),
            P("shard", None),
            P(("shard", "ctx")),
            P("shard", "tensor"),
            P("shard", "tensor"),
            P("shard", "tensor"),
            P("tensor", "shard"),
            P("shard", "tensor"),
            P("shard", "tensor"),
            P("tensor", "shard"),
            P(),
            P(),
            P(("shard", "ctx"), None, None),
        ),
        out_specs=(
            P(("shard", "ctx"), None, None),
            P(("shard", "ctx"), None, None),
            P(("shard", "ctx"), "tensor"),
            P(("shard", "ctx"), "tensor"),
            P(("shard", "ctx"), "tensor"),
            P("tensor", ("shard", "ctx")),
            P(("shard", "ctx"), "tensor"),
            P(("shard", "ctx"), "tensor"),
            P("tensor", ("shard", "ctx")),
            P(),
            P(),
        ),
        check_vma=False,
    )
```
